32 devices in a mesh: wide: 8 (over z, x), narrow: 4 (over y, core).
Axes of the slice: x: 2, y: 2, z: 4, core: 2. Of those that a mesh axis runs over, the one named last changes fastest.
Arguments:
- tokens: bfloat16 [26880, 768], P(('wide', 'narrow')), may hold values from -6 to 6
- patch_counts: int32 [96], P('wide'), may hold values from 100 to 240, as said below
- ln1_gain: float32 [768], replicated, may hold values from 0.25 to 1.75
- ln1_bias: float32 [768], replicated, may hold values from -3 to 3
- w_qkv: bfloat16 [768, 3, 768], P(None, None, 'narrow'), may hold values from -0.21875 to 0.21875
- b_qv: float32 [2, 768], P(None, 'narrow'), may hold values from -3 to 3
- w_out: bfloat16 [768, 768], P('narrow'), may hold values from -0.625 to 0.625
- b_out: float32 [768], replicated, may hold values from -3 to 3
- ln2_gain: float32 [768], replicated, may hold values from 0.25 to 1.75
- ln2_bias: float32 [768], replicated, may hold values from -3 to 3
- w_up: bfloat16 [768, 3072], P(None, 'narrow'), may hold values from -0.21875 to 0.21875
- b_up: bfloat16 [1, 3072], P(None, 'narrow'), may hold values from -3 to 3
- w_down: bfloat16 [3072, 768], P('narrow'), may hold values from -0.109375 to 0.109375
- b_down: float32 [768], replicated, may hold values from -3 to 3
- cotangent: bfloat16 [26880, 768], P(('wide', 'narrow')), may hold values from -6 to 6
Outputs:
- layer_out: float32 [26880, 768], P(('wide', 'narrow'))
- input_grad: float32 [26880, 768], P(('wide', 'narrow'))
- ln1_gain_grad: float32 [768], replicated
- ln1_bias_grad: float32 [768], replicated
- w_qkv_grad: float32 [768, 3, 768], P(None, None, 'narrow')
- b_qv_grad: float32 [2, 768], P(None, 'narrow')
- w_out_grad: float32 [768, 768], P('narrow')
- b_out_grad: float32 [768], replicated
- ln2_gain_grad: float32 [768], replicated
- ln2_bias_grad: float32 [768], replicated
- w_up_grad: float32 [768, 3072], P(None, 'narrow')
- b_up_grad: float32 [1, 3072], P(None, 'narrow')
- w_down_grad: float32 [3072, 768], P('narrow')
- b_down_grad: float32 [768], replicated
The draws below stay inside these ranges and needn't reach their ends.
Inputs may be any that keep to these rules, and one draw needn't show every extreme that they name: patch_counts[i] is the number of real patches of item i; key positions 40 + patch_counts[i] and later of that item are padding.
All inputs are finite; a program needn't handle non-finite values.
Results may differ from the reference program's by a relative error of at most 0.012.
The reference program's roundings to bfloat16 on the way count: a program that leaves them out, or rounds other values in their place, can miss the bound.
Values may be sent and summed in bfloat16 or wider, within the bound.
No kernel may reach another device: no remote copies, remote signals or barrier semaphores. Data moves between devices by JAX's collectives and lax.ppermute only.
A program may use at most 192 MiB of HBM per device.

```python
import jax
import jax.numpy as jnp
from jax import lax

D = 768
HEADS = 12
HEAD = 64
FF = 3072
WORDS = 40
PATCH_MIN = 100
PATCH_MAX = 240
SEQ = 280
ITEMS_GRP = 12
ITEMS = 96
TOKENS = 26880


def draw_patch_counts(key, part):
    key_first, key_second, key_third = jax.random.split(key, 3)
    counts = jax.random.randint(key_first, (ITEMS,), PATCH_MIN, PATCH_MAX + 1)
    top_slot = jax.random.randint(key_second, (), 0, ITEMS)
    least_slot = (top_slot + 1 + jax.random.randint(key_third, (), 0, ITEMS - 1)) % ITEMS
    positions = jnp.arange(ITEMS)
    counts = jnp.where(positions == top_slot, PATCH_MAX, counts)
    counts = jnp.where(positions == least_slot, PATCH_MIN, counts)
    return counts.astype(jnp.int32)


def block_levels(key, dims, pieces, least, largest):
    level = 1.0
    for position, parts in pieces:
        steps = jax.random.uniform(jax.random.fold_in(jax.random.fold_in(key, 6), position), (parts,), jnp.float32, least / len(pieces), largest / len(pieces))
        level = level * jnp.repeat(jnp.exp(steps), dims[position] // parts).reshape((-1,) + (1,) * (len(dims) - 1 - position))
    return level


def normal_values(key, shape, width, reach, shards=(), dtype=jnp.bfloat16):
    loudness = block_levels(key, shape, shards, -0.22, 0.18) if shards else 1.0
    result = jax.random.normal(key, shape, jnp.float32) * width * loudness
    return jnp.minimum(jnp.maximum(result, -reach), reach).astype(dtype)


def setup_inputs(seed: int = 0) -> dict:
    seeds = jax.random.split(jax.random.key(seed), 16)
    return {
        "tokens": normal_values(seeds[0], (TOKENS, D), 1.0, 6.0, ((0, 32),)),
        "patch_counts": draw_patch_counts(jax.random.fold_in(seeds[15], 71), 0),
        "ln1_gain": jnp.clip(1.0 + 0.15 * jax.random.normal(seeds[2], (D,), jnp.float32), 0.25, 1.75),
        "ln1_bias": normal_values(seeds[3], (D,), 0.5, 3.0, (), jnp.float32),
        "w_qkv": normal_values(seeds[4], (D, 3, D), D ** -0.5, 0.21875, ((2, 4),)),
        "b_qv": normal_values(seeds[5], (2, D), 0.5, 3.0, ((1, 4),), jnp.float32),
        "w_out": normal_values(seeds[6], (D, D), (D // 8) ** -0.5, 0.625, ((0, 4),)),
        "b_out": normal_values(seeds[7], (D,), 0.5, 3.0, (), jnp.float32),
        "ln2_gain": jnp.clip(1.0 + 0.15 * jax.random.normal(seeds[8], (D,), jnp.float32), 0.25, 1.75),
        "ln2_bias": normal_values(seeds[9], (D,), 0.5, 3.0, (), jnp.float32),
        "w_up": normal_values(seeds[10], (D, FF), D ** -0.5, 0.21875, ((1, 4),)),
        "b_up": normal_values(seeds[11], (1, FF), 0.5, 3.0, ((1, 4),)),
        "w_down": normal_values(seeds[12], (FF, D), FF ** -0.5, 0.109375, ((0, 4),)),
        "b_down": normal_values(seeds[13], (D,), 0.5, 3.0, (), jnp.float32),
        "cotangent": normal_values(seeds[14], (TOKENS, D), 1.0, 6.0, ((0, 32),)),
    }


@jax.custom_vjp
def low(v):
    return lax.optimization_barrier(v.astype(jnp.bfloat16)).astype(jnp.float32)

@jax.custom_vjp
def low_back(v):
    return v

def low_keep(v):
    return (low(v), None)

def low_pass(kept, grad):
    return (grad,)

def back_keep(v):
    return (v, None)

def back_low(kept, grad):
    return (low(grad),)
low.defvjp(low_keep, low_pass)
low_back.defvjp(back_keep, back_low)
norm_eps = 1e-06
masked_value = -1000000000.0
highest = lax.Precision.HIGHEST

def norm_rows(inputs, gain_row, bias_row):
    mean_rows = lax.optimization_barrier(jnp.mean(inputs, axis=-1, keepdims=True))
    centred = inputs - mean_rows
    var_rows = lax.optimization_barrier(jnp.mean(centred * centred, axis=-1, keepdims=True))
    return centred * lax.rsqrt(var_rows + norm_eps) * gain_row + bias_row

def attend_block(block_parts):
    queries, key_rows, value_rows, count_rows = block_parts
    scores = low_back(jnp.einsum('iqhe,ikhe->ihqk', queries, key_rows, precision=highest))
    positions = jnp.arange(SEQ)
    valid_keys = positions[None, :] < (WORDS + count_rows)[:, None]
    scores = scores + jnp.where(valid_keys, 0.0, masked_value)[:, None, None, :]
    weights = low(jax.nn.softmax(scores, axis=-1))
    return jnp.einsum('ihqk,ikhe->iqhe', weights, value_rows, precision=highest)

def forward(inputs, ln1_gain, ln1_bias, w_qkv, b_qv, w_out, b_out, ln2_gain, ln2_bias, w_up, b_up, w_down, b_down, patch_counts):
    normed1 = low(norm_rows(inputs, ln1_gain, ln1_bias))
    projected = jnp.einsum('td,dcf->tcf', normed1, w_qkv, precision=highest)
    queries = low(low_back((projected[:, 0] + b_qv[0]) * 0.125))
    key_rows = low(low_back(projected[:, 1]))
    value_rows = low(low_back(projected[:, 2] + b_qv[1]))
    blocks = ITEMS // ITEMS_GRP
    shaped = (blocks, ITEMS_GRP, SEQ, HEADS, HEAD)
    mixed = lax.map(jax.checkpoint(attend_block), (queries.reshape(shaped), key_rows.reshape(shaped), value_rows.reshape(shaped), patch_counts.reshape(blocks, ITEMS_GRP)))
    mixed = low(low_back(mixed.reshape(TOKENS, D)))
    middle = inputs + low_back(jnp.dot(mixed, w_out, precision=highest) + b_out)
    normed2 = low(norm_rows(middle, ln2_gain, ln2_bias))
    up_rows = low_back(jnp.dot(normed2, w_up, precision=highest) + b_up)
    hidden = low(jax.nn.gelu(up_rows, approximate=False))
    return middle + jnp.dot(hidden, w_down, precision=highest) + b_down

def reference(tokens, patch_counts, ln1_gain, ln1_bias, w_qkv, b_qv, w_out, b_out, ln2_gain, ln2_bias, w_up, b_up, w_down, b_down, cotangent):
    floats = tuple((member.astype(jnp.float32) for member in (tokens, ln1_gain, ln1_bias, w_qkv, b_qv, w_out, b_out, ln2_gain, ln2_bias, w_up, b_up, w_down, b_down)))

    def run_layer(*params):
        return forward(*params, patch_counts)
    layer_out, pull_back = jax.vjp(run_layer, *floats)
    gradients = pull_back(cotangent.astype(jnp.float32))
    return (layer_out, gradients[0], gradients[1], gradients[2], gradients[3], gradients[4], gradients[5], gradients[6], gradients[7], gradients[8], gradients[9], gradients[10], gradients[11], gradients[12])
```

```python
import functools

import jax
import jax.numpy as jnp
from jax import lax
from jax.experimental import pallas as pl
from jax.experimental.pallas import tpu as pltpu
from jax.sharding import PartitionSpec as P

HEAD = 64
WORDS = 40
PACK = 16
LANES = 128
BLOCK = 256

norm_eps = 1e-06
masked_value = -1000000000.0
bf = jnp.bfloat16
f32 = jnp.float32


def mul_nn(a, b):
    return lax.dot_general(a, b, (((1,), (0,)), ((), ())), preferred_element_type=f32)


def mul_nt(a, b):
    return lax.dot_general(a, b, (((1,), (1,)), ((), ())), preferred_element_type=f32)


def mul_tn(a, b):
    return lax.dot_general(a, b, (((0,), (0,)), ((), ())), preferred_element_type=f32)


def pad_rows(x, rows):
    if x.shape[0] == rows:
        return x
    return jnp.concatenate([x, jnp.zeros((rows - x.shape[0],) + x.shape[1:], x.dtype)], axis=0)


def unit_parts(x):
    centred = x - jnp.mean(x, axis=-1, keepdims=True)
    inv = lax.rsqrt(jnp.mean(centred * centred, axis=-1, keepdims=True) + norm_eps)
    return centred * inv, inv


def norm_back(grad, unit, inv, gain):
    scaled = grad * gain
    inner = (
        scaled
        - jnp.mean(scaled, axis=-1, keepdims=True)
        - unit * jnp.mean(scaled * unit, axis=-1, keepdims=True)
    )
    return inv * inner


def col_sum(x):
    return jnp.sum(x, axis=0, keepdims=True)


def full(shape):
    return pl.BlockSpec(shape, lambda *_: (0,) * len(shape))


def per_item(shape):
    return pl.BlockSpec((None,) + shape, lambda i, *_: (i,) + (0,) * len(shape))


def params(mib):
    return pltpu.CompilerParams(vmem_limit_bytes=mib << 20)


def attend_kernel(first, counts, tokens, gain, bias, w, b, *outs):
    if first:
        q_out, k_out, v_out, mixed_out, log_out, normed_out = outs
    else:
        q_out, k_out, v_out, mixed_out, log_out = outs
    rows, width = q_out.shape
    unit, _ = unit_parts(pad_rows(tokens[...].astype(f32), rows))
    normed = (unit * gain[...] + bias[...]).astype(bf)
    if first:
        normed_out[...] = normed
    q = ((mul_nt(normed, w[0]) + b[0:1]) * 0.125).astype(bf)
    k = mul_nt(normed, w[1]).astype(bf)
    v = (mul_nt(normed, w[2]) + b[1:2]).astype(bf)
    q_out[...] = q
    k_out[...] = k
    v_out[...] = v
    valid = WORDS + counts[pl.program_id(0)]
    mask = jnp.where(lax.broadcasted_iota(jnp.int32, (1, rows), 1) < valid, 0.0, masked_value)
    lane = lax.broadcasted_iota(jnp.int32, (rows, LANES), 1)
    low = lane < HEAD
    logs = jnp.zeros((rows, LANES), f32)
    for p in range(width // LANES):
        at = slice(p * LANES, (p + 1) * LANES)
        q_two, k_two, v_two = q[:, at], k[:, at], v[:, at]
        tops, sums = [], []
        for h in range(2):
            here = low if h == 0 else ~low
            scores = mul_nt(jnp.where(here, q_two, 0), k_two) + mask
            top = jnp.max(scores, axis=1, keepdims=True)
            shifted = jnp.exp(scores - top).astype(bf)
            sums.append(mul_nn(shifted, jnp.where(here, v_two, 1)))
            tops.append(top)
        total = pltpu.roll(jnp.where(low, sums[1], sums[0]), HEAD, 1)
        mixed_out[:, at] = (jnp.where(low, sums[0], sums[1]) / total).astype(bf)
        log_two = jnp.log(total)
        logs = jnp.where(lane == 2 * p, tops[0] + log_two[:, 0:1], logs)
        logs = jnp.where(lane == 2 * p + 1, tops[1] + log_two[:, HEAD : HEAD + 1], logs)
    log_out[...] = logs.T[: log_out.shape[0]]


def attend(first, counts, tokens, gain, bias, w, b, rows):
    items, _, dim = tokens.shape
    width = w.shape[1]
    wide_out = jax.ShapeDtypeStruct((items, rows, width), bf)
    outs = [wide_out] * 4 + [jax.ShapeDtypeStruct((items, 8, rows), f32)]
    specs = [per_item((rows, width))] * 4 + [per_item((8, rows))]
    if first:
        outs.append(jax.ShapeDtypeStruct((items, rows, dim), bf))
        specs.append(per_item((rows, dim)))
    return pl.pallas_call(
        functools.partial(attend_kernel, first),
        grid_spec=pltpu.PrefetchScalarGridSpec(
            num_scalar_prefetch=1,
            grid=(items,),
            in_specs=[
                per_item(tokens.shape[1:]),
                full((1, dim)),
                full((1, dim)),
                full(w.shape),
                full(b.shape),
            ],
            out_specs=specs,
        ),
        out_shape=outs,
        compiler_params=params(32),
        cost_estimate=pl.CostEstimate(
            flops=items * rows * (6 * dim * width + 24 * width // HEAD * LANES * rows),
            bytes_accessed=items * rows * (dim * 4 + width * 8) + w.size * 2,
            transcendentals=items * rows * rows * width // HEAD,
        ),
        name="attend",
    )(counts, tokens, gain, bias, w, b)


def branch_kernel(tokens, cot, mixed_a, mixed_b, w_a, w_b, b_out, gain, bias, middle_out, normed_out, cot_out):
    rows = normed_out.shape[0]
    middle = (
        pad_rows(tokens[...].astype(f32), rows)
        + (mul_nn(mixed_a[...], w_a[...]) + mul_nn(mixed_b[...], w_b[...]))
        + b_out[...]
    )
    middle_out[...] = middle
    unit, _ = unit_parts(middle)
    normed_out[...] = (unit * gain[...] + bias[...]).astype(bf)
    cot_out[...] = pad_rows(cot[...].astype(f32), rows).astype(bf)


def branch(tokens, cot, mixed_a, mixed_b, w_a, w_b, b_out, gain, bias):
    items, seq, dim = tokens.shape
    _, rows, width = mixed_a.shape
    return pl.pallas_call(
        branch_kernel,
        grid=(items,),
        in_specs=[per_item((seq, dim))] * 2
        + [per_item((rows, width))] * 2
        + [full(w_a.shape)] * 2
        + [full((1, dim))] * 3,
        out_specs=[per_item((rows, dim))] * 3,
        out_shape=[
            jax.ShapeDtypeStruct((items, rows, dim), f32),
            jax.ShapeDtypeStruct((items, rows, dim), bf),
            jax.ShapeDtypeStruct((items, rows, dim), bf),
        ],
        compiler_params=params(24),
        cost_estimate=pl.CostEstimate(
            flops=items * rows * 4 * dim * width,
            bytes_accessed=items * rows * dim * 16,
            transcendentals=items * rows,
        ),
        name="branch",
    )(tokens, cot, mixed_a, mixed_b, w_a, w_b, b_out, gain, bias)


def feed_kernel(
    last, per, normed, cot, base, base_grad, b_down, up_a, up_b, down_a, down_b, b_up,
    out_ref, grad_ref, dup_ref, ddown_ref, dbias_ref, hidden_ref, gu_ref, *scratch
):
    step = pl.program_id(0)
    items, rows, dim = normed.shape
    acc = scratch[0] if last else out_ref
    is_a = step < per

    @pl.when(step == 0)
    def _():
        if last:
            acc[...] = base[...]
            grad_ref[...] = base_grad[...]
        else:
            acc[...] = base[...] + b_down[...][None]
            grad_ref[...] = jnp.zeros_like(grad_ref)

    w_up = jnp.where(is_a, up_a[...], up_b[...])
    w_down = jnp.where(is_a, down_a[...], down_b[...])
    bias_sum = jnp.zeros((1, w_up.shape[1]), f32)
    for i in range(items):
        up = mul_nn(normed[i], w_up) + b_up[...]
        grad_hidden = mul_nt(cot[i], w_down)
        cdf = 0.5 * (1.0 + lax.erf(up * 0.7071067811865476))
        slope = cdf + up * (jnp.exp(-0.5 * up * up) * 0.3989422804014327)
        hidden = (up * cdf).astype(bf)
        gu = (slope * grad_hidden).astype(bf)
        hidden_ref[i] = hidden
        gu_ref[i] = gu
        bias_sum = bias_sum + col_sum(gu.astype(f32))
        acc[i] += mul_nn(hidden, w_down)
        grad_ref[i] += mul_nt(gu, w_up)
    dbias_ref[...] = bias_sum
    flat = (items * rows, dim)
    hidden = hidden_ref[...].reshape(items * rows, -1)
    gu = gu_ref[...].reshape(items * rows, -1)
    ddown_ref[...] = mul_tn(hidden, cot[...].reshape(flat)).astype(bf)
    dup_ref[...] = mul_tn(normed[...].reshape(flat), gu).astype(bf)
    if last:

        @pl.when(step == pl.num_programs(0) - 1)
        def _():
            for i in range(items):
                out_ref[i] = acc[i, : out_ref.shape[1]]


def feed(last, normed, cot, base, base_grad, b_down, up_a, up_b, down_a, down_b, b_up, seq):
    items, rows, dim = normed.shape
    units = up_a.shape[1]
    per = units // BLOCK
    steps = 2 * per
    out_rows = seq if last else rows
    full3 = full((items, rows, dim))
    if not last:
        base_grad = b_down
    scratch = [pltpu.VMEM((items, rows, BLOCK), bf)] * 2
    if last:
        scratch.append(pltpu.VMEM((items, rows, dim), f32))
    return pl.pallas_call(
        functools.partial(feed_kernel, last, per),
        grid=(steps,),
        in_specs=[
            full3,
            full3,
            full3,
            full3 if last else full((1, dim)),
            full((1, dim)),
            pl.BlockSpec((dim, BLOCK), lambda j: (0, jnp.minimum(j, per - 1))),
            pl.BlockSpec((dim, BLOCK), lambda j: (0, jnp.maximum(j - per, 0))),
            pl.BlockSpec((BLOCK, dim), lambda j: (jnp.minimum(j, per - 1), 0)),
            pl.BlockSpec((BLOCK, dim), lambda j: (jnp.maximum(j - per, 0), 0)),
            pl.BlockSpec((1, BLOCK), lambda j: (0, j)),
        ],
        out_specs=[
            full((items, out_rows, dim)),
            full3,
            pl.BlockSpec((None, dim, BLOCK), lambda j: (j // per, 0, j % per)),
            pl.BlockSpec((None, BLOCK, dim), lambda j: (j // per, j % per, 0)),
            pl.BlockSpec((1, BLOCK), lambda j: (0, j)),
        ],
        out_shape=[
            jax.ShapeDtypeStruct((items, out_rows, dim), f32),
            jax.ShapeDtypeStruct((items, rows, dim), f32),
            jax.ShapeDtypeStruct((2, dim, units), bf),
            jax.ShapeDtypeStruct((2, units, dim), bf),
            jax.ShapeDtypeStruct((1, 2 * units), f32),
        ],
        scratch_shapes=scratch,
        compiler_params=params(56),
        cost_estimate=pl.CostEstimate(
            flops=steps * items * rows * dim * BLOCK * 12,
            bytes_accessed=items * rows * dim * 20 + units * dim * 16,
            transcendentals=steps * items * rows * BLOCK * 2,
        ),
        name="feed",
    )(normed, cot, base, base_grad, b_down, up_a, up_b, down_a, down_b, b_up)


def unbranch_kernel(
    middle, cot, grad_in, gain, mixed_a, mixed_b, w_a, w_b,
    grad_out, gmix_a, gmix_b, dw_out, small, branch_ref
):
    step = pl.program_id(0)
    unit, inv = unit_parts(middle[...])
    grad = grad_in[...]
    cot_f = cot[...].astype(f32)
    grad_middle = cot_f + norm_back(grad, unit, inv, gain[...])
    grad_out[...] = grad_middle
    grad_branch = grad_middle.astype(bf)
    branch_ref[step] = grad_branch
    gmix_a[...] = mul_nt(grad_branch, w_a[...]).astype(bf)
    gmix_b[...] = mul_nt(grad_branch, w_b[...]).astype(bf)

    @pl.when(step == 0)
    def _():
        small[...] = jnp.zeros_like(small)

    small[0:1] += col_sum(grad * unit)
    small[1:2] += col_sum(grad)
    small[2:3] += col_sum(grad_branch.astype(f32))
    small[3:4] += col_sum(cot_f)

    @pl.when(step == pl.num_programs(0) - 1)
    def _():
        items, rows, dim = branch_ref.shape
        gb = branch_ref[...].reshape(items * rows, dim)
        width = mixed_a.shape[2]
        quarter = width // 2
        for n, mixed in ((0, mixed_a), (1, mixed_b)):
            dw = mul_tn(mixed[...].reshape(items * rows, width), gb).astype(bf)
            dw_out[2 * n] = dw[:quarter]
            dw_out[2 * n + 1] = dw[quarter:]


def unbranch(middle, cot, grad_in, gain, mixed_a, mixed_b, w_a, w_b):
    items, rows, dim = middle.shape
    width = mixed_a.shape[2]
    each = per_item((rows, dim))
    return pl.pallas_call(
        unbranch_kernel,
        grid=(items,),
        in_specs=[each, each, each, full((1, dim))]
        + [full(mixed_a.shape)] * 2
        + [full(w_a.shape)] * 2,
        out_specs=[
            each,
            per_item((rows, width)),
            per_item((rows, width)),
            full((4, width // 2, dim)),
            full((8, dim)),
        ],
        out_shape=[
            jax.ShapeDtypeStruct((items, rows, dim), f32),
            jax.ShapeDtypeStruct((items, rows, width), bf),
            jax.ShapeDtypeStruct((items, rows, width), bf),
            jax.ShapeDtypeStruct((4, width // 2, dim), bf),
            jax.ShapeDtypeStruct((8, dim), f32),
        ],
        scratch_shapes=[pltpu.VMEM((items, rows, dim), bf)],
        compiler_params=params(32),
        cost_estimate=pl.CostEstimate(
            flops=items * rows * 8 * dim * width,
            bytes_accessed=items * rows * dim * 20,
            transcendentals=items * rows,
        ),
        name="unbranch",
    )(middle, cot, grad_in, gain, mixed_a, mixed_b, w_a, w_b)


def unattend_kernel(final, counts, q, k, v, gmix, logs, normed, w, *refs):
    if final:
        grad_in, grad_middle, tokens, gain, x_out, dw_out, db_out, small, g_ref = refs
    else:
        x_out, dw_out, db_out, g_ref = refs
    step = pl.program_id(0)
    rows, width = q.shape
    valid = WORDS + counts[step]
    mask = jnp.where(lax.broadcasted_iota(jnp.int32, (rows, 1), 0) < valid, 0.0, masked_value)
    low = lax.broadcasted_iota(jnp.int32, (rows, LANES), 1) < HEAD
    for p in range(width // LANES):
        at = slice(p * LANES, (p + 1) * LANES)
        q_two, k_two, v_two, g_two = q[:, at], k[:, at], v[:, at], gmix[:, at]
        dq, dk, dv = [], [], []
        for h in range(2):
            here = low if h == 0 else ~low
            scores = mul_nt(jnp.where(here, k_two, 0), q_two) + mask
            prob = jnp.exp(scores - logs[2 * p + h : 2 * p + h + 1])
            grad_prob = mul_nt(jnp.where(here, v_two, 0), g_two)
            inner = jnp.sum(grad_prob * prob, axis=0, keepdims=True)
            grad_scores = (prob * (grad_prob - inner)).astype(bf)
            dv.append(mul_nn(prob.astype(bf), g_two))
            dk.append(mul_nn(grad_scores, q_two))
            dq.append(mul_tn(grad_scores, k_two))
        for c, pair in enumerate((dq, dk, dv)):
            merged = jnp.where(low, pair[0], pair[1]).astype(bf)
            if c == 0:
                merged = merged * jnp.asarray(0.125, bf)
            g_ref[step, :, c * width + p * LANES : c * width + (p + 1) * LANES] = merged
    g = g_ref[step]
    grad = mul_nn(g, w[...].reshape(3 * width, -1))

    @pl.when(step == 0)
    def _():
        db_out[...] = jnp.zeros_like(db_out)
        if final:
            small[...] = jnp.zeros_like(small)

    sums = col_sum(g.astype(f32))
    db_out[0:1] += sums[:, :width]
    db_out[1:2] += sums[:, 2 * width :]
    if final:
        grad = grad + grad_in[...]
        unit, inv = unit_parts(pad_rows(tokens[...].astype(f32), rows))
        small[0:1] += col_sum(grad * unit)
        small[1:2] += col_sum(grad)
        seq = x_out.shape[0]
        x_out[...] = (grad_middle[...] + norm_back(grad, unit, inv, gain[...]))[:seq]
    else:
        x_out[...] = grad

    @pl.when(step == pl.num_programs(0) - 1)
    def _():
        items = g_ref.shape[0]
        flat = normed[...].reshape(items * rows, -1)
        dw = mul_tn(g_ref[...].reshape(items * rows, 3 * width), flat).astype(bf)
        quarter = width // 2
        for c in range(3):
            dw_out[0, c] = dw[c * width : c * width + quarter]
            dw_out[1, c] = dw[c * width + quarter : (c + 1) * width]


def unattend(counts, q, k, v, gmix, logs, normed, w, rest=None):
    final = rest is not None
    items, rows, width = q.shape
    dim = normed.shape[2]
    wide = per_item((rows, width))
    specs = [wide] * 4 + [per_item((8, rows)), full(normed.shape), full(w.shape)]
    args = [counts, q, k, v, gmix, logs, normed, w]
    out_rows = rows
    extra_out, extra_spec = [], []
    if final:
        grad_in, grad_middle, tokens, gain = rest
        out_rows = tokens.shape[1]
        specs += [per_item((rows, dim))] * 2 + [per_item(tokens.shape[1:]), full((1, dim))]
        args += list(rest)
        extra_out, extra_spec = [jax.ShapeDtypeStruct((8, dim), f32)], [full((8, dim))]
    return pl.pallas_call(
        functools.partial(unattend_kernel, final),
        grid_spec=pltpu.PrefetchScalarGridSpec(
            num_scalar_prefetch=1,
            grid=(items,),
            in_specs=specs,
            out_specs=[
                per_item((out_rows, dim)),
                full((2, 3, width // 2, dim)),
                full((8, width)),
            ]
            + extra_spec,
            scratch_shapes=[pltpu.VMEM((items, rows, 3 * width), bf)],
        ),
        out_shape=[
            jax.ShapeDtypeStruct((items, out_rows, dim), f32),
            jax.ShapeDtypeStruct((2, 3, width // 2, dim), bf),
            jax.ShapeDtypeStruct((8, width), f32),
        ]
        + extra_out,
        compiler_params=params(40),
        cost_estimate=pl.CostEstimate(
            flops=items * rows * (12 * dim * width + 60 * width // HEAD * LANES * rows),
            bytes_accessed=items * rows * (dim * 8 + width * 8) + w.size * 4,
            transcendentals=items * rows * rows * width // HEAD,
        ),
        name="unattend",
    )(*args)


def exchange(x, axis, size, mask):
    return lax.ppermute(x, axis, [(i, i ^ mask) for i in range(size)])


def reduce_over(x, axis, size):
    masks = []
    mask = 1
    while mask < size:
        masks.append(mask)
        mask *= 2
    me = lax.axis_index(axis)
    for mask in masks:
        half = x.shape[0] // 2
        up = (me // mask) % 2
        sent = lax.dynamic_slice_in_dim(x, (1 - up) * half, half, 0)
        kept = lax.dynamic_slice_in_dim(x, up * half, half, 0)
        got = exchange(sent, axis, size, mask)
        x = (kept.astype(f32) + got.astype(f32)).astype(bf)
    for mask in reversed(masks):
        up = (me // mask) % 2
        got = exchange(x, axis, size, mask)
        first = jnp.where(up == 0, x, got)
        second = jnp.where(up == 0, got, x)
        x = jnp.concatenate([first, second], axis=0)
    return x


def add_bf(*parts):
    total = parts[0].astype(f32)
    for part in parts[1:]:
        total = total + part.astype(f32)
    return total.astype(bf)


def own_quarter(quarters, narrow):
    one = exchange(quarters[1], "narrow", narrow, 1)
    three = exchange(quarters[3], "narrow", narrow, 1)
    peer = exchange(add_bf(quarters[2], three), "narrow", narrow, 2)
    return add_bf(quarters[0], one, peer)


def on_device(
    wide,
    narrow,
    tokens,
    patch_counts,
    ln1_gain,
    ln1_bias,
    w_qkv,
    b_qv,
    w_out,
    b_out,
    ln2_gain,
    ln2_bias,
    w_up,
    b_up,
    w_down,
    b_down,
    cotangent,
):
    own_rows, dim = tokens.shape
    items = patch_counts.shape[0] // narrow
    seq = own_rows // items
    rows = -(-seq // PACK) * PACK
    heads = w_qkv.shape[2]
    units = w_up.shape[1]
    me = lax.axis_index("narrow")
    counts = lax.dynamic_slice_in_dim(patch_counts, me * items, items, 0)
    tokens3 = tokens.reshape(items, seq, dim)
    cot3 = cotangent.reshape(items, seq, dim)
    row = lambda x: x.reshape(1, dim)

    w_flat = w_qkv.transpose(1, 2, 0)
    small_in = jnp.concatenate(
        [
            jnp.pad(b_qv, ((0, 0), (0, dim - heads))),
            jnp.pad(b_up.astype(f32), ((0, 5), (0, dim - units))),
        ],
        axis=0,
    )

    def others(x):
        mate = exchange(x, "narrow", narrow, 1)
        peer = exchange(x, "narrow", narrow, 2)
        return x, mate, peer, exchange(peer, "narrow", narrow, 1)

    qkv4 = others(w_flat)
    out4 = others(w_out)
    small4 = others(small_in)
    up4 = others(w_up)
    down4 = others(w_down)

    def half(four, n, axis):
        return jnp.concatenate([four[2 * n], four[2 * n + 1]], axis=axis)

    w_half = [half(qkv4, n, 1) for n in range(2)]
    out_half = [half(out4, n, 0) for n in range(2)]
    b_half = [half([s[:2, :heads] for s in small4], n, 1) for n in range(2)]
    up_bias = [half([s[2:3, :units] for s in small4], n, 1) for n in range(2)]

    q_a, k_a, v_a, mixed_a, log_a, normed1 = attend(
        True, counts, tokens3, row(ln1_gain), row(ln1_bias), w_half[0], b_half[0], rows
    )
    q_b, k_b, v_b, mixed_b, log_b = attend(
        False, counts, tokens3, row(ln1_gain), row(ln1_bias), w_half[1], b_half[1], rows
    )
    middle, normed2, cot_pad = branch(
        tokens3, cot3, mixed_a, mixed_b, out_half[0], out_half[1], row(b_out), row(ln2_gain), row(ln2_bias)
    )
    part, grad_part, dup_a, ddown_a, dbias_a = feed(
        False, normed2, cot_pad, middle, None, row(b_down),
        up4[0], up4[1], down4[0], down4[1], up_bias[0], seq,
    )
    layer_out, grad_norm2, dup_b, ddown_b, dbias_b = feed(
        True, normed2, cot_pad, part, grad_part, row(b_down),
        up4[2], up4[3], down4[2], down4[3], up_bias[1], seq,
    )
    grad_middle, gmix_a, gmix_b, dw_out, small_two = unbranch(
        middle, cot_pad, grad_norm2, row(ln2_gain), mixed_a, mixed_b, out_half[0], out_half[1]
    )
    grad_one, dqkv_b, dbqv_b = unattend(counts, q_b, k_b, v_b, gmix_b, log_b, normed1, w_half[1])
    input_grad, dqkv_a, dbqv_a, small_one = unattend(
        counts, q_a, k_a, v_a, gmix_a, log_a, normed1, w_half[0],
        (grad_one, grad_middle, tokens3, row(ln1_gain)),
    )

    feed_quarters = [
        jnp.concatenate([du[n], dd[n]], axis=0)
        for du, dd in ((dup_a, ddown_a), (dup_b, ddown_b))
        for n in range(2)
    ]
    feed_sum = reduce_over(own_quarter(feed_quarters, narrow), "wide", wide)

    vectors = [small_one[0:1], small_one[1:2]] + [small_two[n : n + 1] for n in range(4)]
    quarters = []
    for n in range(4):
        dqkv, dbqv, dbias = ((dqkv_a, dbqv_a, dbias_a), (dqkv_b, dbqv_b, dbias_b))[n // 2]
        at = n % 2
        tail = vectors + [
            dbias[:, at * units : (at + 1) * units],
            jnp.pad(dbqv[0:2, at * heads : (at + 1) * heads], ((0, 0), (0, dim - heads))),
        ]
        tail = jnp.concatenate(tail, axis=0)
        total_rows = 4 * heads + tail.shape[0]
        pad = -total_rows % (8 * wide)
        tail = jnp.pad(tail, ((0, pad), (0, 0))).astype(bf)
        quarters.append(
            jnp.concatenate([dqkv[at].reshape(3 * heads, dim), dw_out[n], tail], axis=0)
        )
    rest_sum = reduce_over(own_quarter(quarters, narrow), "wide", wide).astype(f32)
    feed_sum = feed_sum.astype(f32)
    vec = rest_sum[4 * heads :]
    return (
        layer_out.reshape(own_rows, dim),
        input_grad.reshape(own_rows, dim),
        vec[0],
        vec[1],
        rest_sum[: 3 * heads].reshape(3, heads, dim).transpose(2, 0, 1),
        vec[7:9, :heads],
        rest_sum[3 * heads : 4 * heads],
        vec[4],
        vec[2],
        vec[3],
        feed_sum[:dim],
        vec[6:7, :units],
        feed_sum[dim:],
        vec[5],
    )


def solution(mesh):
    wide, narrow = mesh.shape["wide"], mesh.shape["narrow"]
    assert narrow == 4 and wide & (wide - 1) == 0
    rows = P(("wide", "narrow"), None)
    return jax.shard_map(
        functools.partial(on_device, wide, narrow),
        mesh=mesh,
        in_specs=(
            rows,
            P("wide"),
            P(),
            P(),
            P(None, None, "narrow"),
            P(None, "narrow"),
            P("narrow", None),
            P(),
            P(),
            P(),
            P(None, "narrow"),
            P(None, "narrow"),
            P("narrow", None),
            P(),
            rows,
        ),
        out_specs=(
            rows,
            rows,
            P(),
            P(),
            P(None, None, "narrow"),
            P(None, "narrow"),
            P("narrow", None),
            P(),
            P(),
            P(),
            P(None, "narrow"),
            P(None, "narrow"),
            P("narrow", None),
            P(),
        ),
        check_vma=False,
    )
```

```python
import functools

import jax
import jax.numpy as jnp
from jax import lax
from jax.experimental import pallas as pl
from jax.experimental.pallas import tpu as pltpu
from jax.sharding import PartitionSpec as P

HEAD = 64
WORDS = 40
PACK = 16
LANES = 128
BLOCK = 256

norm_eps = 1e-06
masked_value = -1000000000.0
bf = jnp.bfloat16
f32 = jnp.float32


def mul_nn(a, b):
    return lax.dot_general(a, b, (((1,), (0,)), ((), ())), preferred_element_type=f32)


def mul_nt(a, b):
    return lax.dot_general(a, b, (((1,), (1,)), ((), ())), preferred_element_type=f32)


def mul_tn(a, b):
    return lax.dot_general(a, b, (((0,), (0,)), ((), ())), preferred_element_type=f32)


def pad_rows(x, rows):
    if x.shape[0] == rows:
        return x
    return jnp.concatenate([x, jnp.zeros((rows - x.shape[0],) + x.shape[1:], x.dtype)], axis=0)


def unit_parts(x):
    centred = x - jnp.mean(x, axis=-1, keepdims=True)
    inv = lax.rsqrt(jnp.mean(centred * centred, axis=-1, keepdims=True) + norm_eps)
    return centred * inv, inv


def norm_back(grad, unit, inv, gain):
    scaled = grad * gain
    inner = (
        scaled
        - jnp.mean(scaled, axis=-1, keepdims=True)
        - unit * jnp.mean(scaled * unit, axis=-1, keepdims=True)
    )
    return inv * inner


def col_sum(x):
    return jnp.sum(x, axis=0, keepdims=True)


def full(shape):
    return pl.BlockSpec(shape, lambda *_: (0,) * len(shape))


def per_item(shape):
    return pl.BlockSpec((None,) + shape, lambda i, *_: (i,) + (0,) * len(shape))


TIMES = {"attend": 10, "branch": 3, "feed": 24, "unbranch": 6, "unattend": 13, "outer": 3}


def lasting(us):
    return pl.CostEstimate(flops=int(us * 1.15e9), bytes_accessed=0, transcendentals=0)


def params(mib):
    return pltpu.CompilerParams(vmem_limit_bytes=mib << 20)


def attend_kernel(first, counts, tokens, gain, bias, w, b, *outs):
    if first:
        q_out, k_out, v_out, mixed_out, log_out, normed_out = outs
    else:
        q_out, k_out, v_out, mixed_out, log_out = outs
    rows, width = q_out.shape
    unit, _ = unit_parts(pad_rows(tokens[...].astype(f32), rows))
    normed = (unit * gain[...] + bias[...]).astype(bf)
    if first:
        normed_out[...] = normed
    q = ((mul_nt(normed, w[0]) + b[0:1]) * 0.125).astype(bf)
    k = mul_nt(normed, w[1]).astype(bf)
    v = (mul_nt(normed, w[2]) + b[1:2]).astype(bf)
    q_out[...] = q
    k_out[...] = k
    v_out[...] = v
    valid = WORDS + counts[pl.program_id(0)]
    mask = jnp.where(lax.broadcasted_iota(jnp.int32, (1, rows), 1) < valid, 0.0, masked_value)
    lane = lax.broadcasted_iota(jnp.int32, (rows, LANES), 1)
    low = lane < HEAD
    logs = jnp.zeros((rows, LANES), f32)
    for p in range(width // LANES):
        at = slice(p * LANES, (p + 1) * LANES)
        q_two, k_two, v_two = q[:, at], k[:, at], v[:, at]
        tops, sums = [], []
        for h in range(2):
            here = low if h == 0 else ~low
            scores = mul_nt(jnp.where(here, q_two, 0), k_two) + mask
            top = jnp.max(scores, axis=1, keepdims=True)
            shifted = jnp.exp(scores - top).astype(bf)
            sums.append(mul_nn(shifted, jnp.where(here, v_two, 1)))
            tops.append(top)
        total = pltpu.roll(jnp.where(low, sums[1], sums[0]), HEAD, 1)
        mixed_out[:, at] = (jnp.where(low, sums[0], sums[1]) / total).astype(bf)
        log_two = jnp.log(total)
        logs = jnp.where(lane == 2 * p, tops[0] + log_two[:, 0:1], logs)
        logs = jnp.where(lane == 2 * p + 1, tops[1] + log_two[:, HEAD : HEAD + 1], logs)
    log_out[...] = logs.T[: log_out.shape[0]]


def attend(first, counts, tokens, gain, bias, w, b, rows):
    items, _, dim = tokens.shape
    width = w.shape[1]
    wide_out = jax.ShapeDtypeStruct((items, rows, width), bf)
    outs = [wide_out] * 4 + [jax.ShapeDtypeStruct((items, 8, rows), f32)]
    specs = [per_item((rows, width))] * 4 + [per_item((8, rows))]
    if first:
        outs.append(jax.ShapeDtypeStruct((items, rows, dim), bf))
        specs.append(per_item((rows, dim)))
    return pl.pallas_call(
        functools.partial(attend_kernel, first),
        grid_spec=pltpu.PrefetchScalarGridSpec(
            num_scalar_prefetch=1,
            grid=(items,),
            in_specs=[
                per_item(tokens.shape[1:]),
                full((1, dim)),
                full((1, dim)),
                full(w.shape),
                full(b.shape),
            ],
            out_specs=specs,
        ),
        out_shape=outs,
        compiler_params=params(32),
        cost_estimate=lasting(TIMES["attend"]),
        name="attend",
    )(counts, tokens, gain, bias, w, b)


def branch_kernel(tokens, cot, mixed_a, mixed_b, w_a, w_b, b_out, gain, bias, middle_out, normed_out, cot_out):
    rows = normed_out.shape[0]
    middle = (
        pad_rows(tokens[...].astype(f32), rows)
        + (mul_nn(mixed_a[...], w_a[...]) + mul_nn(mixed_b[...], w_b[...]))
        + b_out[...]
    )
    middle_out[...] = middle
    unit, _ = unit_parts(middle)
    normed_out[...] = (unit * gain[...] + bias[...]).astype(bf)
    cot_out[...] = pad_rows(cot[...].astype(f32), rows).astype(bf)


def branch(tokens, cot, mixed_a, mixed_b, w_a, w_b, b_out, gain, bias):
    items, seq, dim = tokens.shape
    _, rows, width = mixed_a.shape
    return pl.pallas_call(
        branch_kernel,
        grid=(items,),
        in_specs=[per_item((seq, dim))] * 2
        + [per_item((rows, width))] * 2
        + [full(w_a.shape)] * 2
        + [full((1, dim))] * 3,
        out_specs=[per_item((rows, dim))] * 3,
        out_shape=[
            jax.ShapeDtypeStruct((items, rows, dim), f32),
            jax.ShapeDtypeStruct((items, rows, dim), bf),
            jax.ShapeDtypeStruct((items, rows, dim), bf),
        ],
        compiler_params=params(24),
        cost_estimate=lasting(TIMES["branch"]),
        name="branch",
    )(tokens, cot, mixed_a, mixed_b, w_a, w_b, b_out, gain, bias)


def feed_kernel(last, per, low_half, normed, cot, base, base_grad, b_down, *refs):
    n_weights = 8 if last else 4
    weights, (b_up, out_ref, grad_ref, dup_ref, ddown_ref, dbias_ref, hidden_ref, gu_ref, *scratch) = (
        refs[:n_weights],
        refs[n_weights:],
    )
    step = pl.program_id(0)
    items, rows, dim = normed.shape
    acc = scratch[0] if last else out_ref
    is_a = step < per

    @pl.when(step == 0)
    def _():
        if last:
            acc[...] = base[...]
            grad_ref[...] = base_grad[...]
        else:
            acc[...] = base[...] + b_down[...][None]
            grad_ref[...] = jnp.zeros_like(grad_ref)

    if last:
        up_a, up_b, up_c, up_d, down_a, down_b, down_c, down_d = weights
        is_low = low_half[0] == 0

        def joined(first, second, axis):
            low = jnp.where(is_low, first, second)
            high = jnp.where(is_low, second, first)
            return jnp.concatenate([low, high], axis=axis)

        w_up = joined(
            jnp.where(is_a, up_a[...], up_c[...]), jnp.where(is_a, up_b[...], up_d[...]), 0
        )
        w_down = joined(
            jnp.where(is_a, down_a[...], down_c[...]), jnp.where(is_a, down_b[...], down_d[...]), 1
        )
    else:
        up_a, up_c, down_a, down_c = weights
        w_up = jnp.where(is_a, up_a[...], up_c[...])
        w_down = jnp.where(is_a, down_a[...], down_c[...])
    bias_sum = jnp.zeros((1, w_up.shape[1]), f32)
    for i in range(items):
        up = mul_nn(normed[i], w_up) + b_up[...]
        grad_hidden = mul_nt(cot[i], w_down)
        cdf = 0.5 * (1.0 + lax.erf(up * 0.7071067811865476))
        slope = cdf + up * (jnp.exp(-0.5 * up * up) * 0.3989422804014327)
        hidden = (up * cdf).astype(bf)
        gu = (slope * grad_hidden).astype(bf)
        hidden_ref[i] = hidden
        gu_ref[i] = gu
        bias_sum = bias_sum + col_sum(gu.astype(f32))
        acc[i] += mul_nn(hidden, w_down)
        grad_ref[i] += mul_nt(gu, w_up)
    dbias_ref[...] = bias_sum
    flat = (items * rows, dim)
    hidden = hidden_ref[...].reshape(items * rows, -1)
    gu = gu_ref[...].reshape(items * rows, -1)
    ddown_ref[...] = mul_tn(hidden, cot[...].reshape(flat)).astype(bf)
    dup_ref[...] = mul_tn(normed[...].reshape(flat), gu).astype(bf)
    if last:

        @pl.when(step == pl.num_programs(0) - 1)
        def _():
            for i in range(items):
                out_ref[i] = acc[i, : out_ref.shape[1]]


def feed(last, low_half, normed, cot, base, base_grad, b_down, ups, downs, b_up, seq):
    items, rows, dim = normed.shape
    units = ups[0].shape[1]
    per = units // BLOCK
    steps = 2 * per
    out_rows = seq if last else rows
    full3 = full((items, rows, dim))
    if not last:
        base_grad = b_down
    scratch = [pltpu.VMEM((items, rows, BLOCK), bf)] * 2
    if last:
        scratch.append(pltpu.VMEM((items, rows, dim), f32))
    part = dim // (len(ups) // 2)
    half = len(ups) // 2
    first = lambda j: jnp.minimum(j, per - 1)
    second = lambda j: jnp.maximum(j - per, 0)
    return pl.pallas_call(
        functools.partial(feed_kernel, last, per),
        grid_spec=pltpu.PrefetchScalarGridSpec(
            num_scalar_prefetch=1,
            grid=(steps,),
            in_specs=[
                full3,
                full3,
                full3,
                full3 if last else full((1, dim)),
                full((1, dim)),
            ]
            + [pl.BlockSpec((part, BLOCK), lambda j, *_: (0, first(j)))] * half
            + [pl.BlockSpec((part, BLOCK), lambda j, *_: (0, second(j)))] * half
            + [pl.BlockSpec((BLOCK, part), lambda j, *_: (first(j), 0))] * half
            + [pl.BlockSpec((BLOCK, part), lambda j, *_: (second(j), 0))] * half
            + [pl.BlockSpec((1, BLOCK), lambda j, *_: (0, j))],
            out_specs=[
                full((items, out_rows, dim)),
                full3,
                pl.BlockSpec((None, dim, BLOCK), lambda j, *_: (j // per, 0, j % per)),
                pl.BlockSpec((None, BLOCK, dim), lambda j, *_: (j // per, j % per, 0)),
                pl.BlockSpec((1, BLOCK), lambda j, *_: (0, j)),
            ],
            scratch_shapes=scratch,
        ),
        out_shape=[
            jax.ShapeDtypeStruct((items, out_rows, dim), f32),
            jax.ShapeDtypeStruct((items, rows, dim), f32),
            jax.ShapeDtypeStruct((2, dim, units), bf),
            jax.ShapeDtypeStruct((2, units, dim), bf),
            jax.ShapeDtypeStruct((1, 2 * units), f32),
        ],
        compiler_params=params(56),
        cost_estimate=lasting(TIMES["feed"]),
        name="feed",
    )(low_half, normed, cot, base, base_grad, b_down, *ups, *downs, b_up)


def unbranch_kernel(
    middle, cot, grad_in, gain, mixed_a, mixed_b, w_a, w_b,
    grad_out, gmix_a, gmix_b, dw_out, small, branch_ref
):
    step = pl.program_id(0)
    unit, inv = unit_parts(middle[...])
    grad = grad_in[...]
    cot_f = cot[...].astype(f32)
    grad_middle = cot_f + norm_back(grad, unit, inv, gain[...])
    grad_out[...] = grad_middle
    grad_branch = grad_middle.astype(bf)
    branch_ref[step] = grad_branch
    gmix_a[...] = mul_nt(grad_branch, w_a[...]).astype(bf)
    gmix_b[...] = mul_nt(grad_branch, w_b[...]).astype(bf)

    @pl.when(step == 0)
    def _():
        small[...] = jnp.zeros_like(small)

    small[0:1] += col_sum(grad * unit)
    small[1:2] += col_sum(grad)
    small[2:3] += col_sum(grad_branch.astype(f32))
    small[3:4] += col_sum(cot_f)

    @pl.when(step == pl.num_programs(0) - 1)
    def _():
        items, rows, dim = branch_ref.shape
        gb = branch_ref[...].reshape(items * rows, dim)
        width = mixed_a.shape[2]
        quarter = width // 2
        for n, mixed in ((0, mixed_a), (1, mixed_b)):
            dw = mul_tn(mixed[...].reshape(items * rows, width), gb).astype(bf)
            dw_out[2 * n] = dw[:quarter]
            dw_out[2 * n + 1] = dw[quarter:]


def unbranch(middle, cot, grad_in, gain, mixed_a, mixed_b, w_a, w_b):
    items, rows, dim = middle.shape
    width = mixed_a.shape[2]
    each = per_item((rows, dim))
    return pl.pallas_call(
        unbranch_kernel,
        grid=(items,),
        in_specs=[each, each, each, full((1, dim))]
        + [full(mixed_a.shape)] * 2
        + [full(w_a.shape)] * 2,
        out_specs=[
            each,
            per_item((rows, width)),
            per_item((rows, width)),
            full((4, width // 2, dim)),
            full((8, dim)),
        ],
        out_shape=[
            jax.ShapeDtypeStruct((items, rows, dim), f32),
            jax.ShapeDtypeStruct((items, rows, width), bf),
            jax.ShapeDtypeStruct((items, rows, width), bf),
            jax.ShapeDtypeStruct((4, width // 2, dim), bf),
            jax.ShapeDtypeStruct((8, dim), f32),
        ],
        scratch_shapes=[pltpu.VMEM((items, rows, dim), bf)],
        compiler_params=params(32),
        cost_estimate=lasting(TIMES["unbranch"]),
        name="unbranch",
    )(middle, cot, grad_in, gain, mixed_a, mixed_b, w_a, w_b)


def unattend_kernel(final, counts, q, k, v, gmix, logs, w, *refs):
    if final:
        grad_in, grad_middle, tokens, gain, x_out, g_ref, db_out, small = refs
    else:
        x_out, g_ref, db_out = refs
    step = pl.program_id(0)
    rows, width = q.shape
    valid = WORDS + counts[step]
    mask = jnp.where(lax.broadcasted_iota(jnp.int32, (rows, 1), 0) < valid, 0.0, masked_value)
    low = lax.broadcasted_iota(jnp.int32, (rows, LANES), 1) < HEAD
    for p in range(width // LANES):
        at = slice(p * LANES, (p + 1) * LANES)
        q_two, k_two, v_two, g_two = q[:, at], k[:, at], v[:, at], gmix[:, at]
        dq, dk, dv = [], [], []
        for h in range(2):
            here = low if h == 0 else ~low
            scores = mul_nt(jnp.where(here, k_two, 0), q_two) + mask
            prob = jnp.exp(scores - logs[2 * p + h : 2 * p + h + 1])
            grad_prob = mul_nt(jnp.where(here, v_two, 0), g_two)
            inner = jnp.sum(grad_prob * prob, axis=0, keepdims=True)
            grad_scores = (prob * (grad_prob - inner)).astype(bf)
            dv.append(mul_nn(prob.astype(bf), g_two))
            dk.append(mul_nn(grad_scores, q_two))
            dq.append(mul_tn(grad_scores, k_two))
        for c, pair in enumerate((dq, dk, dv)):
            merged = jnp.where(low, pair[0], pair[1]).astype(bf)
            if c == 0:
                merged = merged * jnp.asarray(0.125, bf)
            g_ref[:, c * width + p * LANES : c * width + (p + 1) * LANES] = merged
    g = g_ref[...]
    grad = mul_nn(g, w[...].reshape(3 * width, -1))

    @pl.when(step == 0)
    def _():
        db_out[...] = jnp.zeros_like(db_out)
        if final:
            small[...] = jnp.zeros_like(small)

    sums = col_sum(g.astype(f32))
    db_out[0:1] += sums[:, :width]
    db_out[1:2] += sums[:, 2 * width :]
    if final:
        grad = grad + grad_in[...]
        unit, inv = unit_parts(pad_rows(tokens[...].astype(f32), rows))
        small[0:1] += col_sum(grad * unit)
        small[1:2] += col_sum(grad)
        seq = x_out.shape[0]
        x_out[...] = (grad_middle[...] + norm_back(grad, unit, inv, gain[...]))[:seq]
    else:
        x_out[...] = grad


def unattend(counts, q, k, v, gmix, logs, w, rest=None):
    final = rest is not None
    items, rows, width = q.shape
    dim = w.shape[2]
    wide = per_item((rows, width))
    specs = [wide] * 4 + [per_item((8, rows)), full(w.shape)]
    args = [counts, q, k, v, gmix, logs, w]
    out_rows = rows
    extra_out, extra_spec = [], []
    if final:
        grad_in, grad_middle, tokens, gain = rest
        out_rows = tokens.shape[1]
        specs += [per_item((rows, dim))] * 2 + [per_item(tokens.shape[1:]), full((1, dim))]
        args += list(rest)
        extra_out, extra_spec = [jax.ShapeDtypeStruct((8, dim), f32)], [full((8, dim))]
    return pl.pallas_call(
        functools.partial(unattend_kernel, final),
        grid_spec=pltpu.PrefetchScalarGridSpec(
            num_scalar_prefetch=1,
            grid=(items,),
            in_specs=specs,
            out_specs=[
                per_item((out_rows, dim)),
                per_item((rows, 3 * width)),
                full((8, width)),
            ]
            + extra_spec,
        ),
        out_shape=[
            jax.ShapeDtypeStruct((items, out_rows, dim), f32),
            jax.ShapeDtypeStruct((items, rows, 3 * width), bf),
            jax.ShapeDtypeStruct((8, width), f32),
        ]
        + extra_out,
        compiler_params=params(40),
        cost_estimate=lasting(TIMES["unattend"]),
        name="unattend",
    )(*args)


def outer_kernel(g, normed, dw_out):
    items, rows, dim = normed.shape
    dw = mul_tn(g[...].reshape(items * rows, -1), normed[...].reshape(items * rows, dim)).astype(bf)
    quarter = dw.shape[0] // 2
    dw_out[0] = dw[:quarter]
    dw_out[1] = dw[quarter:]


def outer(g, normed):
    items, rows, width3 = g.shape
    dim = normed.shape[2]
    width = width3 // 3
    return pl.pallas_call(
        outer_kernel,
        grid=(3,),
        in_specs=[pl.BlockSpec((items, rows, width), lambda c: (0, 0, c)), full(normed.shape)],
        out_specs=pl.BlockSpec((2, None, width // 2, dim), lambda c: (0, c, 0, 0)),
        out_shape=jax.ShapeDtypeStruct((2, 3, width // 2, dim), bf),
        compiler_params=params(24),
        cost_estimate=lasting(TIMES["outer"]),
        name="outer",
    )(g, normed)


def exchange(x, axis, size, mask):
    return lax.ppermute(x, axis, [(i, i ^ mask) for i in range(size)])


def tie(*values):
    return lax.optimization_barrier(values)


def add_bf(*parts):
    total = parts[0].astype(f32)
    for part in parts[1:]:
        total = total + part.astype(f32)
    return total.astype(bf)


def piece(x, index, count):
    rows = x.shape[0] // count
    return lax.dynamic_slice_in_dim(x, index * rows, rows, 0)


class Wide:
    def __init__(self, size):
        self.size = size
        self.me = lax.axis_index("wide")
        self.groups = []
        bit = 1
        if size > 1:
            self.groups.append((1, 2))
            bit = 2
        while bit < size:
            members = min(4, size // bit)
            self.groups.append((bit, members))
            bit *= members

    def at(self, group):
        bit, members = group
        return (self.me // bit) % members

    def send(self, group, x):
        bit, members = group
        mine = self.at(group)
        got = [
            exchange(piece(x, mine ^ k, members), "wide", self.size, bit * k)
            for k in range(1, members)
        ]
        return piece(x, mine, members), got

    def gather(self, group, x):
        bit, members = group
        mine = self.at(group)
        got = [exchange(x, "wide", self.size, bit * k) for k in range(1, members)]
        if members == 2:
            first = jnp.where(mine == 0, x, got[0])
            second = jnp.where(mine == 0, got[0], x)
            return jnp.concatenate([first, second], axis=0)
        rows = x.shape[0]
        out = jnp.zeros((members * rows,) + x.shape[1:], x.dtype)
        for k, part in enumerate([x] + got):
            out = lax.dynamic_update_slice_in_dim(out, part, (mine ^ k) * rows, 0)
        return out


def on_device(
    wide,
    narrow,
    tokens,
    patch_counts,
    ln1_gain,
    ln1_bias,
    w_qkv,
    b_qv,
    w_out,
    b_out,
    ln2_gain,
    ln2_bias,
    w_up,
    b_up,
    w_down,
    b_down,
    cotangent,
):
    own_rows, dim = tokens.shape
    items = patch_counts.shape[0] // narrow
    seq = own_rows // items
    rows = -(-seq // PACK) * PACK
    heads = w_qkv.shape[2]
    units = w_up.shape[1]
    me = lax.axis_index("narrow")
    counts = lax.dynamic_slice_in_dim(patch_counts, me * items, items, 0)
    tokens3 = tokens.reshape(items, seq, dim)
    cot3 = cotangent.reshape(items, seq, dim)
    row = lambda x: x.reshape(1, dim)
    mate = lambda x: exchange(x, "narrow", narrow, 1)
    peer = lambda x: exchange(x, "narrow", narrow, 2)

    ring = Wide(wide)
    x_axis, tail_axes = ring.groups[0], ring.groups[1:]
    across = lambda x: exchange(x, "wide", wide, 1)
    low_half = (ring.me % 2).astype(jnp.int32)
    half_dim = dim // 2

    def my_half(x, axis):
        return lax.dynamic_slice_in_dim(x, low_half * half_dim, half_dim, axis)

    w_flat = w_qkv.transpose(1, 2, 0)
    parts, rest = [], b_qv
    for _ in range(3):
        parts.append(lax.reduce_precision(rest, 8, 7))
        rest = rest - parts[-1]
    vectors = jnp.pad(jnp.concatenate(parts, axis=0).astype(bf), ((0, 0), (0, dim - heads)))
    vectors = jnp.concatenate([vectors, b_up, jnp.zeros((1, dim), bf)], axis=0)
    out_own = jnp.concatenate([w_out, vectors], axis=0)

    def biases(block):
        three = block[heads : heads + 6, :heads].astype(f32)
        return three[0:2] + three[2:4] + three[4:6], block[heads + 6 : heads + 7, :units].astype(f32)

    def halves(one, two):
        b_one, u_one = biases(one)
        b_two, u_two = biases(two)
        return (
            jnp.concatenate([one[:heads], two[:heads]], axis=0),
            jnp.concatenate([b_one, b_two], axis=1),
            jnp.concatenate([u_one, u_two], axis=1),
        )

    w_first = peer(my_half(w_flat, 2))
    w_mate, out_mate = mate(w_flat), mate(out_own)
    out_peer = peer(out_own)
    up_mate, down_mate = mate(w_up), mate(w_down)
    up_part, down_part = my_half(w_up, 0), my_half(w_down, 1)
    gain1, bias1 = row(ln1_gain), row(ln1_bias)
    w_a = jnp.concatenate([w_flat, w_mate], axis=1)
    out_a, b_a, ub_a = halves(out_own, out_mate)
    q_a, k_a, v_a, mixed_a, log_a, normed1 = attend(
        True, counts, tokens3, gain1, bias1, w_a, b_a, rows
    )

    log_a, w_first, out_peer, up_part = tie(log_a, w_first, out_peer, up_part)
    w_second, up_first = across(w_first), peer(up_part)
    out_far = mate(out_peer)
    w_first, w_second, up_first, down_part = tie(w_first, w_second, up_first, down_part)
    up_second, down_first = across(up_first), peer(down_part)
    w_peer = jnp.where(
        low_half == 0,
        jnp.concatenate([w_first, w_second], axis=2),
        jnp.concatenate([w_second, w_first], axis=2),
    )
    w_b = jnp.concatenate([w_peer, mate(w_peer)], axis=1)
    out_b, b_b, ub_b = halves(out_peer, out_far)
    q_b, k_b, v_b, mixed_b, log_b = attend(False, counts, tokens3, gain1, bias1, w_b, b_b, rows)

    middle, normed2, cot_pad = branch(
        tokens3, cot3, mixed_a, mixed_b, out_a, out_b, row(b_out), row(ln2_gain), row(ln2_bias)
    )
    normed2, up_first, up_second, down_first = tie(normed2, up_first, up_second, down_first)
    down_second = across(down_first)
    ups = [up_first, up_second, mate(up_first), mate(up_second)]
    flag = low_half.reshape(1)
    part, grad_part, dup_a, ddown_a, dbias_a = feed(
        False, flag, normed2, cot_pad, middle, None, row(b_down), [w_up, up_mate], [w_down, down_mate], ub_a, seq
    )
    part, down_first, down_second = tie(part, down_first, down_second)
    downs = [down_first, down_second, mate(down_first), mate(down_second)]
    got_up, got_down = mate(dup_a[1]), mate(ddown_a[1])
    layer_out, grad_norm2, dup_b, ddown_b, dbias_b = feed(
        True, flag, normed2, cot_pad, part, grad_part, row(b_down), ups, downs, ub_b, seq
    )

    grad_norm2, got_up, got_down = tie(grad_norm2, got_up, got_down)
    far_up, far_down = mate(dup_b[1]), mate(ddown_b[1])
    up_own = add_bf(dup_a[0], got_up)
    down_keep, down_got = ring.send(x_axis, add_bf(ddown_a[0], got_down))
    grad_middle, gmix_a, gmix_b, dw_out, small_two = unbranch(
        middle, cot_pad, grad_norm2, row(ln2_gain), mixed_a, mixed_b, out_a, out_b
    )
    gmix_b, far_up, far_down = tie(gmix_b, far_up, far_down)
    up_got = peer(add_bf(dup_b[0], far_up))
    pair_keep, pair_got = ring.send(x_axis, add_bf(ddown_b[0], far_down))
    grad_one, g_b, dbqv_b = unattend(counts, q_b, k_b, v_b, gmix_b, log_b, w_b)
    g_b, pair_got, down_got = tie(g_b, pair_got[0], down_got[0])
    pair_half = peer(add_bf(pair_keep, pair_got))
    down_half = add_bf(down_keep, down_got)
    dqkv_b = outer(g_b, normed1)

    later = [jnp.zeros((2, dim), f32)] + [small_two[n : n + 1] for n in range(4)]

    def block(n, dqkv, dbqv, dbias):
        at = n % 2
        tail = later + [
            dbias[:, at * units : (at + 1) * units],
            jnp.pad(dbqv[0:2, at * heads : (at + 1) * heads], ((0, 0), (0, dim - heads))),
        ]
        tail = jnp.concatenate(tail, axis=0)
        pad = -(4 * heads + tail.shape[0]) % (8 * wide)
        tail = jnp.pad(tail, ((0, pad), (0, 0))).astype(bf)
        return jnp.concatenate([dqkv[at].reshape(3 * heads, dim), dw_out[n], tail], axis=0)

    far_rest = mate(block(3, dqkv_b, dbqv_b, dbias_b))
    gmix_a, far_rest = tie(gmix_a, far_rest)
    rest_keep, rest_got = ring.send(x_axis, add_bf(block(2, dqkv_b, dbqv_b, dbias_b), far_rest))
    input_grad, g_a, dbqv_a, small_one = unattend(
        counts, q_a, k_a, v_a, gmix_a, log_a, w_a, (grad_one, grad_middle, tokens3, gain1)
    )
    g_a, up_got, pair_half, rest_got = tie(g_a, up_got, pair_half, rest_got[0])
    rest_half = peer(add_bf(rest_keep, rest_got))
    dqkv_a = outer(g_a, normed1)
    dqkv_a, firsts = tie(dqkv_a, small_one[0:2])
    firsts = firsts + mate(firsts)
    firsts = firsts + peer(firsts)
    rest_mate = mate(block(1, dqkv_a, dbqv_a, dbias_a))

    def over(groups, x):
        for group in groups:
            kept, got = ring.send(group, x)
            x = add_bf(kept, *got)
        return x

    def back(groups, x):
        for group in reversed(groups):
            x = ring.gather(group, x)
        return x

    down_sum = back(ring.groups, over(tail_axes, add_bf(down_half, pair_half)))
    up_sum = back(ring.groups, over(ring.groups, add_bf(up_own, up_got)))
    rest_own = add_bf(block(0, dqkv_a, dbqv_a, dbias_a), rest_mate)
    rest_own = lax.dynamic_update_slice_in_dim(rest_own, firsts.astype(bf), 4 * heads, 0)
    rest_sum = back(ring.groups, over(tail_axes, add_bf(over([x_axis], rest_own), rest_half)))
    vec = rest_sum[4 * heads :].astype(f32)
    return (
        layer_out.reshape(own_rows, dim),
        input_grad.reshape(own_rows, dim),
        vec[0],
        vec[1],
        rest_sum[: 3 * heads].astype(f32).reshape(3, heads, dim).transpose(2, 0, 1),
        vec[7:9, :heads],
        rest_sum[3 * heads : 4 * heads].astype(f32),
        vec[4],
        vec[2],
        vec[3],
        up_sum.astype(f32),
        vec[6:7, :units],
        down_sum.astype(f32),
        vec[5],
    )


def solution(mesh):
    wide, narrow = mesh.shape["wide"], mesh.shape["narrow"]
    assert narrow == 4 and wide & (wide - 1) == 0
    rows = P(("wide", "narrow"), None)
    return jax.shard_map(
        functools.partial(on_device, wide, narrow),
        mesh=mesh,
        in_specs=(
            rows,
            P("wide"),
            P(),
            P(),
            P(None, None, "narrow"),
            P(None, "narrow"),
            P("narrow", None),
            P(),
            P(),
            P(),
            P(None, "narrow"),
            P(None, "narrow"),
            P("narrow", None),
            P(),
            rows,
        ),
        out_specs=(
            rows,
            rows,
            P(),
            P(),
            P(None, None, "narrow"),
            P(None, "narrow"),
            P("narrow", None),
            P(),
            P(),
            P(),
            P(None, "narrow"),
            P(None, "narrow"),
            P("narrow", None),
            P(),
        ),
        check_vma=False,
    )
```

```python
import functools

import jax
import jax.numpy as jnp
from jax import lax
from jax.experimental import pallas as pl
from jax.experimental.pallas import tpu as pltpu
from jax.sharding import PartitionSpec as P

HEAD = 64
WORDS = 40
PACK = 16
LANES = 128
BLOCK = 256

norm_eps = 1e-06
masked_value = -1000000000.0
bf = jnp.bfloat16
f32 = jnp.float32


def mul_nn(a, b):
    return lax.dot_general(a, b, (((1,), (0,)), ((), ())), preferred_element_type=f32)


def mul_nt(a, b):
    return lax.dot_general(a, b, (((1,), (1,)), ((), ())), preferred_element_type=f32)


def mul_tn(a, b):
    return lax.dot_general(a, b, (((0,), (0,)), ((), ())), preferred_element_type=f32)


def pad_rows(x, rows):
    if x.shape[0] == rows:
        return x
    return jnp.concatenate([x, jnp.zeros((rows - x.shape[0],) + x.shape[1:], x.dtype)], axis=0)


def unit_parts(x):
    centred = x - jnp.mean(x, axis=-1, keepdims=True)
    inv = lax.rsqrt(jnp.mean(centred * centred, axis=-1, keepdims=True) + norm_eps)
    return centred * inv, inv


def norm_back(grad, unit, inv, gain):
    scaled = grad * gain
    inner = (
        scaled
        - jnp.mean(scaled, axis=-1, keepdims=True)
        - unit * jnp.mean(scaled * unit, axis=-1, keepdims=True)
    )
    return inv * inner


def col_sum(x):
    return jnp.sum(x, axis=0, keepdims=True)


def full(shape):
    return pl.BlockSpec(shape, lambda *_: (0,) * len(shape))


def per_item(shape):
    return pl.BlockSpec((None,) + shape, lambda i, *_: (i,) + (0,) * len(shape))


TIMES = {
    "attend": 10,
    "branch": 3,
    "feed": 18,
    "project": 6,
    "unbranch": 6,
    "unattend": 11,
    "unnorm": 6,
}


def lasting(us):
    return pl.CostEstimate(flops=int(us * 1.15e9), bytes_accessed=0, transcendentals=0)


def params(mib):
    return pltpu.CompilerParams(vmem_limit_bytes=mib << 20)


def two_rows(w_one, w_two, c):
    return jnp.concatenate([w_one[c], w_two[c]], axis=0)


def attend_kernel(first, counts, tokens, small, w_one, w_two, b_one, b_two, *outs):
    if first:
        q_out, k_out, v_out, mixed_out, log_out, normed_out = outs
    else:
        q_out, k_out, v_out, mixed_out, log_out = outs
    rows, width = q_out.shape
    unit, _ = unit_parts(pad_rows(tokens[...].astype(f32), rows))
    normed = (unit * small[0:1] + small[1:2]).astype(bf)
    b = jnp.concatenate([b_one[...], b_two[...]], axis=1)
    if first:
        normed_out[...] = normed
    q = ((mul_nt(normed, two_rows(w_one, w_two, 0)) + b[0:1]) * 0.125).astype(bf)
    k = mul_nt(normed, two_rows(w_one, w_two, 1)).astype(bf)
    v = (mul_nt(normed, two_rows(w_one, w_two, 2)) + b[1:2]).astype(bf)
    q_out[...] = q
    k_out[...] = k
    v_out[...] = v
    valid = WORDS + counts[pl.program_id(0)]
    mask = jnp.where(lax.broadcasted_iota(jnp.int32, (1, rows), 1) < valid, 0.0, masked_value)
    lane = lax.broadcasted_iota(jnp.int32, (rows, LANES), 1)
    low = lane < HEAD
    logs = jnp.zeros((rows, LANES), f32)
    for p in range(width // LANES):
        at = slice(p * LANES, (p + 1) * LANES)
        q_two, k_two, v_two = q[:, at], k[:, at], v[:, at]
        tops, sums = [], []
        for h in range(2):
            here = low if h == 0 else ~low
            scores = mul_nt(jnp.where(here, q_two, 0), k_two) + mask
            top = jnp.max(scores, axis=1, keepdims=True)
            shifted = jnp.exp(scores - top).astype(bf)
            sums.append(mul_nn(shifted, jnp.where(here, v_two, 1)))
            tops.append(top)
        total = pltpu.roll(jnp.where(low, sums[1], sums[0]), HEAD, 1)
        mixed_out[:, at] = (jnp.where(low, sums[0], sums[1]) / total).astype(bf)
        log_two = jnp.log(total)
        logs = jnp.where(lane == 2 * p, tops[0] + log_two[:, 0:1], logs)
        logs = jnp.where(lane == 2 * p + 1, tops[1] + log_two[:, HEAD : HEAD + 1], logs)
    log_out[...] = logs.T[: log_out.shape[0]]


def attend(first, counts, tokens, small, ws, bs, rows):
    items, _, dim = tokens.shape
    width = 2 * ws[0].shape[1]
    wide_out = jax.ShapeDtypeStruct((items, rows, width), bf)
    outs = [wide_out] * 4 + [jax.ShapeDtypeStruct((items, 8, rows), f32)]
    specs = [per_item((rows, width))] * 4 + [per_item((8, rows))]
    if first:
        outs.append(jax.ShapeDtypeStruct((items, rows, dim), bf))
        specs.append(per_item((rows, dim)))
    return pl.pallas_call(
        functools.partial(attend_kernel, first),
        grid_spec=pltpu.PrefetchScalarGridSpec(
            num_scalar_prefetch=1,
            grid=(items,),
            in_specs=[
                per_item(tokens.shape[1:]),
                full(small.shape),
                full(ws[0].shape),
                full(ws[0].shape),
                full(bs[0].shape),
                full(bs[0].shape),
            ],
            out_specs=specs,
        ),
        out_shape=outs,
        compiler_params=params(8),
        cost_estimate=lasting(TIMES["attend"]),
        name="attend",
    )(counts, tokens, small, *ws, *bs)


def branch_kernel(tokens, cot, mixed_a, mixed_b, w_a, w_b, small, middle_out, normed_out, cot_out):
    rows = normed_out.shape[0]
    middle = (
        pad_rows(tokens[...].astype(f32), rows)
        + (mul_nn(mixed_a[...], w_a[...]) + mul_nn(mixed_b[...], w_b[...]))
        + small[2:3]
    )
    middle_out[...] = middle
    unit, _ = unit_parts(middle)
    normed_out[...] = (unit * small[3:4] + small[4:5]).astype(bf)
    cot_out[...] = pad_rows(cot[...].astype(f32), rows).astype(bf)


def branch(tokens, cot, mixed_a, mixed_b, w_a, w_b, small):
    items, seq, dim = tokens.shape
    _, rows, width = mixed_a.shape
    return pl.pallas_call(
        branch_kernel,
        grid=(items,),
        in_specs=[per_item((seq, dim))] * 2
        + [per_item((rows, width))] * 2
        + [full(w_a.shape)] * 2
        + [full(small.shape)],
        out_specs=[per_item((rows, dim))] * 3,
        out_shape=[
            jax.ShapeDtypeStruct((items, rows, dim), f32),
            jax.ShapeDtypeStruct((items, rows, dim), bf),
            jax.ShapeDtypeStruct((items, rows, dim), bf),
        ],
        compiler_params=params(7),
        cost_estimate=lasting(TIMES["branch"]),
        name="branch",
    )(tokens, cot, mixed_a, mixed_b, w_a, w_b, small)


def feed_kernel(
    again, per, low_half, normed, cot, base_grad, *refs
):
    n_weights = 6 if again else 4
    weights, rest = refs[:n_weights], refs[n_weights:]
    bias_a, bias_b, grad_ref, hidden_ref, dup_a, dup_b, ddown_a, ddown_b, dbias_ref, gu_ref = rest
    step = pl.program_id(0)
    items, rows, dim = normed.shape
    is_a = step < per

    @pl.when(step == 0)
    def _():
        grad_ref[...] = base_grad[...] if again else jnp.zeros_like(grad_ref)

    if again:
        up_a, up_b, up_c, up_d, down_a, down_c = weights
        is_low = low_half[0] == 0
        first = jnp.where(is_a, up_a[...], up_c[...])
        second = jnp.where(is_a, up_b[...], up_d[...])
        w_up = jnp.concatenate(
            [jnp.where(is_low, first, second), jnp.where(is_low, second, first)], axis=0
        )
    else:
        up_a, up_c, down_a, down_c = weights
        w_up = jnp.where(is_a, up_a[...], up_c[...])
    w_down = jnp.where(is_a, down_a[...], down_c[...])
    bias = jnp.where(is_a, bias_a[...].astype(f32), bias_b[...].astype(f32))
    bias_sum = jnp.zeros((1, w_up.shape[1]), f32)
    for i in range(items):
        up = mul_nn(normed[i], w_up) + bias
        grad_hidden = mul_nt(cot[i], w_down)
        cdf = 0.5 * (1.0 + lax.erf(up * 0.7071067811865476))
        slope = cdf + up * (jnp.exp(-0.5 * up * up) * 0.3989422804014327)
        gu = (slope * grad_hidden).astype(bf)
        hidden_ref[i] = (up * cdf).astype(bf)
        gu_ref[i] = gu
        bias_sum = bias_sum + col_sum(gu.astype(f32))
        grad_ref[i] += mul_nt(gu, w_up)
    dbias_ref[...] = bias_sum
    flat = (items * rows, dim)
    hidden = hidden_ref[...].reshape(items * rows, -1)
    gu = gu_ref[...].reshape(items * rows, -1)
    ddown = mul_tn(hidden, cot[...].reshape(flat)).astype(bf)
    dup = mul_tn(normed[...].reshape(flat), gu).astype(bf)

    @pl.when(is_a)
    def _():
        ddown_a[...] = ddown
        dup_a[...] = dup

    @pl.when(jnp.logical_not(is_a))
    def _():
        ddown_b[...] = ddown
        dup_b[...] = dup


def feed(low_half, normed, cot, base_grad, ups, downs, biases):
    again = base_grad is not None
    items, rows, dim = normed.shape
    units = ups[0].shape[1]
    per = units // BLOCK
    steps = 2 * per
    full3 = full((items, rows, dim))
    if not again:
        base_grad = biases[0]
    half = len(ups) // 2
    first = lambda j: jnp.minimum(j, per - 1)
    second = lambda j: jnp.maximum(j - per, 0)
    across = lambda part, place: pl.BlockSpec((part, BLOCK), lambda j, *_: (0, place(j)))
    down = lambda place: pl.BlockSpec((BLOCK, dim), lambda j, *_: (place(j), 0))
    return pl.pallas_call(
        functools.partial(feed_kernel, again, per),
        grid_spec=pltpu.PrefetchScalarGridSpec(
            num_scalar_prefetch=1,
            grid=(steps,),
            in_specs=[full3, full3, full3 if again else full(base_grad.shape)]
            + [across(dim // half, first)] * half
            + [across(dim // half, second)] * half
            + [down(first), down(second)]
            + [across(1, first), across(1, second)],
            out_specs=[
                full3,
                pl.BlockSpec((items, rows, BLOCK), lambda j, *_: (0, 0, j)),
                across(dim, first),
                across(dim, second),
                down(first),
                down(second),
                pl.BlockSpec((1, BLOCK), lambda j, *_: (0, j)),
            ],
            scratch_shapes=[pltpu.VMEM((items, rows, BLOCK), bf)],
        ),
        out_shape=[
            jax.ShapeDtypeStruct((items, rows, dim), f32),
            jax.ShapeDtypeStruct((items, rows, 2 * units), bf),
            jax.ShapeDtypeStruct((dim, units), bf),
            jax.ShapeDtypeStruct((dim, units), bf),
            jax.ShapeDtypeStruct((units, dim), bf),
            jax.ShapeDtypeStruct((units, dim), bf),
            jax.ShapeDtypeStruct((1, 2 * units), f32),
        ],
        compiler_params=params(14),
        cost_estimate=lasting(TIMES["feed"]),
        name="feed",
    )(low_half, normed, cot, base_grad, *ups, *downs, *biases)


def project_kernel(middle, small, hidden_a, hidden_b, *refs):
    weights, out_ref = refs[:4], refs[4]
    units = weights[0].shape[0]
    total = middle[...] + small[5:6]
    for n, w in enumerate(weights):
        hidden = (hidden_a, hidden_b)[n // 2]
        total = total + mul_nn(hidden[:, (n % 2) * units : (n % 2 + 1) * units], w[...])
    out_ref[...] = total[: out_ref.shape[0]]


def project(middle, small, hidden_a, hidden_b, weights, seq):
    items, rows, dim = middle.shape
    both = per_item(hidden_a.shape[1:])
    return pl.pallas_call(
        project_kernel,
        grid=(items,),
        in_specs=[per_item((rows, dim)), full(small.shape), both, both] + [full(weights[0].shape)] * 4,
        out_specs=per_item((seq, dim)),
        out_shape=jax.ShapeDtypeStruct((items, seq, dim), f32),
        compiler_params=params(14),
        cost_estimate=lasting(TIMES["project"]),
        name="project",
    )(middle, small, hidden_a, hidden_b, *weights)


def unbranch_kernel(
    middle, cot, grad_in, vectors, mixed_a, mixed_b, w_a, w_b,
    grad_out, gmix_a, gmix_b, dw_out, small, branch_ref
):
    step = pl.program_id(0)
    unit, inv = unit_parts(middle[...])
    grad = grad_in[...]
    cot_f = cot[...].astype(f32)
    grad_middle = cot_f + norm_back(grad, unit, inv, vectors[3:4])
    grad_out[...] = grad_middle
    grad_branch = grad_middle.astype(bf)
    branch_ref[step] = grad_branch
    gmix_a[...] = mul_nt(grad_branch, w_a[...]).astype(bf)
    gmix_b[...] = mul_nt(grad_branch, w_b[...]).astype(bf)

    @pl.when(step == 0)
    def _():
        small[...] = jnp.zeros_like(small)

    small[0:1] += col_sum(grad * unit)
    small[1:2] += col_sum(grad)
    small[2:3] += col_sum(grad_branch.astype(f32))
    small[3:4] += col_sum(cot_f)

    @pl.when(step == pl.num_programs(0) - 1)
    def _():
        items, rows, dim = branch_ref.shape
        gb = branch_ref[...].reshape(items * rows, dim)
        width = mixed_a.shape[2]
        quarter = width // 2
        for n, mixed in ((0, mixed_a), (1, mixed_b)):
            dw = mul_tn(mixed[...].reshape(items * rows, width), gb).astype(bf)
            dw_out[2 * n] = dw[:quarter]
            dw_out[2 * n + 1] = dw[quarter:]


def unbranch(middle, cot, grad_in, vectors, mixed_a, mixed_b, w_a, w_b):
    items, rows, dim = middle.shape
    width = mixed_a.shape[2]
    each = per_item((rows, dim))
    return pl.pallas_call(
        unbranch_kernel,
        grid=(items,),
        in_specs=[each, each, each, full(vectors.shape)]
        + [full(mixed_a.shape)] * 2
        + [full(w_a.shape)] * 2,
        out_specs=[
            each,
            per_item((rows, width)),
            per_item((rows, width)),
            full((4, width // 2, dim)),
            full((8, dim)),
        ],
        out_shape=[
            jax.ShapeDtypeStruct((items, rows, dim), f32),
            jax.ShapeDtypeStruct((items, rows, width), bf),
            jax.ShapeDtypeStruct((items, rows, width), bf),
            jax.ShapeDtypeStruct((4, width // 2, dim), bf),
            jax.ShapeDtypeStruct((8, dim), f32),
        ],
        scratch_shapes=[pltpu.VMEM((items, rows, dim), bf)],
        compiler_params=params(12),
        cost_estimate=lasting(TIMES["unbranch"]),
        name="unbranch",
    )(middle, cot, grad_in, vectors, mixed_a, mixed_b, w_a, w_b)


def unattend_kernel(counts, q, k, v, gmix, logs, normed, g_ref, dw_out, db_out):
    step = pl.program_id(0)
    rows, width = q.shape
    valid = WORDS + counts[step]
    mask = jnp.where(lax.broadcasted_iota(jnp.int32, (rows, 1), 0) < valid, 0.0, masked_value)
    low = lax.broadcasted_iota(jnp.int32, (rows, LANES), 1) < HEAD
    for p in range(width // LANES):
        at = slice(p * LANES, (p + 1) * LANES)
        q_two, k_two, v_two, g_two = q[:, at], k[:, at], v[:, at], gmix[:, at]
        dq, dk, dv = [], [], []
        for h in range(2):
            here = low if h == 0 else ~low
            scores = mul_nt(jnp.where(here, k_two, 0), q_two) + mask
            prob = jnp.exp(scores - logs[2 * p + h : 2 * p + h + 1])
            grad_prob = mul_nt(jnp.where(here, v_two, 0), g_two)
            inner = jnp.sum(grad_prob * prob, axis=0, keepdims=True)
            grad_scores = (prob * (grad_prob - inner)).astype(bf)
            dv.append(mul_nn(prob.astype(bf), g_two))
            dk.append(mul_nn(grad_scores, q_two))
            dq.append(mul_tn(grad_scores, k_two))
        for c, pair in enumerate((dq, dk, dv)):
            merged = jnp.where(low, pair[0], pair[1]).astype(bf)
            if c == 0:
                merged = merged * jnp.asarray(0.125, bf)
            g_ref[step, :, c * width + p * LANES : c * width + (p + 1) * LANES] = merged

    @pl.when(step == 0)
    def _():
        db_out[...] = jnp.zeros_like(db_out)

    db_out[0:1] += col_sum(g_ref[step, :, :width].astype(f32))
    db_out[1:2] += col_sum(g_ref[step, :, 2 * width :].astype(f32))

    @pl.when(step == pl.num_programs(0) - 1)
    def _():
        items, _, dim = normed.shape
        flat = normed[...].reshape(items * rows, dim)
        quarter = width // 2
        for c in range(3):
            g = g_ref[:, :, c * width : (c + 1) * width].reshape(items * rows, width)
            dw = mul_tn(g, flat).astype(bf)
            dw_out[0, c] = dw[:quarter]
            dw_out[1, c] = dw[quarter:]


def unattend(counts, q, k, v, gmix, logs, normed):
    items, rows, width = q.shape
    dim = normed.shape[2]
    return pl.pallas_call(
        unattend_kernel,
        grid_spec=pltpu.PrefetchScalarGridSpec(
            num_scalar_prefetch=1,
            grid=(items,),
            in_specs=[per_item((rows, width))] * 4 + [per_item((8, rows)), full(normed.shape)],
            out_specs=[
                full((items, rows, 3 * width)),
                full((2, 3, width // 2, dim)),
                full((8, width)),
            ],
        ),
        out_shape=[
            jax.ShapeDtypeStruct((items, rows, 3 * width), bf),
            jax.ShapeDtypeStruct((2, 3, width // 2, dim), bf),
            jax.ShapeDtypeStruct((8, width), f32),
        ],
        compiler_params=params(12),
        cost_estimate=lasting(TIMES["unattend"]),
        name="unattend",
    )(counts, q, k, v, gmix, logs, normed)


def unnorm_kernel(g_a, g_b, w_one, w_two, w_three, w_four, tokens, vectors, grad_middle, x_out, small):
    rows = g_a.shape[0]
    grad = 0.0
    for g, one, two in ((g_a, w_one, w_two), (g_b, w_three, w_four)):
        w = jnp.concatenate([two_rows(one, two, c) for c in range(3)], axis=0)
        grad = grad + mul_nn(g[...], w)
    unit, inv = unit_parts(pad_rows(tokens[...].astype(f32), rows))

    @pl.when(pl.program_id(0) == 0)
    def _():
        small[...] = jnp.zeros_like(small)

    small[0:1] += col_sum(grad * unit)
    small[1:2] += col_sum(grad)
    x_out[...] = (grad_middle[...] + norm_back(grad, unit, inv, vectors[0:1]))[: x_out.shape[0]]


def unnorm(g_a, g_b, ws, tokens, vectors, grad_middle):
    items, rows, width3 = g_a.shape
    seq, dim = tokens.shape[1:]
    return pl.pallas_call(
        unnorm_kernel,
        grid=(items,),
        in_specs=[per_item((rows, width3))] * 2
        + [full(ws[0].shape)] * 4
        + [per_item((seq, dim)), full(vectors.shape), per_item((rows, dim))],
        out_specs=[per_item((seq, dim)), full((8, dim))],
        out_shape=[
            jax.ShapeDtypeStruct((items, seq, dim), f32),
            jax.ShapeDtypeStruct((8, dim), f32),
        ],
        compiler_params=params(12),
        cost_estimate=lasting(TIMES["unnorm"]),
        name="unnorm",
    )(g_a, g_b, *ws, tokens, vectors, grad_middle)


def outer_kernel(g, normed, dw_out):
    items, rows, dim = normed.shape
    dw = mul_tn(g[...].reshape(items * rows, -1), normed[...].reshape(items * rows, dim)).astype(bf)
    quarter = dw.shape[0] // 2
    dw_out[0] = dw[:quarter]
    dw_out[1] = dw[quarter:]


def outer(g, normed):
    items, rows, width3 = g.shape
    dim = normed.shape[2]
    width = width3 // 3
    return pl.pallas_call(
        outer_kernel,
        grid=(3,),
        in_specs=[pl.BlockSpec((items, rows, width), lambda c: (0, 0, c)), full(normed.shape)],
        out_specs=pl.BlockSpec((2, None, width // 2, dim), lambda c: (0, c, 0, 0)),
        out_shape=jax.ShapeDtypeStruct((2, 3, width // 2, dim), bf),
        compiler_params=params(10),
        cost_estimate=lasting(TIMES["outer"]),
        name="outer",
    )(g, normed)


def exchange(x, axis, size, mask):
    return lax.ppermute(x, axis, [(i, i ^ mask) for i in range(size)])


def tie(*values):
    return lax.optimization_barrier(values)


def add_bf(*parts):
    total = parts[0].astype(f32)
    for part in parts[1:]:
        total = total + part.astype(f32)
    return total.astype(bf)


def piece(x, index, count):
    rows = x.shape[0] // count
    return lax.dynamic_slice_in_dim(x, index * rows, rows, 0)


class Wide:
    def __init__(self, size):
        self.size = size
        self.me = lax.axis_index("wide")
        self.groups = [(1, 2)]
        bit = 2
        while bit < size:
            self.groups.append((bit, min(4, size // bit)))
            bit *= self.groups[-1][1]

    def send(self, group, x):
        bit, members = group
        mine = (self.me // bit) % members
        got = [
            exchange(piece(x, mine ^ k, members), "wide", self.size, bit * k)
            for k in range(1, members)
        ]
        return [piece(x, mine, members)] + got

    def gather(self, group, x):
        bit, members = group
        mine = (self.me // bit) % members
        got = [exchange(x, "wide", self.size, bit * k) for k in range(1, members)]
        if members == 2:
            low = mine == 0
            return jnp.concatenate([jnp.where(low, x, got[0]), jnp.where(low, got[0], x)], axis=0)
        rows = x.shape[0]
        out = jnp.zeros((members * rows,) + x.shape[1:], x.dtype)
        for k, part in enumerate([x] + got):
            out = lax.dynamic_update_slice_in_dim(out, part, (mine ^ k) * rows, 0)
        return out

    def over(self, groups, x):
        for group in groups:
            x = add_bf(*self.send(group, x))
        return x

    def back(self, groups, x):
        for group in reversed(groups):
            x = self.gather(group, x)
        return x


def on_device(
    wide,
    narrow,
    tokens,
    patch_counts,
    ln1_gain,
    ln1_bias,
    w_qkv,
    b_qv,
    w_out,
    b_out,
    ln2_gain,
    ln2_bias,
    w_up,
    b_up,
    w_down,
    b_down,
    cotangent,
):
    own_rows, dim = tokens.shape
    items = patch_counts.shape[0] // narrow
    seq = own_rows // items
    rows = -(-seq // PACK) * PACK
    heads = w_qkv.shape[2]
    units = w_up.shape[1]
    me = lax.axis_index("narrow")
    counts = lax.dynamic_slice_in_dim(patch_counts, me * items, items, 0)
    tokens3 = tokens.reshape(items, seq, dim)
    cot3 = cotangent.reshape(items, seq, dim)
    mate = lambda x: exchange(x, "narrow", narrow, 1)
    peer = lambda x: exchange(x, "narrow", narrow, 2)

    ring = Wide(wide)
    across = lambda x: exchange(x, "wide", wide, 1)
    x_axis, z_axis, more = ring.groups[0], ring.groups[1], ring.groups[2:]
    low_half = (ring.me % 2).astype(jnp.int32)
    half_dim = dim // 2

    w_own = w_qkv.transpose(1, 2, 0)
    w_peer, w_mate = peer(w_own), mate(w_own)
    b_peer, b_mate = peer(b_qv), mate(b_qv)
    vectors = jnp.concatenate([ln1_gain, ln1_bias, b_out, ln2_gain, ln2_bias, b_down]).reshape(6, dim)
    w_a = [w_own, w_mate]
    q_a, k_a, v_a, mixed_a, log_a, normed1 = attend(
        True, counts, tokens3, vectors, w_a, [b_qv, b_mate], rows
    )

    log_a, out_later, w_up, w_down, b_up = tie(log_a, w_out, w_up, w_down, b_up)
    out_peer, bias_peer = peer(out_later), peer(b_up)
    out_mate, bias_mate = mate(out_later), mate(b_up)
    up_mate, down_mate = mate(w_up), mate(w_down)
    up_part = lax.dynamic_slice_in_dim(w_up, low_half * half_dim, half_dim, 0)
    log_a, w_peer, b_peer, up_part = tie(log_a, w_peer, b_peer, up_part)
    up_first = peer(up_part)
    w_b = [w_peer, mate(w_peer)]
    q_b, k_b, v_b, mixed_b, log_b = attend(
        False, counts, tokens3, vectors, w_b, [b_peer, mate(b_peer)], rows
    )
    mixed_b, out_peer, up_first, down_later = tie(mixed_b, out_peer, up_first, w_down)
    down_peer = peer(down_later)
    out_a = jnp.concatenate([w_out, out_mate], axis=0)
    out_b = jnp.concatenate([out_peer, mate(out_peer)], axis=0)
    middle, normed2, cot_pad = branch(
        tokens3, cot3, mixed_a, mixed_b, out_a, out_b, vectors
    )
    middle, normed2, cot_pad, up_first = tie(middle, normed2, cot_pad, up_first)
    up_second, up_first_far = across(up_first), mate(up_first)
    flag = low_half.reshape(1)
    grad_part, hidden_a, dup_own, dup_mate, ddown_own, ddown_mate, dbias_a = feed(
        flag, normed2, cot_pad, None, [w_up, up_mate], [w_down, down_mate], [b_up, bias_mate]
    )

    grad_part, dup_own, dup_mate, ddown_own, ddown_mate, up_second, up_first_far = tie(
        grad_part, dup_own, dup_mate, ddown_own, ddown_mate, up_second, up_first_far
    )
    got_up, got_down = mate(dup_mate), mate(ddown_mate)
    up_second_far = mate(up_second)
    grad_part, down_peer = tie(grad_part, down_peer)
    ups = [up_first, up_second, up_first_far, up_second_far]
    downs = [down_peer, mate(down_peer)]
    grad_norm2, hidden_b, dup_peer, dup_far, ddown_peer, ddown_far, dbias_b = feed(
        flag, normed2, cot_pad, grad_part, ups, downs, [bias_peer, mate(bias_peer)]
    )
    grad_norm2, dup_peer, dup_far, ddown_peer, ddown_far, got_up, got_down = tie(
        grad_norm2, dup_peer, dup_far, ddown_peer, ddown_far, got_up, got_down
    )
    far_up, far_down = mate(dup_far), mate(ddown_far)
    down_keep, down_got = ring.send(x_axis, add_bf(ddown_own, got_down))
    grad_middle, gmix_a, gmix_b, dw_out, small_two = unbranch(
        middle, cot_pad, grad_norm2, vectors, mixed_a, mixed_b, out_a, out_b
    )

    grad_middle, gmix_a, gmix_b, dw_out, small_two, far_up, far_down = tie(
        grad_middle, gmix_a, gmix_b, dw_out, small_two, far_up, far_down
    )
    top = lambda x: x[:half_dim]
    bottom = lambda x: x[half_dim:]
    up_one = peer(add_bf(top(dup_peer), top(far_up)))
    pair_keep, pair_got = ring.send(x_axis, add_bf(ddown_peer, far_down))
    out_far, out_near = mate(dw_out[3]), mate(dw_out[1])
    g_b, dqkv_b, dbqv_b = unattend(counts, q_b, k_b, v_b, gmix_b, log_b, normed1)
    g_b, dqkv_b, dbqv_b, up_one, pair_keep, pair_got, down_keep, down_got, out_far, out_near, far_up, dup_peer = tie(
        g_b, dqkv_b, dbqv_b, up_one, pair_keep, pair_got, down_keep, down_got, out_far, out_near, far_up, dup_peer
    )

    def block(n, dqkv, dbqv, dbias):
        at = n % 2
        tail = [
            small_two[0:4],
            dbias[:, at * units : (at + 1) * units],
            jnp.pad(dbqv[0:2, at * heads : (at + 1) * heads], ((0, 0), (0, dim - heads))),
        ]
        tail = jnp.concatenate(tail, axis=0)
        pad = -(3 * heads + tail.shape[0]) % (8 * wide)
        tail = jnp.pad(tail, ((0, pad), (0, 0))).astype(bf)
        return jnp.concatenate([dqkv[at].reshape(3 * heads, dim), tail], axis=0)

    far_rest = mate(block(3, dqkv_b, dbqv_b, dbias_b))
    pair_half = peer(add_bf(pair_keep, pair_got))
    one_keep, one_got = ring.send(x_axis, add_bf(top(dup_own), top(got_up), up_one))
    vectors_late, dbqv_b = tie(vectors, dbqv_b)
    layer_out = project(middle, vectors_late, hidden_a, hidden_b, [w_down, down_mate] + downs, seq)
    gmix_a, far_rest, pair_half, layer_out = tie(gmix_a, far_rest, pair_half, layer_out)
    two_got = peer(
        jnp.concatenate([add_bf(bottom(dup_peer), bottom(far_up)), add_bf(dw_out[2], out_far)], axis=0)
    )
    rest_keep, rest_got = ring.send(x_axis, add_bf(block(2, dqkv_b, dbqv_b, dbias_b), far_rest))
    down_parts = ring.send(z_axis, add_bf(down_keep, down_got, pair_half))
    g_a, dqkv_a, dbqv_a = unattend(counts, q_a, k_a, v_a, gmix_a, log_a, normed1)
    g_a, dqkv_a, dbqv_a, rest_keep, rest_got, one_keep, one_got, two_got, *down_parts = tie(
        g_a, dqkv_a, dbqv_a, rest_keep, rest_got, one_keep, one_got, two_got, *down_parts
    )

    rest_mate = mate(block(1, dqkv_a, dbqv_a, dbias_a))
    rest_half = peer(add_bf(rest_keep, rest_got))
    two_own = jnp.concatenate([add_bf(bottom(dup_own), bottom(got_up)), add_bf(dw_out[0], out_near)], axis=0)
    two_keep, two_got = ring.send(x_axis, add_bf(two_own, two_got))
    down_sum = ring.back(ring.groups[1:], ring.over(more, add_bf(*down_parts)))
    rest_own = add_bf(block(0, dqkv_a, dbqv_a, dbias_a), rest_mate)
    rest_own, g_a = tie(rest_own, g_a)
    rest_keep, rest_got = ring.send(x_axis, rest_own)
    input_grad, small_one = unnorm(g_a, g_b, w_a + w_b, tokens3, vectors, grad_middle)
    input_grad, rest_keep, rest_got, two_keep, two_got, down_sum = tie(
        input_grad, rest_keep, rest_got, two_keep, two_got, down_sum
    )
    firsts = small_one[0:2]
    firsts = firsts + mate(firsts)
    firsts = firsts + peer(firsts)
    firsts = firsts + across(firsts)
    up_half = jnp.concatenate([add_bf(one_keep, one_got), add_bf(two_keep, two_got)], axis=0)
    rest_sum = add_bf(rest_keep, rest_got, rest_half)
    spot = lax.broadcasted_iota(jnp.int32, (rest_sum.shape[0], 1), 0) - (
        3 * heads + 7 - low_half * rest_sum.shape[0]
    )
    whole = firsts.astype(bf)
    rest_sum = jnp.where(spot == 0, whole[0:1], jnp.where(spot == 1, whole[1:2], rest_sum))
    rest_sum = ring.back(ring.groups, ring.over(ring.groups[1:], rest_sum))
    up_sum = ring.back(ring.groups, ring.over(ring.groups[1:], up_half))
    down_sum = ring.back([x_axis], down_sum)
    quarter = half_dim // 2
    parts = [up_sum[: up_sum.shape[0] // 2], up_sum[up_sum.shape[0] // 2 :]]
    up_sum = jnp.concatenate([x[:quarter] for x in parts] + [x[quarter:] for x in parts], axis=0)
    firsts = rest_sum[3 * heads + 7 : 3 * heads + 9].astype(f32)
    up_grad, out_grad = up_sum[:dim], up_sum[dim:]
    vec = rest_sum[3 * heads :].astype(f32)
    return (
        layer_out.reshape(own_rows, dim),
        input_grad.reshape(own_rows, dim),
        firsts[0],
        firsts[1],
        rest_sum[: 3 * heads].astype(f32).reshape(3, heads, dim).transpose(2, 0, 1),
        vec[5:7, :heads],
        out_grad.astype(f32),
        vec[2],
        vec[0],
        vec[1],
        up_grad.astype(f32),
        vec[4:5, :units],
        down_sum.astype(f32),
        vec[3],
    )


def solution(mesh):
    wide, narrow = mesh.shape["wide"], mesh.shape["narrow"]
    assert narrow == 4 and wide >= 4 and wide & (wide - 1) == 0
    rows = P(("wide", "narrow"), None)
    return jax.shard_map(
        functools.partial(on_device, wide, narrow),
        mesh=mesh,
        in_specs=(
            rows,
            P("wide"),
            P(),
            P(),
            P(None, None, "narrow"),
            P(None, "narrow"),
            P("narrow", None),
            P(),
            P(),
            P(),
            P(None, "narrow"),
            P(None, "narrow"),
            P("narrow", None),
            P(),
            rows,
        ),
        out_specs=(
            rows,
            rows,
            P(),
            P(),
            P(None, None, "narrow"),
            P(None, "narrow"),
            P("narrow", None),
            P(),
            P(),
            P(),
            P(None, "narrow"),
            P(None, "narrow"),
            P("narrow", None),
            P(),
        ),
        check_vma=False,
    )
```

```python
import functools

import jax
import jax.numpy as jnp
from jax import lax
from jax.experimental import pallas as pl
from jax.experimental.pallas import tpu as pltpu
from jax.sharding import PartitionSpec as P

HEAD = 64
WORDS = 40
PACK = 16
LANES = 128
BLOCK = 256

norm_eps = 1e-06
masked_value = -1000000000.0
bf = jnp.bfloat16
f32 = jnp.float32


def mul_nn(a, b):
    return lax.dot_general(a, b, (((1,), (0,)), ((), ())), preferred_element_type=f32)


def mul_nt(a, b):
    return lax.dot_general(a, b, (((1,), (1,)), ((), ())), preferred_element_type=f32)


def mul_tn(a, b):
    return lax.dot_general(a, b, (((0,), (0,)), ((), ())), preferred_element_type=f32)


def pad_rows(x, rows):
    if x.shape[0] == rows:
        return x
    return jnp.concatenate([x, jnp.zeros((rows - x.shape[0],) + x.shape[1:], x.dtype)], axis=0)


def unit_parts(x):
    centred = x - jnp.mean(x, axis=-1, keepdims=True)
    inv = lax.rsqrt(jnp.mean(centred * centred, axis=-1, keepdims=True) + norm_eps)
    return centred * inv, inv


def norm_back(grad, unit, inv, gain):
    scaled = grad * gain
    inner = (
        scaled
        - jnp.mean(scaled, axis=-1, keepdims=True)
        - unit * jnp.mean(scaled * unit, axis=-1, keepdims=True)
    )
    return inv * inner


def col_sum(x):
    return jnp.sum(x, axis=0, keepdims=True)


def full(shape):
    return pl.BlockSpec(shape, lambda *_: (0,) * len(shape))


def per_item(shape):
    return pl.BlockSpec((None,) + shape, lambda i, *_: (i,) + (0,) * len(shape))


TIMES = {
    "attend": 10,
    "branch": 3,
    "feed": 18,
    "project": 6,
    "unbranch": 6,
    "unattend": 11,
    "unnorm": 6,
}


def lasting(us):
    return pl.CostEstimate(flops=int(us * 1.15e9), bytes_accessed=0, transcendentals=0)


def params(mib):
    return pltpu.CompilerParams(vmem_limit_bytes=mib << 20)


def two_rows(w_one, w_two, c):
    return jnp.concatenate([w_one[c], w_two[c]], axis=0)


def attend_kernel(first, counts, tokens, small, w_one, w_two, b_one, b_two, *outs):
    if first:
        q_out, k_out, v_out, mixed_out, log_out, normed_out = outs
    else:
        q_out, k_out, v_out, mixed_out, log_out = outs
    rows, width = q_out.shape
    unit, _ = unit_parts(pad_rows(tokens[...].astype(f32), rows))
    normed = (unit * small[0:1] + small[1:2]).astype(bf)
    b = jnp.concatenate([b_one[...], b_two[...]], axis=1)
    if first:
        normed_out[...] = normed
    q = ((mul_nt(normed, two_rows(w_one, w_two, 0)) + b[0:1]) * 0.125).astype(bf)
    k = mul_nt(normed, two_rows(w_one, w_two, 1)).astype(bf)
    v = (mul_nt(normed, two_rows(w_one, w_two, 2)) + b[1:2]).astype(bf)
    q_out[...] = q
    k_out[...] = k
    v_out[...] = v
    valid = WORDS + counts[pl.program_id(0)]
    mask = jnp.where(lax.broadcasted_iota(jnp.int32, (1, rows), 1) < valid, 0.0, masked_value)
    lane = lax.broadcasted_iota(jnp.int32, (rows, LANES), 1)
    low = lane < HEAD
    logs = jnp.zeros((rows, LANES), f32)
    for p in range(width // LANES):
        at = slice(p * LANES, (p + 1) * LANES)
        q_two, k_two, v_two = q[:, at], k[:, at], v[:, at]
        tops, sums = [], []
        for h in range(2):
            here = low if h == 0 else ~low
            scores = mul_nt(jnp.where(here, q_two, 0), k_two) + mask
            top = jnp.max(scores, axis=1, keepdims=True)
            shifted = jnp.exp(scores - top).astype(bf)
            sums.append(mul_nn(shifted, jnp.where(here, v_two, 1)))
            tops.append(top)
        total = pltpu.roll(jnp.where(low, sums[1], sums[0]), HEAD, 1)
        mixed_out[:, at] = (jnp.where(low, sums[0], sums[1]) / total).astype(bf)
        log_two = jnp.log(total)
        logs = jnp.where(lane == 2 * p, tops[0] + log_two[:, 0:1], logs)
        logs = jnp.where(lane == 2 * p + 1, tops[1] + log_two[:, HEAD : HEAD + 1], logs)
    log_out[...] = logs.T[: log_out.shape[0]]


def attend(first, counts, tokens, small, ws, bs, rows):
    items, _, dim = tokens.shape
    width = 2 * ws[0].shape[1]
    wide_out = jax.ShapeDtypeStruct((items, rows, width), bf)
    outs = [wide_out] * 4 + [jax.ShapeDtypeStruct((items, 8, rows), f32)]
    specs = [per_item((rows, width))] * 4 + [per_item((8, rows))]
    if first:
        outs.append(jax.ShapeDtypeStruct((items, rows, dim), bf))
        specs.append(per_item((rows, dim)))
    return pl.pallas_call(
        functools.partial(attend_kernel, first),
        grid_spec=pltpu.PrefetchScalarGridSpec(
            num_scalar_prefetch=1,
            grid=(items,),
            in_specs=[
                per_item(tokens.shape[1:]),
                full(small.shape),
                full(ws[0].shape),
                full(ws[0].shape),
                full(bs[0].shape),
                full(bs[0].shape),
            ],
            out_specs=specs,
        ),
        out_shape=outs,
        compiler_params=params(8),
        cost_estimate=lasting(TIMES["attend"]),
        name="attend",
    )(counts, tokens, small, *ws, *bs)


def branch_kernel(tokens, cot, mixed_a, mixed_b, w_a, w_b, small, middle_out, normed_out, cot_out):
    rows = normed_out.shape[0]
    middle = (
        pad_rows(tokens[...].astype(f32), rows)
        + (mul_nn(mixed_a[...], w_a[...]) + mul_nn(mixed_b[...], w_b[...]))
        + small[2:3]
    )
    middle_out[...] = middle
    unit, _ = unit_parts(middle)
    normed_out[...] = (unit * small[3:4] + small[4:5]).astype(bf)
    cot_out[...] = pad_rows(cot[...].astype(f32), rows).astype(bf)


def branch(tokens, cot, mixed_a, mixed_b, w_a, w_b, small):
    items, seq, dim = tokens.shape
    _, rows, width = mixed_a.shape
    return pl.pallas_call(
        branch_kernel,
        grid=(items,),
        in_specs=[per_item((seq, dim))] * 2
        + [per_item((rows, width))] * 2
        + [full(w_a.shape)] * 2
        + [full(small.shape)],
        out_specs=[per_item((rows, dim))] * 3,
        out_shape=[
            jax.ShapeDtypeStruct((items, rows, dim), f32),
            jax.ShapeDtypeStruct((items, rows, dim), bf),
            jax.ShapeDtypeStruct((items, rows, dim), bf),
        ],
        compiler_params=params(7),
        cost_estimate=lasting(TIMES["branch"]),
        name="branch",
    )(tokens, cot, mixed_a, mixed_b, w_a, w_b, small)


def feed_kernel(
    again, per, low_half, normed, cot, base_grad, *refs
):
    n_weights = 6 if again else 4
    weights, rest = refs[:n_weights], refs[n_weights:]
    bias_a, bias_b, grad_ref, hidden_ref, dup_a, dup_b, ddown_a, ddown_b, dbias_ref, gu_ref = rest
    step = pl.program_id(0)
    items, rows, dim = normed.shape
    is_a = step < per

    @pl.when(step == 0)
    def _():
        grad_ref[...] = base_grad[...] if again else jnp.zeros_like(grad_ref)

    if again:
        up_a, up_b, up_c, up_d, down_a, down_c = weights
        is_low = low_half[0] == 0
        first = jnp.where(is_a, up_a[...], up_c[...])
        second = jnp.where(is_a, up_b[...], up_d[...])
        w_up = jnp.concatenate(
            [jnp.where(is_low, first, second), jnp.where(is_low, second, first)], axis=0
        )
    else:
        up_a, up_c, down_a, down_c = weights
        w_up = jnp.where(is_a, up_a[...], up_c[...])
    w_down = jnp.where(is_a, down_a[...], down_c[...])
    bias = jnp.where(is_a, bias_a[...].astype(f32), bias_b[...].astype(f32))
    bias_sum = jnp.zeros((1, w_up.shape[1]), f32)
    for i in range(items):
        up = mul_nn(normed[i], w_up) + bias
        grad_hidden = mul_nt(cot[i], w_down)
        cdf = 0.5 * (1.0 + lax.erf(up * 0.7071067811865476))
        slope = cdf + up * (jnp.exp(-0.5 * up * up) * 0.3989422804014327)
        gu = (slope * grad_hidden).astype(bf)
        hidden_ref[i] = (up * cdf).astype(bf)
        gu_ref[i] = gu
        bias_sum = bias_sum + col_sum(gu.astype(f32))
        grad_ref[i] += mul_nt(gu, w_up)
    dbias_ref[...] = bias_sum
    flat = (items * rows, dim)
    hidden = hidden_ref[...].reshape(items * rows, -1)
    gu = gu_ref[...].reshape(items * rows, -1)
    ddown = mul_tn(hidden, cot[...].reshape(flat)).astype(bf)
    dup = mul_tn(normed[...].reshape(flat), gu).astype(bf)

    @pl.when(is_a)
    def _():
        ddown_a[...] = ddown
        dup_a[...] = dup

    @pl.when(jnp.logical_not(is_a))
    def _():
        ddown_b[...] = ddown
        dup_b[...] = dup


def feed(low_half, normed, cot, base_grad, ups, downs, biases):
    again = base_grad is not None
    items, rows, dim = normed.shape
    units = ups[0].shape[1]
    per = units // BLOCK
    steps = 2 * per
    full3 = full((items, rows, dim))
    if not again:
        base_grad = biases[0]
    half = len(ups) // 2
    first = lambda j: jnp.minimum(j, per - 1)
    second = lambda j: jnp.maximum(j - per, 0)
    across = lambda part, place: pl.BlockSpec((part, BLOCK), lambda j, *_: (0, place(j)))
    down = lambda place: pl.BlockSpec((BLOCK, dim), lambda j, *_: (place(j), 0))
    return pl.pallas_call(
        functools.partial(feed_kernel, again, per),
        grid_spec=pltpu.PrefetchScalarGridSpec(
            num_scalar_prefetch=1,
            grid=(steps,),
            in_specs=[full3, full3, full3 if again else full(base_grad.shape)]
            + [across(dim // half, first)] * half
            + [across(dim // half, second)] * half
            + [down(first), down(second)]
            + [across(1, first), across(1, second)],
            out_specs=[
                full3,
                pl.BlockSpec((items, rows, BLOCK), lambda j, *_: (0, 0, j)),
                across(dim, first),
                across(dim, second),
                down(first),
                down(second),
                pl.BlockSpec((1, BLOCK), lambda j, *_: (0, j)),
            ],
            scratch_shapes=[pltpu.VMEM((items, rows, BLOCK), bf)],
        ),
        out_shape=[
            jax.ShapeDtypeStruct((items, rows, dim), f32),
            jax.ShapeDtypeStruct((items, rows, 2 * units), bf),
            jax.ShapeDtypeStruct((dim, units), bf),
            jax.ShapeDtypeStruct((dim, units), bf),
            jax.ShapeDtypeStruct((units, dim), bf),
            jax.ShapeDtypeStruct((units, dim), bf),
            jax.ShapeDtypeStruct((1, 2 * units), f32),
        ],
        compiler_params=params(14),
        cost_estimate=lasting(TIMES["feed"]),
        name="feed",
    )(low_half, normed, cot, base_grad, *ups, *downs, *biases)


def project_kernel(middle, small, hidden_a, hidden_b, *refs):
    weights, out_ref = refs[:4], refs[4]
    units = weights[0].shape[0]
    total = middle[...] + small[5:6]
    for n, w in enumerate(weights):
        hidden = (hidden_a, hidden_b)[n // 2]
        total = total + mul_nn(hidden[:, (n % 2) * units : (n % 2 + 1) * units], w[...])
    out_ref[...] = total[: out_ref.shape[0]]


def project(middle, small, hidden_a, hidden_b, weights, seq):
    items, rows, dim = middle.shape
    both = per_item(hidden_a.shape[1:])
    return pl.pallas_call(
        project_kernel,
        grid=(items,),
        in_specs=[per_item((rows, dim)), full(small.shape), both, both] + [full(weights[0].shape)] * 4,
        out_specs=per_item((seq, dim)),
        out_shape=jax.ShapeDtypeStruct((items, seq, dim), f32),
        compiler_params=params(14),
        cost_estimate=lasting(TIMES["project"]),
        name="project",
    )(middle, small, hidden_a, hidden_b, *weights)


def unbranch_kernel(
    middle, cot, grad_in, vectors, mixed_a, mixed_b, w_a, w_b,
    grad_out, gmix_a, gmix_b, dw_out, small, branch_ref
):
    step = pl.program_id(0)
    unit, inv = unit_parts(middle[...])
    grad = grad_in[...]
    cot_f = cot[...].astype(f32)
    grad_middle = cot_f + norm_back(grad, unit, inv, vectors[3:4])
    grad_out[...] = grad_middle
    grad_branch = grad_middle.astype(bf)
    branch_ref[step] = grad_branch
    gmix_a[...] = mul_nt(grad_branch, w_a[...]).astype(bf)
    gmix_b[...] = mul_nt(grad_branch, w_b[...]).astype(bf)

    @pl.when(step == 0)
    def _():
        small[...] = jnp.zeros_like(small)

    small[0:1] += col_sum(grad * unit)
    small[1:2] += col_sum(grad)
    small[2:3] += col_sum(grad_branch.astype(f32))
    small[3:4] += col_sum(cot_f)

    @pl.when(step == pl.num_programs(0) - 1)
    def _():
        items, rows, dim = branch_ref.shape
        gb = branch_ref[...].reshape(items * rows, dim)
        width = mixed_a.shape[2]
        quarter = width // 2
        for n, mixed in ((0, mixed_a), (1, mixed_b)):
            dw = mul_tn(mixed[...].reshape(items * rows, width), gb).astype(bf)
            dw_out[2 * n] = dw[:quarter]
            dw_out[2 * n + 1] = dw[quarter:]


def unbranch(middle, cot, grad_in, vectors, mixed_a, mixed_b, w_a, w_b):
    items, rows, dim = middle.shape
    width = mixed_a.shape[2]
    each = per_item((rows, dim))
    return pl.pallas_call(
        unbranch_kernel,
        grid=(items,),
        in_specs=[each, each, each, full(vectors.shape)]
        + [full(mixed_a.shape)] * 2
        + [full(w_a.shape)] * 2,
        out_specs=[
            each,
            per_item((rows, width)),
            per_item((rows, width)),
            full((4, width // 2, dim)),
            full((8, dim)),
        ],
        out_shape=[
            jax.ShapeDtypeStruct((items, rows, dim), f32),
            jax.ShapeDtypeStruct((items, rows, width), bf),
            jax.ShapeDtypeStruct((items, rows, width), bf),
            jax.ShapeDtypeStruct((4, width // 2, dim), bf),
            jax.ShapeDtypeStruct((8, dim), f32),
        ],
        scratch_shapes=[pltpu.VMEM((items, rows, dim), bf)],
        compiler_params=params(12),
        cost_estimate=lasting(TIMES["unbranch"]),
        name="unbranch",
    )(middle, cot, grad_in, vectors, mixed_a, mixed_b, w_a, w_b)


def unattend_kernel(counts, q, k, v, gmix, logs, normed, g_ref, dw_out, db_out):
    step = pl.program_id(0)
    rows, width = q.shape
    valid = WORDS + counts[step]
    mask = jnp.where(lax.broadcasted_iota(jnp.int32, (rows, 1), 0) < valid, 0.0, masked_value)
    low = lax.broadcasted_iota(jnp.int32, (rows, LANES), 1) < HEAD
    def one_pair(p, carry):
        at = pl.ds(pl.multiple_of(p * LANES, LANES), LANES)
        q_two, k_two, v_two, g_two = q[:, at], k[:, at], v[:, at], gmix[:, at]
        dq, dk, dv = [], [], []
        for h in range(2):
            here = low if h == 0 else ~low
            scores = mul_nt(jnp.where(here, k_two, 0), q_two) + mask
            prob = jnp.exp(scores - logs[pl.ds(2 * p + h, 1)])
            grad_prob = mul_nt(jnp.where(here, v_two, 0), g_two)
            inner = jnp.sum(grad_prob * prob, axis=0, keepdims=True)
            grad_scores = (prob * (grad_prob - inner)).astype(bf)
            dv.append(mul_nn(prob.astype(bf), g_two))
            dk.append(mul_nn(grad_scores, q_two))
            dq.append(mul_tn(grad_scores, k_two))
        for c, pair in enumerate((dq, dk, dv)):
            merged = jnp.where(low, pair[0], pair[1]).astype(bf)
            if c == 0:
                merged = merged * jnp.asarray(0.125, bf)
            g_ref[step, :, pl.ds(pl.multiple_of(c * width + p * LANES, LANES), LANES)] = merged
        return carry

    lax.fori_loop(0, width // LANES, one_pair, 0)

    @pl.when(step == 0)
    def _():
        db_out[...] = jnp.zeros_like(db_out)

    db_out[0:1] += col_sum(g_ref[step, :, :width].astype(f32))
    db_out[1:2] += col_sum(g_ref[step, :, 2 * width :].astype(f32))

    @pl.when(step == pl.num_programs(0) - 1)
    def _():
        items, _, dim = normed.shape
        flat = normed[...].reshape(items * rows, dim)
        quarter = width // 2
        for c in range(3):
            g = g_ref[:, :, c * width : (c + 1) * width].reshape(items * rows, width)
            dw = mul_tn(g, flat).astype(bf)
            dw_out[0, c] = dw[:quarter]
            dw_out[1, c] = dw[quarter:]


def unattend(counts, q, k, v, gmix, logs, normed):
    items, rows, width = q.shape
    dim = normed.shape[2]
    return pl.pallas_call(
        unattend_kernel,
        grid_spec=pltpu.PrefetchScalarGridSpec(
            num_scalar_prefetch=1,
            grid=(items,),
            in_specs=[per_item((rows, width))] * 4 + [per_item((8, rows)), full(normed.shape)],
            out_specs=[
                full((items, rows, 3 * width)),
                full((2, 3, width // 2, dim)),
                full((8, width)),
            ],
        ),
        out_shape=[
            jax.ShapeDtypeStruct((items, rows, 3 * width), bf),
            jax.ShapeDtypeStruct((2, 3, width // 2, dim), bf),
            jax.ShapeDtypeStruct((8, width), f32),
        ],
        compiler_params=params(12),
        cost_estimate=lasting(TIMES["unattend"]),
        name="unattend",
    )(counts, q, k, v, gmix, logs, normed)


def unnorm_kernel(g_a, g_b, w_one, w_two, w_three, w_four, tokens, vectors, grad_middle, x_out, small):
    rows = g_a.shape[0]
    grad = 0.0
    for g, one, two in ((g_a, w_one, w_two), (g_b, w_three, w_four)):
        w = jnp.concatenate([two_rows(one, two, c) for c in range(3)], axis=0)
        grad = grad + mul_nn(g[...], w)
    unit, inv = unit_parts(pad_rows(tokens[...].astype(f32), rows))

    @pl.when(pl.program_id(0) == 0)
    def _():
        small[...] = jnp.zeros_like(small)

    small[0:1] += col_sum(grad * unit)
    small[1:2] += col_sum(grad)
    x_out[...] = (grad_middle[...] + norm_back(grad, unit, inv, vectors[0:1]))[: x_out.shape[0]]


def unnorm(g_a, g_b, ws, tokens, vectors, grad_middle):
    items, rows, width3 = g_a.shape
    seq, dim = tokens.shape[1:]
    return pl.pallas_call(
        unnorm_kernel,
        grid=(items,),
        in_specs=[per_item((rows, width3))] * 2
        + [full(ws[0].shape)] * 4
        + [per_item((seq, dim)), full(vectors.shape), per_item((rows, dim))],
        out_specs=[per_item((seq, dim)), full((8, dim))],
        out_shape=[
            jax.ShapeDtypeStruct((items, seq, dim), f32),
            jax.ShapeDtypeStruct((8, dim), f32),
        ],
        compiler_params=params(12),
        cost_estimate=lasting(TIMES["unnorm"]),
        name="unnorm",
    )(g_a, g_b, *ws, tokens, vectors, grad_middle)


def outer_kernel(g, normed, dw_out):
    items, rows, dim = normed.shape
    dw = mul_tn(g[...].reshape(items * rows, -1), normed[...].reshape(items * rows, dim)).astype(bf)
    quarter = dw.shape[0] // 2
    dw_out[0] = dw[:quarter]
    dw_out[1] = dw[quarter:]


def outer(g, normed):
    items, rows, width3 = g.shape
    dim = normed.shape[2]
    width = width3 // 3
    return pl.pallas_call(
        outer_kernel,
        grid=(3,),
        in_specs=[pl.BlockSpec((items, rows, width), lambda c: (0, 0, c)), full(normed.shape)],
        out_specs=pl.BlockSpec((2, None, width // 2, dim), lambda c: (0, c, 0, 0)),
        out_shape=jax.ShapeDtypeStruct((2, 3, width // 2, dim), bf),
        compiler_params=params(10),
        cost_estimate=lasting(TIMES["outer"]),
        name="outer",
    )(g, normed)


def exchange(x, axis, size, mask):
    return lax.ppermute(x, axis, [(i, i ^ mask) for i in range(size)])


def tie(*values):
    return lax.optimization_barrier(values)


def add_bf(*parts):
    total = parts[0].astype(f32)
    for part in parts[1:]:
        total = total + part.astype(f32)
    return total.astype(bf)


def piece(x, index, count):
    rows = x.shape[0] // count
    return lax.dynamic_slice_in_dim(x, index * rows, rows, 0)


class Wide:
    def __init__(self, size):
        self.size = size
        self.me = lax.axis_index("wide")
        self.groups = [(1, 2)]
        bit = 2
        while bit < size:
            self.groups.append((bit, min(4, size // bit)))
            bit *= self.groups[-1][1]

    def send(self, group, x):
        bit, members = group
        mine = (self.me // bit) % members
        got = [
            exchange(piece(x, mine ^ k, members), "wide", self.size, bit * k)
            for k in range(1, members)
        ]
        return [piece(x, mine, members)] + got

    def gathered(self, group, x):
        bit, members = group
        return [x] + [exchange(x, "wide", self.size, bit * k) for k in range(1, members)]

    def place(self, group, pieces):
        bit, members = group
        mine = (self.me // bit) % members
        if members == 2:
            low = mine == 0
            x, got = pieces
            return jnp.concatenate([jnp.where(low, x, got), jnp.where(low, got, x)], axis=0)
        x = pieces[0]
        rows = x.shape[0]
        out = jnp.zeros((members * rows,) + x.shape[1:], x.dtype)
        for k, part in enumerate(pieces):
            out = lax.dynamic_update_slice_in_dim(out, part, (mine ^ k) * rows, 0)
        return out

    def gather(self, group, x):
        return self.place(group, self.gathered(group, x))

    def over(self, groups, x):
        for group in groups:
            x = add_bf(*self.send(group, x))
        return x

    def back(self, groups, x):
        for group in reversed(groups):
            x = self.gather(group, x)
        return x


def on_device(
    wide,
    narrow,
    tokens,
    patch_counts,
    ln1_gain,
    ln1_bias,
    w_qkv,
    b_qv,
    w_out,
    b_out,
    ln2_gain,
    ln2_bias,
    w_up,
    b_up,
    w_down,
    b_down,
    cotangent,
):
    own_rows, dim = tokens.shape
    items = patch_counts.shape[0] // narrow
    seq = own_rows // items
    rows = -(-seq // PACK) * PACK
    heads = w_qkv.shape[2]
    units = w_up.shape[1]
    me = lax.axis_index("narrow")
    counts = lax.dynamic_slice_in_dim(patch_counts, me * items, items, 0)
    tokens3 = tokens.reshape(items, seq, dim)
    cot3 = cotangent.reshape(items, seq, dim)
    mate = lambda x: exchange(x, "narrow", narrow, 1)
    peer = lambda x: exchange(x, "narrow", narrow, 2)

    ring = Wide(wide)
    across = lambda x: exchange(x, "wide", wide, 1)
    x_axis, z_axis, more = ring.groups[0], ring.groups[1], ring.groups[2:]
    low_half = (ring.me % 2).astype(jnp.int32)
    half_dim = dim // 2

    w_own = w_qkv.transpose(1, 2, 0)
    w_peer, w_mate = peer(w_own), mate(w_own)
    b_peer, b_mate = peer(b_qv), mate(b_qv)
    vectors = jnp.concatenate([ln1_gain, ln1_bias, b_out, ln2_gain, ln2_bias, b_down]).reshape(6, dim)
    w_a = [w_own, w_mate]
    q_a, k_a, v_a, mixed_a, log_a, normed1 = attend(
        True, counts, tokens3, vectors, w_a, [b_qv, b_mate], rows
    )

    log_a, out_later, w_up, w_down, b_up = tie(log_a, w_out, w_up, w_down, b_up)
    out_peer, bias_peer = peer(out_later), peer(b_up)
    out_mate, bias_mate = mate(out_later), mate(b_up)
    up_mate, down_mate = mate(w_up), mate(w_down)
    up_part = lax.dynamic_slice_in_dim(w_up, low_half * half_dim, half_dim, 0)
    log_a, w_peer, b_peer, up_part = tie(log_a, w_peer, b_peer, up_part)
    up_first = peer(up_part)
    w_b = [w_peer, mate(w_peer)]
    q_b, k_b, v_b, mixed_b, log_b = attend(
        False, counts, tokens3, vectors, w_b, [b_peer, mate(b_peer)], rows
    )
    mixed_b, out_peer, up_first, down_later = tie(mixed_b, out_peer, up_first, w_down)
    down_peer = peer(down_later)
    out_a = jnp.concatenate([w_out, out_mate], axis=0)
    out_b = jnp.concatenate([out_peer, mate(out_peer)], axis=0)
    middle, normed2, cot_pad = branch(
        tokens3, cot3, mixed_a, mixed_b, out_a, out_b, vectors
    )
    middle, normed2, cot_pad, up_first = tie(middle, normed2, cot_pad, up_first)
    up_second, up_first_far = across(up_first), mate(up_first)
    flag = low_half.reshape(1)
    grad_part, hidden_a, dup_own, dup_mate, ddown_own, ddown_mate, dbias_a = feed(
        flag, normed2, cot_pad, None, [w_up, up_mate], [w_down, down_mate], [b_up, bias_mate]
    )

    grad_part, dup_own, dup_mate, ddown_own, ddown_mate, up_second, up_first_far = tie(
        grad_part, dup_own, dup_mate, ddown_own, ddown_mate, up_second, up_first_far
    )
    got_up, got_down = mate(dup_mate), mate(ddown_mate)
    up_second_far = mate(up_second)
    grad_part, down_peer = tie(grad_part, down_peer)
    ups = [up_first, up_second, up_first_far, up_second_far]
    downs = [down_peer, mate(down_peer)]
    grad_norm2, hidden_b, dup_peer, dup_far, ddown_peer, ddown_far, dbias_b = feed(
        flag, normed2, cot_pad, grad_part, ups, downs, [bias_peer, mate(bias_peer)]
    )
    grad_norm2, dup_peer, dup_far, ddown_peer, ddown_far, got_up, got_down = tie(
        grad_norm2, dup_peer, dup_far, ddown_peer, ddown_far, got_up, got_down
    )
    far_up, far_down = mate(dup_far), mate(ddown_far)
    grad_middle, gmix_a, gmix_b, dw_out, small_two = unbranch(
        middle, cot_pad, grad_norm2, vectors, mixed_a, mixed_b, out_a, out_b
    )

    grad_middle, gmix_a, gmix_b, dw_out, small_two, far_up, far_down = tie(
        grad_middle, gmix_a, gmix_b, dw_out, small_two, far_up, far_down
    )
    top = lambda x: x[:half_dim]
    bottom = lambda x: x[half_dim:]
    up_one = peer(add_bf(top(dup_peer), top(far_up)))
    pair_keep, pair_got = ring.send(x_axis, add_bf(ddown_peer, far_down))
    out_far, out_near = mate(dw_out[3]), mate(dw_out[1])
    g_b, dqkv_b, dbqv_b = unattend(counts, q_b, k_b, v_b, gmix_b, log_b, normed1)
    g_b, dqkv_b, dbqv_b, up_one, pair_keep, pair_got, ddown_own, got_down, out_far, out_near, far_up, dup_peer = tie(
        g_b, dqkv_b, dbqv_b, up_one, pair_keep, pair_got, ddown_own, got_down, out_far, out_near, far_up, dup_peer
    )
    down_keep, down_got = ring.send(x_axis, add_bf(ddown_own, got_down))

    def block(n, dqkv, dbqv, dbias):
        at = n % 2
        tail = [
            small_two[0:4],
            dbias[:, at * units : (at + 1) * units],
            jnp.pad(dbqv[0:2, at * heads : (at + 1) * heads], ((0, 0), (0, dim - heads))),
        ]
        tail = jnp.concatenate(tail, axis=0)
        pad = -(3 * heads + tail.shape[0]) % (8 * wide)
        tail = jnp.pad(tail, ((0, pad), (0, 0))).astype(bf)
        return jnp.concatenate([dqkv[at].reshape(3 * heads, dim), tail], axis=0)

    far_rest = mate(block(3, dqkv_b, dbqv_b, dbias_b))
    pair_half = peer(add_bf(pair_keep, pair_got))
    one_keep, one_got = ring.send(x_axis, add_bf(top(dup_own), top(got_up), up_one))
    vectors_late, dbqv_b = tie(vectors, dbqv_b)
    layer_out = project(middle, vectors_late, hidden_a, hidden_b, [w_down, down_mate] + downs, seq)
    gmix_a, far_rest, pair_half, layer_out, down_keep, down_got = tie(
        gmix_a, far_rest, pair_half, layer_out, down_keep, down_got
    )
    two_got = peer(
        jnp.concatenate([add_bf(bottom(dup_peer), bottom(far_up)), add_bf(dw_out[2], out_far)], axis=0)
    )
    rest_keep, rest_got = ring.send(x_axis, add_bf(block(2, dqkv_b, dbqv_b, dbias_b), far_rest))
    down_parts = ring.send(z_axis, add_bf(down_keep, down_got, pair_half))
    g_a, dqkv_a, dbqv_a = unattend(counts, q_a, k_a, v_a, gmix_a, log_a, normed1)
    g_a, dqkv_a, dbqv_a, rest_keep, rest_got, one_keep, one_got, two_got, *down_parts = tie(
        g_a, dqkv_a, dbqv_a, rest_keep, rest_got, one_keep, one_got, two_got, *down_parts
    )

    rest_mate = mate(block(1, dqkv_a, dbqv_a, dbias_a))
    rest_half = peer(add_bf(rest_keep, rest_got))
    two_own = jnp.concatenate([add_bf(bottom(dup_own), bottom(got_up)), add_bf(dw_out[0], out_near)], axis=0)
    two_keep, two_got = ring.send(x_axis, add_bf(two_own, two_got))
    down_all = ring.gathered(z_axis, ring.back(more, ring.over(more, add_bf(*down_parts))))
    rest_own = add_bf(block(0, dqkv_a, dbqv_a, dbias_a), rest_mate)
    rest_own, g_a = tie(rest_own, g_a)
    rest_keep, rest_got = ring.send(x_axis, rest_own)
    input_grad, small_one = unnorm(g_a, g_b, w_a + w_b, tokens3, vectors, grad_middle)
    small_one, rest_keep, rest_got, rest_half, two_keep, two_got, *down_all = tie(
        small_one, rest_keep, rest_got, rest_half, two_keep, two_got, *down_all
    )
    down_sum = ring.place(z_axis, down_all)
    firsts = small_one[0:2]
    firsts = firsts + mate(firsts)
    firsts = firsts + peer(firsts)
    firsts = firsts + across(firsts)
    up_half = jnp.concatenate([add_bf(one_keep, one_got), add_bf(two_keep, two_got)], axis=0)
    rest_sum = add_bf(rest_keep, rest_got, rest_half)
    spot = lax.broadcasted_iota(jnp.int32, (rest_sum.shape[0], 1), 0) - (
        3 * heads + 7 - low_half * rest_sum.shape[0]
    )
    whole = firsts.astype(bf)
    rest_sum = jnp.where(spot == 0, whole[0:1], jnp.where(spot == 1, whole[1:2], rest_sum))
    rest_sum = ring.back(ring.groups, ring.over(ring.groups[1:], rest_sum))
    up_sum = ring.back(ring.groups, ring.over(ring.groups[1:], up_half))
    down_sum = ring.back([x_axis], down_sum)
    quarter = half_dim // 2
    parts = [up_sum[: up_sum.shape[0] // 2], up_sum[up_sum.shape[0] // 2 :]]
    up_sum = jnp.concatenate([x[:quarter] for x in parts] + [x[quarter:] for x in parts], axis=0)
    firsts = rest_sum[3 * heads + 7 : 3 * heads + 9].astype(f32)
    up_grad, out_grad = up_sum[:dim], up_sum[dim:]
    vec = rest_sum[3 * heads :].astype(f32)
    return (
        layer_out.reshape(own_rows, dim),
        input_grad.reshape(own_rows, dim),
        firsts[0],
        firsts[1],
        rest_sum[: 3 * heads].astype(f32).reshape(3, heads, dim).transpose(2, 0, 1),
        vec[5:7, :heads],
        out_grad.astype(f32),
        vec[2],
        vec[0],
        vec[1],
        up_grad.astype(f32),
        vec[4:5, :units],
        down_sum.astype(f32),
        vec[3],
    )


def solution(mesh):
    wide, narrow = mesh.shape["wide"], mesh.shape["narrow"]
    assert narrow == 4 and wide >= 4 and wide & (wide - 1) == 0
    rows = P(("wide", "narrow"), None)
    return jax.shard_map(
        functools.partial(on_device, wide, narrow),
        mesh=mesh,
        in_specs=(
            rows,
            P("wide"),
            P(),
            P(),
            P(None, None, "narrow"),
            P(None, "narrow"),
            P("narrow", None),
            P(),
            P(),
            P(),
            P(None, "narrow"),
            P(None, "narrow"),
            P("narrow", None),
            P(),
            rows,
        ),
        out_specs=(
            rows,
            rows,
            P(),
            P(),
            P(None, None, "narrow"),
            P(None, "narrow"),
            P("narrow", None),
            P(),
            P(),
            P(),
            P(None, "narrow"),
            P(None, "narrow"),
            P("narrow", None),
            P(),
        ),
        check_vma=False,
    )
```

```python
import functools

import jax
import jax.numpy as jnp
from jax import lax
from jax.experimental import pallas as pl
from jax.experimental.pallas import tpu as pltpu
from jax.sharding import PartitionSpec as P

HEAD = 64
WORDS = 40
PACK = 16
LANES = 128
BLOCK = 768
CHUNK = 256

norm_eps = 1e-06
masked_value = -1000000000.0
bf = jnp.bfloat16
f32 = jnp.float32


def mul_nn(a, b):
    return lax.dot_general(a, b, (((1,), (0,)), ((), ())), preferred_element_type=f32)


def mul_nt(a, b):
    return lax.dot_general(a, b, (((1,), (1,)), ((), ())), preferred_element_type=f32)


def mul_tn(a, b):
    return lax.dot_general(a, b, (((0,), (0,)), ((), ())), preferred_element_type=f32)


def pad_rows(x, rows):
    if x.shape[0] == rows:
        return x
    return jnp.concatenate([x, jnp.zeros((rows - x.shape[0],) + x.shape[1:], x.dtype)], axis=0)


def unit_parts(x):
    centred = x - jnp.mean(x, axis=-1, keepdims=True)
    inv = lax.rsqrt(jnp.mean(centred * centred, axis=-1, keepdims=True) + norm_eps)
    return centred * inv, inv


def norm_back(grad, unit, inv, gain):
    scaled = grad * gain
    inner = (
        scaled
        - jnp.mean(scaled, axis=-1, keepdims=True)
        - unit * jnp.mean(scaled * unit, axis=-1, keepdims=True)
    )
    return inv * inner


def col_sum(x):
    return jnp.sum(x, axis=0, keepdims=True)


def full(shape):
    return pl.BlockSpec(shape, lambda *_: (0,) * len(shape))


def per_item(shape):
    return pl.BlockSpec((None,) + shape, lambda i, *_: (i,) + (0,) * len(shape))


TIMES = {
    "attend": 10,
    "branch": 3,
    "feed": 18,
    "project": 6,
    "unbranch": 6,
    "unattend": 11,
    "unnorm": 6,
}


def lasting(us):
    return pl.CostEstimate(flops=int(us * 1.15e9), bytes_accessed=0, transcendentals=0)


def later(shape, dtype):
    return pltpu.HBM(shape, dtype)


def in_hbm(x):
    return pltpu.with_memory_space_constraint(x, pltpu.HBM)


def params(mib):
    return pltpu.CompilerParams(vmem_limit_bytes=mib << 20)


def two_rows(w_one, w_two, c):
    return jnp.concatenate([w_one[c], w_two[c]], axis=0)


def attend_kernel(first, counts, tokens, small, w_one, w_two, b_one, b_two, *outs):
    if first:
        q_out, k_out, v_out, mixed_out, log_out, normed_out = outs
    else:
        q_out, k_out, v_out, mixed_out, log_out = outs
    rows, width = q_out.shape
    unit, _ = unit_parts(pad_rows(tokens[...].astype(f32), rows))
    normed = (unit * small[0:1] + small[1:2]).astype(bf)
    b = jnp.concatenate([b_one[...], b_two[...]], axis=1)
    if first:
        normed_out[...] = normed
    q = ((mul_nt(normed, two_rows(w_one, w_two, 0)) + b[0:1]) * 0.125).astype(bf)
    k = mul_nt(normed, two_rows(w_one, w_two, 1)).astype(bf)
    v = (mul_nt(normed, two_rows(w_one, w_two, 2)) + b[1:2]).astype(bf)
    q_out[...] = q
    k_out[...] = k
    v_out[...] = v
    valid = WORDS + counts[pl.program_id(0)]
    mask = jnp.where(lax.broadcasted_iota(jnp.int32, (1, rows), 1) < valid, 0.0, masked_value)
    lane = lax.broadcasted_iota(jnp.int32, (rows, LANES), 1)
    low = lane < HEAD
    logs = jnp.zeros((rows, LANES), f32)
    for p in range(width // LANES):
        at = slice(p * LANES, (p + 1) * LANES)
        q_two, k_two, v_two = q[:, at], k[:, at], v[:, at]
        tops, sums = [], []
        for h in range(2):
            here = low if h == 0 else ~low
            scores = mul_nt(jnp.where(here, q_two, 0), k_two) + mask
            top = jnp.max(scores, axis=1, keepdims=True)
            shifted = jnp.exp(scores - top).astype(bf)
            sums.append(mul_nn(shifted, jnp.where(here, v_two, 1)))
            tops.append(top)
        total = pltpu.roll(jnp.where(low, sums[1], sums[0]), HEAD, 1)
        mixed_out[:, at] = (jnp.where(low, sums[0], sums[1]) / total).astype(bf)
        log_two = jnp.log(total)
        logs = jnp.where(lane == 2 * p, tops[0] + log_two[:, 0:1], logs)
        logs = jnp.where(lane == 2 * p + 1, tops[1] + log_two[:, HEAD : HEAD + 1], logs)
    log_out[...] = logs.T[: log_out.shape[0]]


def attend(first, counts, tokens, small, ws, bs, rows):
    items, _, dim = tokens.shape
    width = 2 * ws[0].shape[1]
    wide_out = jax.ShapeDtypeStruct((items, rows, width), bf)
    outs = [wide_out] * 4 + [jax.ShapeDtypeStruct((items, 8, rows), f32)]
    specs = [per_item((rows, width))] * 4 + [per_item((8, rows))]
    if first:
        outs.append(jax.ShapeDtypeStruct((items, rows, dim), bf))
        specs.append(per_item((rows, dim)))
    return pl.pallas_call(
        functools.partial(attend_kernel, first),
        grid_spec=pltpu.PrefetchScalarGridSpec(
            num_scalar_prefetch=1,
            grid=(items,),
            in_specs=[
                per_item(tokens.shape[1:]),
                full(small.shape),
                full(ws[0].shape),
                full(ws[0].shape),
                full(bs[0].shape),
                full(bs[0].shape),
            ],
            out_specs=specs,
        ),
        out_shape=outs,
        compiler_params=params(8),
        cost_estimate=lasting(TIMES["attend"]),
        name="attend",
    )(counts, tokens, small, *ws, *bs)


def branch_kernel(tokens, cot, mixed_a, mixed_b, w_a, w_b, small, middle_out, normed_out, cot_out):
    rows = normed_out.shape[0]
    middle = (
        pad_rows(tokens[...].astype(f32), rows)
        + (mul_nn(mixed_a[...], w_a[...]) + mul_nn(mixed_b[...], w_b[...]))
        + small[2:3]
    )
    middle_out[...] = middle
    unit, _ = unit_parts(middle)
    normed_out[...] = (unit * small[3:4] + small[4:5]).astype(bf)
    cot_out[...] = pad_rows(cot[...].astype(f32), rows).astype(bf)


def branch(tokens, cot, mixed_a, mixed_b, w_a, w_b, small):
    items, seq, dim = tokens.shape
    _, rows, width = mixed_a.shape
    return pl.pallas_call(
        branch_kernel,
        grid=(items,),
        in_specs=[per_item((seq, dim))] * 2
        + [per_item((rows, width))] * 2
        + [full(w_a.shape)] * 2
        + [full(small.shape)],
        out_specs=[per_item((rows, dim))] * 3,
        out_shape=[
            jax.ShapeDtypeStruct((items, rows, dim), f32),
            jax.ShapeDtypeStruct((items, rows, dim), bf),
            jax.ShapeDtypeStruct((items, rows, dim), bf),
        ],
        compiler_params=params(7),
        cost_estimate=lasting(TIMES["branch"]),
        name="branch",
    )(tokens, cot, mixed_a, mixed_b, w_a, w_b, small)


def feed_kernel(
    again, per, low_half, normed, cot, base_grad, *refs
):
    n_weights = 6 if again else 4
    weights, rest = refs[:n_weights], refs[n_weights:]
    bias_a, bias_b, grad_ref, hidden_ref, dup_a, dup_b, ddown_a, ddown_b, dbias_ref, gu_ref, ddown_all, dup_all = rest
    step = pl.program_id(0)
    items, rows, dim = normed.shape
    is_a = step < per

    @pl.when(step == 0)
    def _():
        grad_ref[...] = base_grad[...] if again else jnp.zeros_like(grad_ref)

    if again:
        up_a, up_b, up_c, up_d, down_a, down_c = weights
        is_low = low_half[0] == 0
        first = jnp.where(is_a, up_a[...], up_c[...])
        second = jnp.where(is_a, up_b[...], up_d[...])
        w_up = jnp.concatenate(
            [jnp.where(is_low, first, second), jnp.where(is_low, second, first)], axis=0
        )
    else:
        up_a, up_c, down_a, down_c = weights
        w_up = jnp.where(is_a, up_a[...], up_c[...])
    w_down = jnp.where(is_a, down_a[...], down_c[...])
    bias = jnp.where(is_a, bias_a[...].astype(f32), bias_b[...].astype(f32))
    def one_item(i, bias_sum):
        up = mul_nn(normed[i], w_up) + bias
        grad_hidden = mul_nt(cot[i], w_down)
        cdf = 0.5 * (1.0 + lax.erf(up * 0.7071067811865476))
        slope = cdf + up * (jnp.exp(-0.5 * up * up) * 0.3989422804014327)
        gu = (slope * grad_hidden).astype(bf)
        hidden_ref[i] = (up * cdf).astype(bf)
        gu_ref[i] = gu
        grad_ref[i] += mul_nt(gu, w_up)
        return bias_sum + col_sum(gu.astype(f32))

    bias_sum = lax.fori_loop(
        0, items, one_item, jnp.zeros((1, w_up.shape[1]), f32), unroll=bool(again)
    )
    dbias_ref[...] = bias_sum
    flat = items * rows

    def rows_of(n, carry):
        at = pl.ds(pl.multiple_of(n * CHUNK, CHUNK), CHUNK)
        take = lambda ref: ref[:, :, at].reshape(flat, CHUNK)
        ddown_all[at, :] = mul_tn(take(hidden_ref), cot[...].reshape(flat, dim)).astype(bf)
        dup_all[at, :] = mul_tn(take(normed), gu_ref[...].reshape(flat, -1)).astype(bf)
        return carry

    lax.fori_loop(0, dim // CHUNK, rows_of, 0)

    @pl.when(is_a)
    def _():
        ddown_a[...] = ddown_all[...]
        dup_a[...] = dup_all[...]

    @pl.when(jnp.logical_not(is_a))
    def _():
        ddown_b[...] = ddown_all[...]
        dup_b[...] = dup_all[...]


def feed(low_half, normed, cot, base_grad, ups, downs, biases):
    again = base_grad is not None
    items, rows, dim = normed.shape
    units = ups[0].shape[1]
    per = units // BLOCK
    steps = 2 * per
    full3 = full((items, rows, dim))
    if not again:
        base_grad = biases[0]
    half = len(ups) // 2
    first = lambda j: jnp.minimum(j, per - 1)
    second = lambda j: jnp.maximum(j - per, 0)
    across = lambda part, place: pl.BlockSpec((part, BLOCK), lambda j, *_: (0, place(j)))
    down = lambda place: pl.BlockSpec((BLOCK, dim), lambda j, *_: (place(j), 0))
    return pl.pallas_call(
        functools.partial(feed_kernel, again, per),
        grid_spec=pltpu.PrefetchScalarGridSpec(
            num_scalar_prefetch=1,
            grid=(steps,),
            in_specs=[full3, full3, full3 if again else full(base_grad.shape)]
            + [across(dim // half, first)] * half
            + [across(dim // half, second)] * half
            + [down(first), down(second)]
            + [across(1, first), across(1, second)],
            out_specs=[
                full3,
                pl.BlockSpec((items, rows, BLOCK), lambda j, *_: (0, 0, j)),
                across(dim, first),
                across(dim, second),
                down(first),
                down(second),
                pl.BlockSpec((1, BLOCK), lambda j, *_: (0, j)),
            ],
            scratch_shapes=[pltpu.VMEM((items, rows, BLOCK), bf)] + [pltpu.VMEM((dim, dim), bf)] * 2,
        ),
        out_shape=[
            jax.ShapeDtypeStruct((items, rows, dim), f32),
            later((items, rows, 2 * units), bf),
            jax.ShapeDtypeStruct((dim, units), bf),
            jax.ShapeDtypeStruct((dim, units), bf),
            jax.ShapeDtypeStruct((units, dim), bf),
            jax.ShapeDtypeStruct((units, dim), bf),
            jax.ShapeDtypeStruct((1, 2 * units), f32),
        ],
        compiler_params=params(36 if again else 24),
        cost_estimate=lasting(TIMES["feed"]),
        name="feed",
    )(low_half, *(map(in_hbm, (normed, cot, base_grad, *ups, *downs)) if again else (normed, cot, base_grad, *ups, *downs)), *biases)


def project_kernel(middle, small, hidden_a, hidden_b, *refs):
    weights, out_ref = refs[:4], refs[4]
    units = weights[0].shape[0]
    total = middle[...] + small[5:6]
    for n, w in enumerate(weights):
        hidden = (hidden_a, hidden_b)[n // 2]
        total = total + mul_nn(hidden[:, (n % 2) * units : (n % 2 + 1) * units], w[...])
    out_ref[...] = total[: out_ref.shape[0]]


def project(middle, small, hidden_a, hidden_b, weights, seq):
    items, rows, dim = middle.shape
    both = per_item(hidden_a.shape[1:])
    return pl.pallas_call(
        project_kernel,
        grid=(items,),
        in_specs=[per_item((rows, dim)), full(small.shape), both, both] + [full(weights[0].shape)] * 4,
        out_specs=per_item((seq, dim)),
        out_shape=jax.ShapeDtypeStruct((items, seq, dim), f32),
        compiler_params=params(14),
        cost_estimate=lasting(TIMES["project"]),
        name="project",
    )(middle, small, hidden_a, hidden_b, *weights)


def unbranch_kernel(
    middle, cot, grad_in, vectors, mixed_a, mixed_b, w_a, w_b,
    grad_out, gmix_a, gmix_b, dw_out, small, branch_ref
):
    step = pl.program_id(0)
    unit, inv = unit_parts(middle[...])
    grad = grad_in[...]
    cot_f = cot[...].astype(f32)
    grad_middle = cot_f + norm_back(grad, unit, inv, vectors[3:4])
    grad_out[...] = grad_middle
    grad_branch = grad_middle.astype(bf)
    branch_ref[step] = grad_branch
    gmix_a[...] = mul_nt(grad_branch, w_a[...]).astype(bf)
    gmix_b[...] = mul_nt(grad_branch, w_b[...]).astype(bf)

    @pl.when(step == 0)
    def _():
        small[...] = jnp.zeros_like(small)

    small[0:1] += col_sum(grad * unit)
    small[1:2] += col_sum(grad)
    small[2:3] += col_sum(grad_branch.astype(f32))
    small[3:4] += col_sum(cot_f)

    @pl.when(step == pl.num_programs(0) - 1)
    def _():
        items, rows, dim = branch_ref.shape
        gb = branch_ref[...].reshape(items * rows, dim)
        width = mixed_a.shape[2]
        quarter = width // 2
        for n, mixed in ((0, mixed_a), (1, mixed_b)):
            dw = mul_tn(mixed[...].reshape(items * rows, width), gb).astype(bf)
            dw_out[2 * n] = dw[:quarter]
            dw_out[2 * n + 1] = dw[quarter:]


def unbranch(middle, cot, grad_in, vectors, mixed_a, mixed_b, w_a, w_b):
    items, rows, dim = middle.shape
    width = mixed_a.shape[2]
    each = per_item((rows, dim))
    return pl.pallas_call(
        unbranch_kernel,
        grid=(items,),
        in_specs=[each, each, each, full(vectors.shape)]
        + [full(mixed_a.shape)] * 2
        + [full(w_a.shape)] * 2,
        out_specs=[
            each,
            per_item((rows, width)),
            per_item((rows, width)),
            full((4, width // 2, dim)),
            full((8, dim)),
        ],
        out_shape=[
            jax.ShapeDtypeStruct((items, rows, dim), f32),
            jax.ShapeDtypeStruct((items, rows, width), bf),
            jax.ShapeDtypeStruct((items, rows, width), bf),
            jax.ShapeDtypeStruct((4, width // 2, dim), bf),
            jax.ShapeDtypeStruct((8, dim), f32),
        ],
        scratch_shapes=[pltpu.VMEM((items, rows, dim), bf)],
        compiler_params=params(12),
        cost_estimate=lasting(TIMES["unbranch"]),
        name="unbranch",
    )(middle, cot, grad_in, vectors, mixed_a, mixed_b, w_a, w_b)


def unattend_kernel(counts, q, k, v, gmix, logs, normed, g_ref, dw_out, db_out):
    step = pl.program_id(0)
    rows, width = q.shape
    valid = WORDS + counts[step]
    mask = jnp.where(lax.broadcasted_iota(jnp.int32, (rows, 1), 0) < valid, 0.0, masked_value)
    low = lax.broadcasted_iota(jnp.int32, (rows, LANES), 1) < HEAD
    def one_pair(p, carry):
        at = pl.ds(pl.multiple_of(p * LANES, LANES), LANES)
        q_two, k_two, v_two, g_two = q[:, at], k[:, at], v[:, at], gmix[:, at]
        dq, dk, dv = [], [], []
        for h in range(2):
            here = low if h == 0 else ~low
            scores = mul_nt(jnp.where(here, k_two, 0), q_two) + mask
            prob = jnp.exp(scores - logs[pl.ds(2 * p + h, 1)])
            grad_prob = mul_nt(jnp.where(here, v_two, 0), g_two)
            inner = jnp.sum(grad_prob * prob, axis=0, keepdims=True)
            grad_scores = (prob * (grad_prob - inner)).astype(bf)
            dv.append(mul_nn(prob.astype(bf), g_two))
            dk.append(mul_nn(grad_scores, q_two))
            dq.append(mul_tn(grad_scores, k_two))
        for c, pair in enumerate((dq, dk, dv)):
            merged = jnp.where(low, pair[0], pair[1]).astype(bf)
            if c == 0:
                merged = merged * jnp.asarray(0.125, bf)
            g_ref[step, :, pl.ds(pl.multiple_of(c * width + p * LANES, LANES), LANES)] = merged
        return carry

    lax.fori_loop(0, width // LANES, one_pair, 0)

    @pl.when(step == 0)
    def _():
        db_out[...] = jnp.zeros_like(db_out)

    db_out[0:1] += col_sum(g_ref[step, :, :width].astype(f32))
    db_out[1:2] += col_sum(g_ref[step, :, 2 * width :].astype(f32))

    @pl.when(step == pl.num_programs(0) - 1)
    def _():
        items, _, dim = normed.shape
        flat = normed[...].reshape(items * rows, dim)
        quarter = width // 2
        def one_kind(c, carry):
            at = pl.ds(pl.multiple_of(c * width, LANES), width)
            dw = mul_tn(g_ref[:, :, at].reshape(items * rows, width), flat).astype(bf)
            dw_out[0, c] = dw[:quarter]
            dw_out[1, c] = dw[quarter:]
            return carry

        lax.fori_loop(0, 3, one_kind, 0)


def unattend(counts, q, k, v, gmix, logs, normed):
    items, rows, width = q.shape
    dim = normed.shape[2]
    return pl.pallas_call(
        unattend_kernel,
        grid_spec=pltpu.PrefetchScalarGridSpec(
            num_scalar_prefetch=1,
            grid=(items,),
            in_specs=[per_item((rows, width))] * 4 + [per_item((8, rows)), full(normed.shape)],
            out_specs=[
                full((items, rows, 3 * width)),
                full((2, 3, width // 2, dim)),
                full((8, width)),
            ],
        ),
        out_shape=[
            jax.ShapeDtypeStruct((items, rows, 3 * width), bf),
            jax.ShapeDtypeStruct((2, 3, width // 2, dim), bf),
            jax.ShapeDtypeStruct((8, width), f32),
        ],
        compiler_params=params(12),
        cost_estimate=lasting(TIMES["unattend"]),
        name="unattend",
    )(counts, q, k, v, gmix, logs, normed)


def unnorm_kernel(g_a, g_b, w_one, w_two, w_three, w_four, tokens, vectors, grad_middle, x_out, small):
    rows = g_a.shape[0]
    grad = 0.0
    for g, one, two in ((g_a, w_one, w_two), (g_b, w_three, w_four)):
        w = jnp.concatenate([two_rows(one, two, c) for c in range(3)], axis=0)
        grad = grad + mul_nn(g[...], w)
    unit, inv = unit_parts(pad_rows(tokens[...].astype(f32), rows))

    @pl.when(pl.program_id(0) == 0)
    def _():
        small[...] = jnp.zeros_like(small)

    small[0:1] += col_sum(grad * unit)
    small[1:2] += col_sum(grad)
    x_out[...] = (grad_middle[...] + norm_back(grad, unit, inv, vectors[0:1]))[: x_out.shape[0]]


def unnorm(g_a, g_b, ws, tokens, vectors, grad_middle):
    items, rows, width3 = g_a.shape
    seq, dim = tokens.shape[1:]
    return pl.pallas_call(
        unnorm_kernel,
        grid=(items,),
        in_specs=[per_item((rows, width3))] * 2
        + [full(ws[0].shape)] * 4
        + [per_item((seq, dim)), full(vectors.shape), per_item((rows, dim))],
        out_specs=[per_item((seq, dim)), full((8, dim))],
        out_shape=[
            jax.ShapeDtypeStruct((items, seq, dim), f32),
            jax.ShapeDtypeStruct((8, dim), f32),
        ],
        compiler_params=params(12),
        cost_estimate=lasting(TIMES["unnorm"]),
        name="unnorm",
    )(g_a, g_b, *ws, tokens, vectors, grad_middle)


def outer_kernel(g, normed, dw_out):
    items, rows, dim = normed.shape
    dw = mul_tn(g[...].reshape(items * rows, -1), normed[...].reshape(items * rows, dim)).astype(bf)
    quarter = dw.shape[0] // 2
    dw_out[0] = dw[:quarter]
    dw_out[1] = dw[quarter:]


def outer(g, normed):
    items, rows, width3 = g.shape
    dim = normed.shape[2]
    width = width3 // 3
    return pl.pallas_call(
        outer_kernel,
        grid=(3,),
        in_specs=[pl.BlockSpec((items, rows, width), lambda c: (0, 0, c)), full(normed.shape)],
        out_specs=pl.BlockSpec((2, None, width // 2, dim), lambda c: (0, c, 0, 0)),
        out_shape=jax.ShapeDtypeStruct((2, 3, width // 2, dim), bf),
        compiler_params=params(10),
        cost_estimate=lasting(TIMES["outer"]),
        name="outer",
    )(g, normed)


def exchange(x, axis, size, mask):
    return lax.ppermute(x, axis, [(i, i ^ mask) for i in range(size)])


def tie(*values):
    return lax.optimization_barrier(values)


def add_bf(*parts):
    total = parts[0].astype(f32)
    for part in parts[1:]:
        total = total + part.astype(f32)
    return total.astype(bf)


def piece(x, index, count):
    rows = x.shape[0] // count
    return lax.dynamic_slice_in_dim(x, index * rows, rows, 0)


class Wide:
    def __init__(self, size):
        self.size = size
        self.me = lax.axis_index("wide")
        self.groups = [(1, 2)]
        bit = 2
        while bit < size:
            self.groups.append((bit, min(4, size // bit)))
            bit *= self.groups[-1][1]

    def send(self, group, x):
        bit, members = group
        mine = (self.me // bit) % members
        got = [
            exchange(piece(x, mine ^ k, members), "wide", self.size, bit * k)
            for k in range(1, members)
        ]
        return [piece(x, mine, members)] + got

    def gathered(self, group, x):
        bit, members = group
        return [x] + [exchange(x, "wide", self.size, bit * k) for k in range(1, members)]

    def place(self, group, pieces):
        bit, members = group
        mine = (self.me // bit) % members
        if members == 2:
            low = mine == 0
            x, got = pieces
            return jnp.concatenate([jnp.where(low, x, got), jnp.where(low, got, x)], axis=0)
        x = pieces[0]
        rows = x.shape[0]
        out = jnp.zeros((members * rows,) + x.shape[1:], x.dtype)
        for k, part in enumerate(pieces):
            out = lax.dynamic_update_slice_in_dim(out, part, (mine ^ k) * rows, 0)
        return out

    def gather(self, group, x):
        return self.place(group, self.gathered(group, x))

    def over(self, groups, x):
        for group in groups:
            x = add_bf(*self.send(group, x))
        return x

    def back(self, groups, x):
        for group in reversed(groups):
            x = self.gather(group, x)
        return x


def on_device(
    wide,
    narrow,
    tokens,
    patch_counts,
    ln1_gain,
    ln1_bias,
    w_qkv,
    b_qv,
    w_out,
    b_out,
    ln2_gain,
    ln2_bias,
    w_up,
    b_up,
    w_down,
    b_down,
    cotangent,
):
    own_rows, dim = tokens.shape
    items = patch_counts.shape[0] // narrow
    seq = own_rows // items
    rows = -(-seq // PACK) * PACK
    heads = w_qkv.shape[2]
    units = w_up.shape[1]
    me = lax.axis_index("narrow")
    counts = lax.dynamic_slice_in_dim(patch_counts, me * items, items, 0)
    tokens3 = tokens.reshape(items, seq, dim)
    cot3 = cotangent.reshape(items, seq, dim)
    mate = lambda x: exchange(x, "narrow", narrow, 1)
    peer = lambda x: exchange(x, "narrow", narrow, 2)

    ring = Wide(wide)
    across = lambda x: exchange(x, "wide", wide, 1)
    x_axis, z_axis, more = ring.groups[0], ring.groups[1], ring.groups[2:]
    low_half = (ring.me % 2).astype(jnp.int32)
    half_dim = dim // 2

    w_own = w_qkv.transpose(1, 2, 0)
    w_peer, w_mate = peer(w_own), mate(w_own)
    b_peer, b_mate = peer(b_qv), mate(b_qv)
    vectors = jnp.concatenate([ln1_gain, ln1_bias, b_out, ln2_gain, ln2_bias, b_down]).reshape(6, dim)
    w_a = [w_own, w_mate]
    q_a, k_a, v_a, mixed_a, log_a, normed1 = attend(
        True, counts, tokens3, vectors, w_a, [b_qv, b_mate], rows
    )

    log_a, out_later, w_up, w_down, b_up = tie(log_a, w_out, w_up, w_down, b_up)
    out_peer, bias_peer = peer(out_later), peer(b_up)
    out_mate, bias_mate = mate(out_later), mate(b_up)
    up_mate, down_mate = mate(w_up), mate(w_down)
    up_part = lax.dynamic_slice_in_dim(w_up, low_half * half_dim, half_dim, 0)
    log_a, w_peer, b_peer, up_part = tie(log_a, w_peer, b_peer, up_part)
    up_first = peer(up_part)
    w_b = [w_peer, mate(w_peer)]
    q_b, k_b, v_b, mixed_b, log_b = attend(
        False, counts, tokens3, vectors, w_b, [b_peer, mate(b_peer)], rows
    )
    mixed_b, out_peer, up_first, bias_peer, down_later = tie(mixed_b, out_peer, up_first, bias_peer, w_down)
    bias_far = mate(bias_peer)
    down_peer = peer(down_later)
    out_a = jnp.concatenate([w_out, out_mate], axis=0)
    out_b = jnp.concatenate([out_peer, mate(out_peer)], axis=0)
    middle, normed2, cot_pad = branch(
        tokens3, cot3, mixed_a, mixed_b, out_a, out_b, vectors
    )
    middle, normed2, cot_pad, up_first = tie(middle, normed2, cot_pad, up_first)
    up_second, up_first_far = across(up_first), mate(up_first)
    flag = low_half.reshape(1)
    grad_part, hidden_a, dup_own, dup_mate, ddown_own, ddown_mate, dbias_a = feed(
        flag, normed2, cot_pad, None, [w_up, up_mate], [w_down, down_mate], [b_up, bias_mate]
    )

    grad_part, dup_own, dup_mate, ddown_own, ddown_mate, up_second, up_first_far = tie(
        grad_part, dup_own, dup_mate, ddown_own, ddown_mate, up_second, up_first_far
    )
    got_up, got_down = mate(dup_mate), mate(ddown_mate)
    up_second_far = mate(up_second)
    grad_part, down_peer = tie(grad_part, down_peer)
    ups = [up_first, up_second, up_first_far, up_second_far]
    downs = [down_peer, mate(down_peer)]
    grad_norm2, hidden_b, dup_peer, dup_far, ddown_peer, ddown_far, dbias_b = feed(
        flag, normed2, cot_pad, grad_part, ups, downs, [bias_peer, bias_far]
    )
    grad_norm2, dup_peer, dup_far, ddown_peer, ddown_far, got_up, got_down = tie(
        grad_norm2, dup_peer, dup_far, ddown_peer, ddown_far, got_up, got_down
    )
    far_up, far_down = mate(dup_far), mate(ddown_far)
    grad_middle, gmix_a, gmix_b, dw_out, small_two = unbranch(
        middle, cot_pad, grad_norm2, vectors, mixed_a, mixed_b, out_a, out_b
    )

    grad_middle, gmix_a, gmix_b, dw_out, small_two, far_up, far_down = tie(
        grad_middle, gmix_a, gmix_b, dw_out, small_two, far_up, far_down
    )
    top = lambda x: x[:half_dim]
    bottom = lambda x: x[half_dim:]
    up_one = peer(add_bf(top(dup_peer), top(far_up)))
    pair_keep, pair_got = ring.send(x_axis, add_bf(ddown_peer, far_down))
    out_far, out_near = mate(dw_out[3]), mate(dw_out[1])
    g_b, dqkv_b, dbqv_b = unattend(counts, q_b, k_b, v_b, gmix_b, log_b, normed1)
    g_b, dqkv_b, dbqv_b, up_one, pair_keep, pair_got, ddown_own, got_down, out_far, out_near, far_up, dup_peer = tie(
        g_b, dqkv_b, dbqv_b, up_one, pair_keep, pair_got, ddown_own, got_down, out_far, out_near, far_up, dup_peer
    )
    down_keep, down_got = ring.send(x_axis, add_bf(ddown_own, got_down))

    def block(n, dqkv, dbqv, dbias):
        at = n % 2
        tail = [
            small_two[0:4],
            dbias[:, at * units : (at + 1) * units],
            jnp.pad(dbqv[0:2, at * heads : (at + 1) * heads], ((0, 0), (0, dim - heads))),
        ]
        tail = jnp.concatenate(tail, axis=0)
        pad = -(3 * heads + tail.shape[0]) % (8 * wide)
        tail = jnp.pad(tail, ((0, pad), (0, 0))).astype(bf)
        return jnp.concatenate([dqkv[at].reshape(3 * heads, dim), tail], axis=0)

    far_rest = mate(block(3, dqkv_b, dbqv_b, dbias_b))
    pair_half = peer(add_bf(pair_keep, pair_got))
    one_keep, one_got = ring.send(x_axis, add_bf(top(dup_own), top(got_up), up_one))
    vectors_late, dbqv_b = tie(vectors, dbqv_b)
    layer_out = project(middle, vectors_late, hidden_a, hidden_b, [w_down, down_mate] + downs, seq)
    gmix_a, far_rest, pair_half, layer_out, down_keep, down_got = tie(
        gmix_a, far_rest, pair_half, layer_out, down_keep, down_got
    )
    two_got = peer(
        jnp.concatenate([add_bf(bottom(dup_peer), bottom(far_up)), add_bf(dw_out[2], out_far)], axis=0)
    )
    rest_keep, rest_got = ring.send(x_axis, add_bf(block(2, dqkv_b, dbqv_b, dbias_b), far_rest))
    down_parts = ring.send(z_axis, add_bf(down_keep, down_got, pair_half))
    g_a, dqkv_a, dbqv_a = unattend(counts, q_a, k_a, v_a, gmix_a, log_a, normed1)
    g_a, dqkv_a, dbqv_a, rest_keep, rest_got, one_keep, one_got, two_got, *down_parts = tie(
        g_a, dqkv_a, dbqv_a, rest_keep, rest_got, one_keep, one_got, two_got, *down_parts
    )

    rest_mate = mate(block(1, dqkv_a, dbqv_a, dbias_a))
    rest_half = peer(add_bf(rest_keep, rest_got))
    two_own = jnp.concatenate([add_bf(bottom(dup_own), bottom(got_up)), add_bf(dw_out[0], out_near)], axis=0)
    two_keep, two_got = ring.send(x_axis, add_bf(two_own, two_got))
    down_all = ring.gathered(z_axis, ring.back(more, ring.over(more, add_bf(*down_parts))))
    rest_own = add_bf(block(0, dqkv_a, dbqv_a, dbias_a), rest_mate)
    rest_own, g_a = tie(rest_own, g_a)
    rest_keep, rest_got = ring.send(x_axis, rest_own)
    input_grad, small_one = unnorm(g_a, g_b, w_a + w_b, tokens3, vectors, grad_middle)
    small_one, rest_keep, rest_got, rest_half, two_keep, two_got, *down_all = tie(
        small_one, rest_keep, rest_got, rest_half, two_keep, two_got, *down_all
    )
    down_sum = ring.place(z_axis, down_all)
    firsts = small_one[0:2]
    firsts = firsts + mate(firsts)
    firsts = firsts + peer(firsts)
    firsts = firsts + across(firsts)
    up_half = jnp.concatenate([add_bf(one_keep, one_got), add_bf(two_keep, two_got)], axis=0)
    rest_sum = add_bf(rest_keep, rest_got, rest_half)
    spot = lax.broadcasted_iota(jnp.int32, (rest_sum.shape[0], 1), 0) - (
        3 * heads + 7 - low_half * rest_sum.shape[0]
    )
    whole = firsts.astype(bf)
    rest_sum = jnp.where(spot == 0, whole[0:1], jnp.where(spot == 1, whole[1:2], rest_sum))
    rest_sum = ring.back(ring.groups, ring.over(ring.groups[1:], rest_sum))
    up_sum = ring.back(ring.groups, ring.over(ring.groups[1:], up_half))
    down_sum = ring.back([x_axis], down_sum)
    quarter = half_dim // 2
    parts = [up_sum[: up_sum.shape[0] // 2], up_sum[up_sum.shape[0] // 2 :]]
    up_sum = jnp.concatenate([x[:quarter] for x in parts] + [x[quarter:] for x in parts], axis=0)
    firsts = rest_sum[3 * heads + 7 : 3 * heads + 9].astype(f32)
    up_grad, out_grad = up_sum[:dim], up_sum[dim:]
    vec = rest_sum[3 * heads :].astype(f32)
    return (
        layer_out.reshape(own_rows, dim),
        input_grad.reshape(own_rows, dim),
        firsts[0],
        firsts[1],
        rest_sum[: 3 * heads].astype(f32).reshape(3, heads, dim).transpose(2, 0, 1),
        vec[5:7, :heads],
        out_grad.astype(f32),
        vec[2],
        vec[0],
        vec[1],
        up_grad.astype(f32),
        vec[4:5, :units],
        down_sum.astype(f32),
        vec[3],
    )


def solution(mesh):
    wide, narrow = mesh.shape["wide"], mesh.shape["narrow"]
    assert narrow == 4 and wide >= 4 and wide & (wide - 1) == 0
    rows = P(("wide", "narrow"), None)
    return jax.shard_map(
        functools.partial(on_device, wide, narrow),
        mesh=mesh,
        in_specs=(
            rows,
            P("wide"),
            P(),
            P(),
            P(None, None, "narrow"),
            P(None, "narrow"),
            P("narrow", None),
            P(),
            P(),
            P(),
            P(None, "narrow"),
            P(None, "narrow"),
            P("narrow", None),
            P(),
            rows,
        ),
        out_specs=(
            rows,
            rows,
            P(),
            P(),
            P(None, None, "narrow"),
            P(None, "narrow"),
            P("narrow", None),
            P(),
            P(),
            P(),
            P(None, "narrow"),
            P(None, "narrow"),
            P("narrow", None),
            P(),
        ),
        check_vma=False,
    )
```

```python
import functools

import jax
import jax.numpy as jnp
from jax import lax
from jax.experimental import pallas as pl
from jax.experimental.pallas import tpu as pltpu
from jax.sharding import PartitionSpec as P

HEAD = 64
WORDS = 40
PACK = 16
LANES = 128
BLOCK = 768
CHUNK = 256

norm_eps = 1e-06
masked_value = -1000000000.0
bf = jnp.bfloat16
f32 = jnp.float32


def mul_nn(a, b):
    return lax.dot_general(a, b, (((1,), (0,)), ((), ())), preferred_element_type=f32)


def mul_nt(a, b):
    return lax.dot_general(a, b, (((1,), (1,)), ((), ())), preferred_element_type=f32)


def mul_tn(a, b):
    return lax.dot_general(a, b, (((0,), (0,)), ((), ())), preferred_element_type=f32)


def pad_rows(x, rows):
    if x.shape[0] == rows:
        return x
    return jnp.concatenate([x, jnp.zeros((rows - x.shape[0],) + x.shape[1:], x.dtype)], axis=0)


def unit_parts(x):
    centred = x - jnp.mean(x, axis=-1, keepdims=True)
    inv = lax.rsqrt(jnp.mean(centred * centred, axis=-1, keepdims=True) + norm_eps)
    return centred * inv, inv


def norm_back(grad, unit, inv, gain):
    scaled = grad * gain
    inner = (
        scaled
        - jnp.mean(scaled, axis=-1, keepdims=True)
        - unit * jnp.mean(scaled * unit, axis=-1, keepdims=True)
    )
    return inv * inner


def col_sum(x):
    return jnp.sum(x, axis=0, keepdims=True)


def full(shape):
    return pl.BlockSpec(shape, lambda *_: (0,) * len(shape))


def per_item(shape):
    return pl.BlockSpec((None,) + shape, lambda i, *_: (i,) + (0,) * len(shape))


TIMES = {
    "attend": 30,
    "branch": 0.01,
    "feed": 54,
    "project": 18,
    "unbranch": 18,
    "unattend": 33,
    "unnorm": 18,
}


def lasting(us):
    return pl.CostEstimate(flops=int(us * 1.15e9), bytes_accessed=0, transcendentals=0)


def later(shape, dtype):
    return pltpu.HBM(shape, dtype)


def in_hbm(x):
    return pltpu.with_memory_space_constraint(x, pltpu.HBM)


def params(mib):
    return pltpu.CompilerParams(vmem_limit_bytes=mib << 20)


def two_rows(w_one, w_two, c):
    return jnp.concatenate([w_one[c], w_two[c]], axis=0)


def attend_kernel(first, counts, tokens, small, w_one, w_two, b_one, b_two, *outs):
    if first:
        q_out, k_out, v_out, mixed_out, log_out, normed_out = outs
    else:
        q_out, k_out, v_out, mixed_out, log_out = outs
    rows, width = q_out.shape
    unit, _ = unit_parts(pad_rows(tokens[...].astype(f32), rows))
    normed = (unit * small[0:1] + small[1:2]).astype(bf)
    b = jnp.concatenate([b_one[...], b_two[...]], axis=1)
    if first:
        normed_out[...] = normed
    q = ((mul_nt(normed, two_rows(w_one, w_two, 0)) + b[0:1]) * 0.125).astype(bf)
    k = mul_nt(normed, two_rows(w_one, w_two, 1)).astype(bf)
    v = (mul_nt(normed, two_rows(w_one, w_two, 2)) + b[1:2]).astype(bf)
    q_out[...] = q
    k_out[...] = k
    v_out[...] = v
    valid = WORDS + counts[pl.program_id(0)]
    mask = jnp.where(lax.broadcasted_iota(jnp.int32, (1, rows), 1) < valid, 0.0, masked_value)
    lane = lax.broadcasted_iota(jnp.int32, (rows, LANES), 1)
    low = lane < HEAD
    logs = jnp.zeros((rows, LANES), f32)
    for p in range(width // LANES):
        at = slice(p * LANES, (p + 1) * LANES)
        q_two, k_two, v_two = q[:, at], k[:, at], v[:, at]
        tops, sums = [], []
        for h in range(2):
            here = low if h == 0 else ~low
            scores = mul_nt(jnp.where(here, q_two, 0), k_two) + mask
            top = jnp.max(scores, axis=1, keepdims=True)
            shifted = jnp.exp(scores - top).astype(bf)
            sums.append(mul_nn(shifted, jnp.where(here, v_two, 1)))
            tops.append(top)
        total = pltpu.roll(jnp.where(low, sums[1], sums[0]), HEAD, 1)
        mixed_out[:, at] = (jnp.where(low, sums[0], sums[1]) / total).astype(bf)
        log_two = jnp.log(total)
        logs = jnp.where(lane == 2 * p, tops[0] + log_two[:, 0:1], logs)
        logs = jnp.where(lane == 2 * p + 1, tops[1] + log_two[:, HEAD : HEAD + 1], logs)
    log_out[...] = logs.T[: log_out.shape[0]]


def attend(first, counts, tokens, small, ws, bs, rows):
    items, _, dim = tokens.shape
    width = 2 * ws[0].shape[1]
    outs = [later((items, rows, width), bf)] * 3 + [
        jax.ShapeDtypeStruct((items, rows, width), bf),
        later((items, 8, rows), f32),
    ]
    specs = [per_item((rows, width))] * 4 + [per_item((8, rows))]
    if first:
        outs.append(later((items, rows, dim), bf))
        specs.append(per_item((rows, dim)))
    return pl.pallas_call(
        functools.partial(attend_kernel, first),
        grid_spec=pltpu.PrefetchScalarGridSpec(
            num_scalar_prefetch=1,
            grid=(items,),
            in_specs=[
                per_item(tokens.shape[1:]),
                full(small.shape),
                full(ws[0].shape),
                full(ws[0].shape),
                full(bs[0].shape),
                full(bs[0].shape),
            ],
            out_specs=specs,
        ),
        out_shape=outs,
        compiler_params=params(8),
        cost_estimate=lasting(TIMES["attend"]),
        name="attend",
    )(counts, tokens, small, *ws, *bs)


def branch_kernel(tokens, cot, mixed_a, mixed_b, w_a, w_b, small, middle_out, normed_out, cot_out):
    rows = normed_out.shape[0]
    middle = (
        pad_rows(tokens[...].astype(f32), rows)
        + (mul_nn(mixed_a[...], w_a[...]) + mul_nn(mixed_b[...], w_b[...]))
        + small[2:3]
    )
    middle_out[...] = middle
    unit, _ = unit_parts(middle)
    normed_out[...] = (unit * small[3:4] + small[4:5]).astype(bf)
    cot_out[...] = pad_rows(cot[...].astype(f32), rows).astype(bf)


def branch(tokens, cot, mixed_a, mixed_b, w_a, w_b, small):
    items, seq, dim = tokens.shape
    _, rows, width = mixed_a.shape
    return pl.pallas_call(
        branch_kernel,
        grid=(items,),
        in_specs=[per_item((seq, dim))] * 2
        + [per_item((rows, width))] * 2
        + [full(w_a.shape)] * 2
        + [full(small.shape)],
        out_specs=[per_item((rows, dim))] * 3,
        out_shape=[
            later((items, rows, dim), f32),
            jax.ShapeDtypeStruct((items, rows, dim), bf),
            jax.ShapeDtypeStruct((items, rows, dim), bf),
        ],
        compiler_params=params(7),
        cost_estimate=lasting(TIMES["branch"]),
        name="branch",
    )(tokens, cot, mixed_a, mixed_b, w_a, w_b, small)


def feed_kernel(
    again, per, low_half, normed, cot, base_grad, *refs
):
    n_weights = 6 if again else 4
    weights, rest = refs[:n_weights], refs[n_weights:]
    bias_a, bias_b, grad_ref, hidden_ref, dup_a, dup_b, ddown_a, ddown_b, dbias_ref, gu_ref, ddown_all, dup_all = rest
    step = pl.program_id(0)
    items, rows, dim = normed.shape
    is_a = step < per

    @pl.when(step == 0)
    def _():
        grad_ref[...] = base_grad[...] if again else jnp.zeros_like(grad_ref)

    if again:
        up_a, up_b, up_c, up_d, down_a, down_c = weights
        is_low = low_half[0] == 0
        first = jnp.where(is_a, up_a[...], up_c[...])
        second = jnp.where(is_a, up_b[...], up_d[...])
        w_up = jnp.concatenate(
            [jnp.where(is_low, first, second), jnp.where(is_low, second, first)], axis=0
        )
    else:
        up_a, up_c, down_a, down_c = weights
        w_up = jnp.where(is_a, up_a[...], up_c[...])
    w_down = jnp.where(is_a, down_a[...], down_c[...])
    bias = jnp.where(is_a, bias_a[...].astype(f32), bias_b[...].astype(f32))
    def one_item(i, bias_sum):
        up = mul_nn(normed[i], w_up) + bias
        grad_hidden = mul_nt(cot[i], w_down)
        cdf = 0.5 * (1.0 + lax.erf(up * 0.7071067811865476))
        slope = cdf + up * (jnp.exp(-0.5 * up * up) * 0.3989422804014327)
        gu = (slope * grad_hidden).astype(bf)
        hidden_ref[i] = (up * cdf).astype(bf)
        gu_ref[i] = gu
        grad_ref[i] += mul_nt(gu, w_up)
        return bias_sum + col_sum(gu.astype(f32))

    bias_sum = lax.fori_loop(
        0, items, one_item, jnp.zeros((1, w_up.shape[1]), f32), unroll=bool(again)
    )
    dbias_ref[...] = bias_sum
    flat = items * rows

    def rows_of(n, carry):
        at = pl.ds(pl.multiple_of(n * CHUNK, CHUNK), CHUNK)
        take = lambda ref: ref[:, :, at].reshape(flat, CHUNK)
        ddown_all[at, :] = mul_tn(take(hidden_ref), cot[...].reshape(flat, dim)).astype(bf)
        dup_all[at, :] = mul_tn(take(normed), gu_ref[...].reshape(flat, -1)).astype(bf)
        return carry

    lax.fori_loop(0, dim // CHUNK, rows_of, 0)

    @pl.when(is_a)
    def _():
        ddown_a[...] = ddown_all[...]
        dup_a[...] = dup_all[...]

    @pl.when(jnp.logical_not(is_a))
    def _():
        ddown_b[...] = ddown_all[...]
        dup_b[...] = dup_all[...]


def feed(low_half, normed, cot, base_grad, ups, downs, biases):
    again = base_grad is not None
    items, rows, dim = normed.shape
    units = ups[0].shape[1]
    per = units // BLOCK
    steps = 2 * per
    full3 = full((items, rows, dim))
    if not again:
        base_grad = biases[0]
    half = len(ups) // 2
    first = lambda j: jnp.minimum(j, per - 1)
    second = lambda j: jnp.maximum(j - per, 0)
    across = lambda part, place: pl.BlockSpec((part, BLOCK), lambda j, *_: (0, place(j)))
    down = lambda place: pl.BlockSpec((BLOCK, dim), lambda j, *_: (place(j), 0))
    return pl.pallas_call(
        functools.partial(feed_kernel, again, per),
        grid_spec=pltpu.PrefetchScalarGridSpec(
            num_scalar_prefetch=1,
            grid=(steps,),
            in_specs=[full3, full3, full3 if again else full(base_grad.shape)]
            + [across(dim // half, first)] * half
            + [across(dim // half, second)] * half
            + [down(first), down(second)]
            + [across(1, first), across(1, second)],
            out_specs=[
                full3,
                pl.BlockSpec((items, rows, BLOCK), lambda j, *_: (0, 0, j)),
                across(dim, first),
                across(dim, second),
                down(first),
                down(second),
                pl.BlockSpec((1, BLOCK), lambda j, *_: (0, j)),
            ],
            scratch_shapes=[pltpu.VMEM((items, rows, BLOCK), bf)] + [pltpu.VMEM((dim, dim), bf)] * 2,
        ),
        out_shape=[
            jax.ShapeDtypeStruct((items, rows, dim), f32),
            later((items, rows, 2 * units), bf),
            jax.ShapeDtypeStruct((dim, units), bf),
            jax.ShapeDtypeStruct((dim, units), bf),
            jax.ShapeDtypeStruct((units, dim), bf),
            jax.ShapeDtypeStruct((units, dim), bf),
            jax.ShapeDtypeStruct((1, 2 * units), f32),
        ],
        compiler_params=params(36 if again else 24),
        cost_estimate=lasting(TIMES["feed"]),
        name="feed",
    )(low_half, *(map(in_hbm, (normed, cot, base_grad, *ups, *downs)) if again else (normed, cot, base_grad, *ups, *downs)), *biases)


def project_kernel(middle, small, hidden_a, hidden_b, *refs):
    weights, out_ref = refs[:4], refs[4]
    units = weights[0].shape[0]
    total = middle[...] + small[5:6]
    for n, w in enumerate(weights):
        hidden = (hidden_a, hidden_b)[n // 2]
        total = total + mul_nn(hidden[:, (n % 2) * units : (n % 2 + 1) * units], w[...])
    out_ref[...] = total[: out_ref.shape[0]]


def project(middle, small, hidden_a, hidden_b, weights, seq):
    items, rows, dim = middle.shape
    both = per_item(hidden_a.shape[1:])
    return pl.pallas_call(
        project_kernel,
        grid=(items,),
        in_specs=[per_item((rows, dim)), full(small.shape), both, both] + [full(weights[0].shape)] * 4,
        out_specs=per_item((seq, dim)),
        out_shape=jax.ShapeDtypeStruct((items, seq, dim), f32),
        compiler_params=params(14),
        cost_estimate=lasting(TIMES["project"]),
        name="project",
    )(middle, small, hidden_a, hidden_b, *weights)


def unbranch_kernel(
    middle, cot, grad_in, vectors, mixed_a, mixed_b, w_a, w_b,
    grad_out, gmix_a, gmix_b, dw_out, small, branch_ref
):
    step = pl.program_id(0)
    unit, inv = unit_parts(middle[...])
    grad = grad_in[...]
    cot_f = cot[...].astype(f32)
    grad_middle = cot_f + norm_back(grad, unit, inv, vectors[3:4])
    grad_out[...] = grad_middle
    grad_branch = grad_middle.astype(bf)
    branch_ref[step] = grad_branch
    gmix_a[...] = mul_nt(grad_branch, w_a[...]).astype(bf)
    gmix_b[...] = mul_nt(grad_branch, w_b[...]).astype(bf)

    @pl.when(step == 0)
    def _():
        small[...] = jnp.zeros_like(small)

    small[0:1] += col_sum(grad * unit)
    small[1:2] += col_sum(grad)
    small[2:3] += col_sum(grad_branch.astype(f32))
    small[3:4] += col_sum(cot_f)

    @pl.when(step == pl.num_programs(0) - 1)
    def _():
        items, rows, dim = branch_ref.shape
        gb = branch_ref[...].reshape(items * rows, dim)
        width = mixed_a.shape[2]
        quarter = width // 2
        for n, mixed in ((0, mixed_a), (1, mixed_b)):
            dw = mul_tn(mixed[...].reshape(items * rows, width), gb).astype(bf)
            dw_out[2 * n] = dw[:quarter]
            dw_out[2 * n + 1] = dw[quarter:]


def unbranch(middle, cot, grad_in, vectors, mixed_a, mixed_b, w_a, w_b):
    items, rows, dim = middle.shape
    width = mixed_a.shape[2]
    each = per_item((rows, dim))
    return pl.pallas_call(
        unbranch_kernel,
        grid=(items,),
        in_specs=[each, each, each, full(vectors.shape)]
        + [full(mixed_a.shape)] * 2
        + [full(w_a.shape)] * 2,
        out_specs=[
            each,
            per_item((rows, width)),
            per_item((rows, width)),
            full((4, width // 2, dim)),
            full((8, dim)),
        ],
        out_shape=[
            jax.ShapeDtypeStruct((items, rows, dim), f32),
            jax.ShapeDtypeStruct((items, rows, width), bf),
            jax.ShapeDtypeStruct((items, rows, width), bf),
            jax.ShapeDtypeStruct((4, width // 2, dim), bf),
            jax.ShapeDtypeStruct((8, dim), f32),
        ],
        scratch_shapes=[pltpu.VMEM((items, rows, dim), bf)],
        compiler_params=params(12),
        cost_estimate=lasting(TIMES["unbranch"]),
        name="unbranch",
    )(middle, cot, grad_in, vectors, mixed_a, mixed_b, w_a, w_b)


def unattend_kernel(counts, q, k, v, gmix, logs, normed, g_ref, dw_out, db_out):
    step = pl.program_id(0)
    rows, width = q.shape
    valid = WORDS + counts[step]
    mask = jnp.where(lax.broadcasted_iota(jnp.int32, (rows, 1), 0) < valid, 0.0, masked_value)
    low = lax.broadcasted_iota(jnp.int32, (rows, LANES), 1) < HEAD
    def one_pair(p, carry):
        at = pl.ds(pl.multiple_of(p * LANES, LANES), LANES)
        q_two, k_two, v_two, g_two = q[:, at], k[:, at], v[:, at], gmix[:, at]
        dq, dk, dv = [], [], []
        for h in range(2):
            here = low if h == 0 else ~low
            scores = mul_nt(jnp.where(here, k_two, 0), q_two) + mask
            prob = jnp.exp(scores - logs[pl.ds(2 * p + h, 1)])
            grad_prob = mul_nt(jnp.where(here, v_two, 0), g_two)
            inner = jnp.sum(grad_prob * prob, axis=0, keepdims=True)
            grad_scores = (prob * (grad_prob - inner)).astype(bf)
            dv.append(mul_nn(prob.astype(bf), g_two))
            dk.append(mul_nn(grad_scores, q_two))
            dq.append(mul_tn(grad_scores, k_two))
        for c, pair in enumerate((dq, dk, dv)):
            merged = jnp.where(low, pair[0], pair[1]).astype(bf)
            if c == 0:
                merged = merged * jnp.asarray(0.125, bf)
            g_ref[step, :, pl.ds(pl.multiple_of(c * width + p * LANES, LANES), LANES)] = merged
        return carry

    lax.fori_loop(0, width // LANES, one_pair, 0)

    @pl.when(step == 0)
    def _():
        db_out[...] = jnp.zeros_like(db_out)

    db_out[0:1] += col_sum(g_ref[step, :, :width].astype(f32))
    db_out[1:2] += col_sum(g_ref[step, :, 2 * width :].astype(f32))

    @pl.when(step == pl.num_programs(0) - 1)
    def _():
        items, _, dim = normed.shape
        flat = normed[...].reshape(items * rows, dim)
        quarter = width // 2
        def one_kind(c, carry):
            at = pl.ds(pl.multiple_of(c * width, LANES), width)
            dw = mul_tn(g_ref[:, :, at].reshape(items * rows, width), flat).astype(bf)
            dw_out[0, c] = dw[:quarter]
            dw_out[1, c] = dw[quarter:]
            return carry

        lax.fori_loop(0, 3, one_kind, 0)


def unattend(counts, q, k, v, gmix, logs, normed):
    items, rows, width = q.shape
    dim = normed.shape[2]
    return pl.pallas_call(
        unattend_kernel,
        grid_spec=pltpu.PrefetchScalarGridSpec(
            num_scalar_prefetch=1,
            grid=(items,),
            in_specs=[per_item((rows, width))] * 4 + [per_item((8, rows)), full(normed.shape)],
            out_specs=[
                full((items, rows, 3 * width)),
                full((2, 3, width // 2, dim)),
                full((8, width)),
            ],
        ),
        out_shape=[
            jax.ShapeDtypeStruct((items, rows, 3 * width), bf),
            jax.ShapeDtypeStruct((2, 3, width // 2, dim), bf),
            jax.ShapeDtypeStruct((8, width), f32),
        ],
        compiler_params=params(12),
        cost_estimate=lasting(TIMES["unattend"]),
        name="unattend",
    )(counts, q, k, v, gmix, logs, normed)


def unnorm_kernel(g_a, g_b, w_one, w_two, w_three, w_four, tokens, vectors, grad_middle, x_out, small):
    rows = g_a.shape[0]
    grad = 0.0
    for g, one, two in ((g_a, w_one, w_two), (g_b, w_three, w_four)):
        w = jnp.concatenate([two_rows(one, two, c) for c in range(3)], axis=0)
        grad = grad + mul_nn(g[...], w)
    unit, inv = unit_parts(pad_rows(tokens[...].astype(f32), rows))

    @pl.when(pl.program_id(0) == 0)
    def _():
        small[...] = jnp.zeros_like(small)

    small[0:1] += col_sum(grad * unit)
    small[1:2] += col_sum(grad)
    x_out[...] = (grad_middle[...] + norm_back(grad, unit, inv, vectors[0:1]))[: x_out.shape[0]]


def unnorm(g_a, g_b, ws, tokens, vectors, grad_middle):
    items, rows, width3 = g_a.shape
    seq, dim = tokens.shape[1:]
    return pl.pallas_call(
        unnorm_kernel,
        grid=(items,),
        in_specs=[per_item((rows, width3))] * 2
        + [full(ws[0].shape)] * 4
        + [per_item((seq, dim)), full(vectors.shape), per_item((rows, dim))],
        out_specs=[per_item((seq, dim)), full((8, dim))],
        out_shape=[
            jax.ShapeDtypeStruct((items, seq, dim), f32),
            jax.ShapeDtypeStruct((8, dim), f32),
        ],
        compiler_params=params(12),
        cost_estimate=lasting(TIMES["unnorm"]),
        name="unnorm",
    )(g_a, g_b, *ws, tokens, vectors, grad_middle)


def outer_kernel(g, normed, dw_out):
    items, rows, dim = normed.shape
    dw = mul_tn(g[...].reshape(items * rows, -1), normed[...].reshape(items * rows, dim)).astype(bf)
    quarter = dw.shape[0] // 2
    dw_out[0] = dw[:quarter]
    dw_out[1] = dw[quarter:]


def outer(g, normed):
    items, rows, width3 = g.shape
    dim = normed.shape[2]
    width = width3 // 3
    return pl.pallas_call(
        outer_kernel,
        grid=(3,),
        in_specs=[pl.BlockSpec((items, rows, width), lambda c: (0, 0, c)), full(normed.shape)],
        out_specs=pl.BlockSpec((2, None, width // 2, dim), lambda c: (0, c, 0, 0)),
        out_shape=jax.ShapeDtypeStruct((2, 3, width // 2, dim), bf),
        compiler_params=params(10),
        cost_estimate=lasting(TIMES["outer"]),
        name="outer",
    )(g, normed)


def exchange(x, axis, size, mask):
    return lax.ppermute(x, axis, [(i, i ^ mask) for i in range(size)])


def tie(*values):
    return lax.optimization_barrier(values)


def add_bf(*parts):
    total = parts[0].astype(f32)
    for part in parts[1:]:
        total = total + part.astype(f32)
    return total.astype(bf)


def piece(x, index, count):
    rows = x.shape[0] // count
    return lax.dynamic_slice_in_dim(x, index * rows, rows, 0)


class Wide:
    def __init__(self, size):
        self.size = size
        self.me = lax.axis_index("wide")
        self.groups = [(1, 2)]
        bit = 2
        while bit < size:
            self.groups.append((bit, min(4, size // bit)))
            bit *= self.groups[-1][1]

    def send(self, group, x):
        bit, members = group
        mine = (self.me // bit) % members
        got = [
            exchange(piece(x, mine ^ k, members), "wide", self.size, bit * k)
            for k in range(1, members)
        ]
        return [piece(x, mine, members)] + got

    def gathered(self, group, x):
        bit, members = group
        return [x] + [exchange(x, "wide", self.size, bit * k) for k in range(1, members)]

    def place(self, group, pieces):
        bit, members = group
        mine = (self.me // bit) % members
        if members == 2:
            low = mine == 0
            x, got = pieces
            return jnp.concatenate([jnp.where(low, x, got), jnp.where(low, got, x)], axis=0)
        x = pieces[0]
        rows = x.shape[0]
        out = jnp.zeros((members * rows,) + x.shape[1:], x.dtype)
        for k, part in enumerate(pieces):
            out = lax.dynamic_update_slice_in_dim(out, part, (mine ^ k) * rows, 0)
        return out

    def gather(self, group, x):
        return self.place(group, self.gathered(group, x))

    def over(self, groups, x):
        for group in groups:
            x = add_bf(*self.send(group, x))
        return x

    def back(self, groups, x):
        for group in reversed(groups):
            x = self.gather(group, x)
        return x


def on_device(
    wide,
    narrow,
    tokens,
    patch_counts,
    ln1_gain,
    ln1_bias,
    w_qkv,
    b_qv,
    w_out,
    b_out,
    ln2_gain,
    ln2_bias,
    w_up,
    b_up,
    w_down,
    b_down,
    cotangent,
):
    own_rows, dim = tokens.shape
    items = patch_counts.shape[0] // narrow
    seq = own_rows // items
    rows = -(-seq // PACK) * PACK
    heads = w_qkv.shape[2]
    units = w_up.shape[1]
    me = lax.axis_index("narrow")
    counts = lax.dynamic_slice_in_dim(patch_counts, me * items, items, 0)
    tokens3 = tokens.reshape(items, seq, dim)
    cot3 = cotangent.reshape(items, seq, dim)
    mate = lambda x: exchange(x, "narrow", narrow, 1)
    peer = lambda x: exchange(x, "narrow", narrow, 2)

    ring = Wide(wide)
    across = lambda x: exchange(x, "wide", wide, 1)
    x_axis, z_axis, more = ring.groups[0], ring.groups[1], ring.groups[2:]
    low_half = (ring.me % 2).astype(jnp.int32)
    half_dim = dim // 2

    w_own = w_qkv.transpose(1, 2, 0)
    w_peer, w_mate = peer(w_own), mate(w_own)
    b_peer, b_mate = peer(b_qv), mate(b_qv)
    vectors = jnp.concatenate([ln1_gain, ln1_bias, b_out, ln2_gain, ln2_bias, b_down]).reshape(6, dim)
    w_a = [w_own, w_mate]
    q_a, k_a, v_a, mixed_a, log_a, normed1 = attend(
        True, counts, tokens3, vectors, w_a, [b_qv, b_mate], rows
    )

    log_a, out_later, w_up, w_down, b_up = tie(log_a, w_out, w_up, w_down, b_up)
    out_peer, bias_peer = peer(out_later), peer(b_up)
    out_mate, bias_mate = mate(out_later), mate(b_up)
    up_mate, down_mate = mate(w_up), mate(w_down)
    up_part = lax.dynamic_slice_in_dim(w_up, low_half * half_dim, half_dim, 0)
    log_a, w_peer, b_peer, up_part = tie(log_a, w_peer, b_peer, up_part)
    up_first = peer(up_part)
    w_b = [w_peer, mate(w_peer)]
    q_b, k_b, v_b, mixed_b, log_b = attend(
        False, counts, tokens3, vectors, w_b, [b_peer, mate(b_peer)], rows
    )
    mixed_b, out_peer, bias_peer, down_later = tie(mixed_b, out_peer, bias_peer, w_down)
    bias_far = mate(bias_peer)
    down_peer = peer(down_later)
    out_a = jnp.concatenate([w_out, out_mate], axis=0)
    out_b = jnp.concatenate([out_peer, mate(out_peer)], axis=0)
    middle, normed2, cot_pad = branch(
        tokens3, cot3, mixed_a, mixed_b, out_a, out_b, vectors
    )
    middle, normed2, cot_pad, up_first = tie(middle, normed2, cot_pad, up_first)
    up_second, up_first_far = across(up_first), mate(up_first)
    flag = low_half.reshape(1)
    grad_part, hidden_a, dup_own, dup_mate, ddown_own, ddown_mate, dbias_a = feed(
        flag, normed2, cot_pad, None, [w_up, up_mate], [w_down, down_mate], [b_up, bias_mate]
    )

    grad_part, dup_own, dup_mate, ddown_own, ddown_mate, up_second, up_first_far = tie(
        grad_part, dup_own, dup_mate, ddown_own, ddown_mate, up_second, up_first_far
    )
    got_up, got_down = mate(dup_mate), mate(ddown_mate)
    up_second_far = mate(up_second)
    grad_part, down_peer = tie(grad_part, down_peer)
    ups = [up_first, up_second, up_first_far, up_second_far]
    downs = [down_peer, mate(down_peer)]
    grad_norm2, hidden_b, dup_peer, dup_far, ddown_peer, ddown_far, dbias_b = feed(
        flag, normed2, cot_pad, grad_part, ups, downs, [bias_peer, bias_far]
    )
    grad_norm2, dup_peer, dup_far, ddown_peer, ddown_far, got_up, got_down = tie(
        grad_norm2, dup_peer, dup_far, ddown_peer, ddown_far, got_up, got_down
    )
    far_up, far_down = mate(dup_far), mate(ddown_far)
    grad_middle, gmix_a, gmix_b, dw_out, small_two = unbranch(
        middle, cot_pad, grad_norm2, vectors, mixed_a, mixed_b, out_a, out_b
    )

    grad_middle, gmix_a, gmix_b, dw_out, small_two, far_up, far_down = tie(
        grad_middle, gmix_a, gmix_b, dw_out, small_two, far_up, far_down
    )
    top = lambda x: x[:half_dim]
    bottom = lambda x: x[half_dim:]
    up_one = peer(add_bf(top(dup_peer), top(far_up)))
    pair_keep, pair_got = ring.send(x_axis, add_bf(ddown_peer, far_down))
    out_far, out_near = mate(dw_out[3]), mate(dw_out[1])
    g_b, dqkv_b, dbqv_b = unattend(counts, q_b, k_b, v_b, gmix_b, log_b, normed1)
    g_b, dqkv_b, dbqv_b, up_one, pair_keep, pair_got, ddown_own, got_down, out_far, out_near, far_up, dup_peer = tie(
        g_b, dqkv_b, dbqv_b, up_one, pair_keep, pair_got, ddown_own, got_down, out_far, out_near, far_up, dup_peer
    )
    down_keep, down_got = ring.send(x_axis, add_bf(ddown_own, got_down))

    def block(n, dqkv, dbqv, dbias):
        at = n % 2
        tail = [
            small_two[0:4],
            dbias[:, at * units : (at + 1) * units],
            jnp.pad(dbqv[0:2, at * heads : (at + 1) * heads], ((0, 0), (0, dim - heads))),
        ]
        tail = jnp.concatenate(tail, axis=0)
        pad = -(3 * heads + tail.shape[0]) % (8 * wide)
        tail = jnp.pad(tail, ((0, pad), (0, 0))).astype(bf)
        return jnp.concatenate([dqkv[at].reshape(3 * heads, dim), tail], axis=0)

    far_rest = mate(block(3, dqkv_b, dbqv_b, dbias_b))
    pair_half = peer(add_bf(pair_keep, pair_got))
    one_keep, one_got = ring.send(x_axis, add_bf(top(dup_own), top(got_up), up_one))
    vectors_late, dbqv_b = tie(vectors, dbqv_b)
    layer_out = project(middle, vectors_late, hidden_a, hidden_b, [w_down, down_mate] + downs, seq)
    gmix_a, far_rest, pair_half, layer_out, down_keep, down_got = tie(
        gmix_a, far_rest, pair_half, layer_out, down_keep, down_got
    )
    two_got = peer(
        jnp.concatenate([add_bf(bottom(dup_peer), bottom(far_up)), add_bf(dw_out[2], out_far)], axis=0)
    )
    rest_keep, rest_got = ring.send(x_axis, add_bf(block(2, dqkv_b, dbqv_b, dbias_b), far_rest))
    down_parts = ring.send(z_axis, add_bf(down_keep, down_got, pair_half))
    g_a, dqkv_a, dbqv_a = unattend(counts, q_a, k_a, v_a, gmix_a, log_a, normed1)
    g_a, dqkv_a, dbqv_a, rest_keep, rest_got, one_keep, one_got, two_got, *down_parts = tie(
        g_a, dqkv_a, dbqv_a, rest_keep, rest_got, one_keep, one_got, two_got, *down_parts
    )

    rest_mate = mate(block(1, dqkv_a, dbqv_a, dbias_a))
    rest_half = peer(add_bf(rest_keep, rest_got))
    two_own = jnp.concatenate([add_bf(bottom(dup_own), bottom(got_up)), add_bf(dw_out[0], out_near)], axis=0)
    two_keep, two_got = ring.send(x_axis, add_bf(two_own, two_got))
    down_all = ring.gathered(z_axis, ring.back(more, ring.over(more, add_bf(*down_parts))))
    rest_own = add_bf(block(0, dqkv_a, dbqv_a, dbias_a), rest_mate)
    rest_own, g_a = tie(rest_own, g_a)
    rest_keep, rest_got = ring.send(x_axis, rest_own)
    input_grad, small_one = unnorm(g_a, g_b, w_a + w_b, tokens3, vectors, grad_middle)
    small_one, rest_keep, rest_got, rest_half, two_keep, two_got, *down_all = tie(
        small_one, rest_keep, rest_got, rest_half, two_keep, two_got, *down_all
    )
    down_sum = ring.place(z_axis, down_all)
    firsts = small_one[0:2]
    firsts = firsts + mate(firsts)
    firsts = firsts + peer(firsts)
    firsts = firsts + across(firsts)
    up_half = jnp.concatenate([add_bf(one_keep, one_got), add_bf(two_keep, two_got)], axis=0)
    rest_sum = add_bf(rest_keep, rest_got, rest_half)
    spot = lax.broadcasted_iota(jnp.int32, (rest_sum.shape[0], 1), 0) - (
        3 * heads + 7 - low_half * rest_sum.shape[0]
    )
    whole = firsts.astype(bf)
    rest_sum = jnp.where(spot == 0, whole[0:1], jnp.where(spot == 1, whole[1:2], rest_sum))
    rest_sum = ring.back(ring.groups, ring.over(ring.groups[1:], rest_sum))
    up_sum = ring.back(ring.groups, ring.over(ring.groups[1:], up_half))
    down_sum = ring.back([x_axis], down_sum)
    quarter = half_dim // 2
    parts = [up_sum[: up_sum.shape[0] // 2], up_sum[up_sum.shape[0] // 2 :]]
    up_sum = jnp.concatenate([x[:quarter] for x in parts] + [x[quarter:] for x in parts], axis=0)
    firsts = rest_sum[3 * heads + 7 : 3 * heads + 9].astype(f32)
    up_grad, out_grad = up_sum[:dim], up_sum[dim:]
    vec = rest_sum[3 * heads :].astype(f32)
    return (
        layer_out.reshape(own_rows, dim),
        input_grad.reshape(own_rows, dim),
        firsts[0],
        firsts[1],
        rest_sum[: 3 * heads].astype(f32).reshape(3, heads, dim).transpose(2, 0, 1),
        vec[5:7, :heads],
        out_grad.astype(f32),
        vec[2],
        vec[0],
        vec[1],
        up_grad.astype(f32),
        vec[4:5, :units],
        down_sum.astype(f32),
        vec[3],
    )


def solution(mesh):
    wide, narrow = mesh.shape["wide"], mesh.shape["narrow"]
    assert narrow == 4 and wide >= 4 and wide & (wide - 1) == 0
    rows = P(("wide", "narrow"), None)
    return jax.shard_map(
        functools.partial(on_device, wide, narrow),
        mesh=mesh,
        in_specs=(
            rows,
            P("wide"),
            P(),
            P(),
            P(None, None, "narrow"),
            P(None, "narrow"),
            P("narrow", None),
            P(),
            P(),
            P(),
            P(None, "narrow"),
            P(None, "narrow"),
            P("narrow", None),
            P(),
            rows,
        ),
        out_specs=(
            rows,
            rows,
            P(),
            P(),
            P(None, None, "narrow"),
            P(None, "narrow"),
            P("narrow", None),
            P(),
            P(),
            P(),
            P(None, "narrow"),
            P(None, "narrow"),
            P("narrow", None),
            P(),
        ),
        check_vma=False,
    )
```

```python
import functools

import jax
import jax.numpy as jnp
from jax import lax
from jax.experimental import pallas as pl
from jax.experimental.pallas import tpu as pltpu
from jax.sharding import PartitionSpec as P

HEAD = 64
WORDS = 40
PACK = 16
LANES = 128
BLOCK = 768
CHUNK = 256

norm_eps = 1e-06
masked_value = -1000000000.0
bf = jnp.bfloat16
f32 = jnp.float32


def mul_nn(a, b):
    return lax.dot_general(a, b, (((1,), (0,)), ((), ())), preferred_element_type=f32)


def mul_nt(a, b):
    return lax.dot_general(a, b, (((1,), (1,)), ((), ())), preferred_element_type=f32)


def mul_tn(a, b):
    return lax.dot_general(a, b, (((0,), (0,)), ((), ())), preferred_element_type=f32)


def pad_rows(x, rows):
    if x.shape[0] == rows:
        return x
    return jnp.concatenate([x, jnp.zeros((rows - x.shape[0],) + x.shape[1:], x.dtype)], axis=0)


def unit_parts(x):
    centred = x - jnp.mean(x, axis=-1, keepdims=True)
    inv = lax.rsqrt(jnp.mean(centred * centred, axis=-1, keepdims=True) + norm_eps)
    return centred * inv, inv


def norm_back(grad, unit, inv, gain):
    scaled = grad * gain
    inner = (
        scaled
        - jnp.mean(scaled, axis=-1, keepdims=True)
        - unit * jnp.mean(scaled * unit, axis=-1, keepdims=True)
    )
    return inv * inner


def col_sum(x):
    return jnp.sum(x, axis=0, keepdims=True)


def full(shape):
    return pl.BlockSpec(shape, lambda *_: (0,) * len(shape))


def per_item(shape):
    return pl.BlockSpec((None,) + shape, lambda i, *_: (i,) + (0,) * len(shape))


TIMES = {
    "attend": 30,
    "branch": 0.01,
    "feed": 54,
    "project": 18,
    "unbranch": 18,
    "unattend": 33,
    "unnorm": 18,
}


def lasting(us):
    return pl.CostEstimate(flops=int(us * 1.15e9), bytes_accessed=0, transcendentals=0)


def later(shape, dtype):
    return pltpu.HBM(shape, dtype)


def in_hbm(x):
    return pltpu.with_memory_space_constraint(x, pltpu.HBM)


def params(mib):
    return pltpu.CompilerParams(vmem_limit_bytes=mib << 20)


def two_rows(w_one, w_two, c):
    return jnp.concatenate([w_one[c], w_two[c]], axis=0)


def attend_kernel(first, counts, tokens, small, w_one, w_two, b_one, b_two, *outs):
    if first:
        q_out, k_out, v_out, mixed_out, log_out, normed_out = outs
    else:
        q_out, k_out, v_out, mixed_out, log_out = outs
    rows, width = q_out.shape
    unit, _ = unit_parts(pad_rows(tokens[...].astype(f32), rows))
    normed = (unit * small[0:1] + small[1:2]).astype(bf)
    b = jnp.concatenate([b_one[...], b_two[...]], axis=1)
    if first:
        normed_out[...] = normed
    q = ((mul_nt(normed, two_rows(w_one, w_two, 0)) + b[0:1]) * 0.125).astype(bf)
    k = mul_nt(normed, two_rows(w_one, w_two, 1)).astype(bf)
    v = (mul_nt(normed, two_rows(w_one, w_two, 2)) + b[1:2]).astype(bf)
    q_out[...] = q
    k_out[...] = k
    v_out[...] = v
    valid = WORDS + counts[pl.program_id(0)]
    mask = jnp.where(lax.broadcasted_iota(jnp.int32, (1, rows), 1) < valid, 0.0, masked_value)
    lane = lax.broadcasted_iota(jnp.int32, (rows, LANES), 1)
    low = lane < HEAD
    logs = jnp.zeros((rows, LANES), f32)
    for p in range(width // LANES):
        at = slice(p * LANES, (p + 1) * LANES)
        q_two, k_two, v_two = q[:, at], k[:, at], v[:, at]
        tops, sums = [], []
        for h in range(2):
            here = low if h == 0 else ~low
            scores = mul_nt(jnp.where(here, q_two, 0), k_two) + mask
            top = jnp.max(scores, axis=1, keepdims=True)
            shifted = jnp.exp(scores - top).astype(bf)
            sums.append(mul_nn(shifted, jnp.where(here, v_two, 1)))
            tops.append(top)
        total = pltpu.roll(jnp.where(low, sums[1], sums[0]), HEAD, 1)
        mixed_out[:, at] = (jnp.where(low, sums[0], sums[1]) / total).astype(bf)
        log_two = jnp.log(total)
        logs = jnp.where(lane == 2 * p, tops[0] + log_two[:, 0:1], logs)
        logs = jnp.where(lane == 2 * p + 1, tops[1] + log_two[:, HEAD : HEAD + 1], logs)
    log_out[...] = logs.T[: log_out.shape[0]]


def attend(first, counts, tokens, small, ws, bs, rows):
    items, _, dim = tokens.shape
    width = 2 * ws[0].shape[1]
    outs = [later((items, rows, width), bf)] * 3 + [
        jax.ShapeDtypeStruct((items, rows, width), bf),
        later((items, 8, rows), f32),
    ]
    specs = [per_item((rows, width))] * 4 + [per_item((8, rows))]
    if first:
        outs.append(later((items, rows, dim), bf))
        specs.append(per_item((rows, dim)))
    return pl.pallas_call(
        functools.partial(attend_kernel, first),
        grid_spec=pltpu.PrefetchScalarGridSpec(
            num_scalar_prefetch=1,
            grid=(items,),
            in_specs=[
                per_item(tokens.shape[1:]),
                full(small.shape),
                full(ws[0].shape),
                full(ws[0].shape),
                full(bs[0].shape),
                full(bs[0].shape),
            ],
            out_specs=specs,
        ),
        out_shape=outs,
        compiler_params=params(8),
        cost_estimate=lasting(TIMES["attend"]),
        name="attend",
    )(counts, tokens, small, *ws, *bs)


def branch_kernel(tokens, cot, mixed_a, mixed_b, w_a, w_b, small, middle_out, normed_out, cot_out):
    rows = normed_out.shape[0]
    middle = (
        pad_rows(tokens[...].astype(f32), rows)
        + (mul_nn(mixed_a[...], w_a[...]) + mul_nn(mixed_b[...], w_b[...]))
        + small[2:3]
    )
    middle_out[...] = middle
    unit, _ = unit_parts(middle)
    normed_out[...] = (unit * small[3:4] + small[4:5]).astype(bf)
    cot_out[...] = pad_rows(cot[...].astype(f32), rows).astype(bf)


def branch(tokens, cot, mixed_a, mixed_b, w_a, w_b, small):
    items, seq, dim = tokens.shape
    _, rows, width = mixed_a.shape
    return pl.pallas_call(
        branch_kernel,
        grid=(items,),
        in_specs=[per_item((seq, dim))] * 2
        + [per_item((rows, width))] * 2
        + [full(w_a.shape)] * 2
        + [full(small.shape)],
        out_specs=[per_item((rows, dim))] * 3,
        out_shape=[
            later((items, rows, dim), f32),
            jax.ShapeDtypeStruct((items, rows, dim), bf),
            jax.ShapeDtypeStruct((items, rows, dim), bf),
        ],
        compiler_params=params(7),
        cost_estimate=lasting(TIMES["branch"]),
        name="branch",
    )(tokens, cot, mixed_a, mixed_b, w_a, w_b, small)


def feed_kernel(
    again, per, low_half, normed, cot, base_grad, *refs
):
    n_weights = 6 if again else 4
    weights, rest = refs[:n_weights], refs[n_weights:]
    bias_a, bias_b, grad_ref, hidden_ref, dup_a, dup_b, ddown_a, ddown_b, dbias_ref, gu_ref, ddown_all, dup_all = rest
    step = pl.program_id(0)
    items, rows, dim = normed.shape
    is_a = step < per

    @pl.when(step == 0)
    def _():
        grad_ref[...] = base_grad[...] if again else jnp.zeros_like(grad_ref)

    if again:
        up_a, up_b, up_c, up_d, down_a, down_c = weights
        is_low = low_half[0] == 0
        first = jnp.where(is_a, up_a[...], up_c[...])
        second = jnp.where(is_a, up_b[...], up_d[...])
        w_up = jnp.concatenate(
            [jnp.where(is_low, first, second), jnp.where(is_low, second, first)], axis=0
        )
    else:
        up_a, up_c, down_a, down_c = weights
        w_up = jnp.where(is_a, up_a[...], up_c[...])
    w_down = jnp.where(is_a, down_a[...], down_c[...])
    bias = jnp.where(is_a, bias_a[...].astype(f32), bias_b[...].astype(f32))
    def one_item(i, bias_sum):
        up = mul_nn(normed[i], w_up) + bias
        grad_hidden = mul_nt(cot[i], w_down)
        cdf = 0.5 * (1.0 + lax.erf(up * 0.7071067811865476))
        slope = cdf + up * (jnp.exp(-0.5 * up * up) * 0.3989422804014327)
        gu = (slope * grad_hidden).astype(bf)
        hidden_ref[i] = (up * cdf).astype(bf)
        gu_ref[i] = gu
        grad_ref[i] += mul_nt(gu, w_up)
        return bias_sum + col_sum(gu.astype(f32))

    bias_sum = lax.fori_loop(
        0, items, one_item, jnp.zeros((1, w_up.shape[1]), f32), unroll=bool(again)
    )
    dbias_ref[...] = bias_sum
    flat = items * rows

    def rows_of(n, carry):
        at = pl.ds(pl.multiple_of(n * CHUNK, CHUNK), CHUNK)
        take = lambda ref: ref[:, :, at].reshape(flat, CHUNK)
        ddown_all[at, :] = mul_tn(take(hidden_ref), cot[...].reshape(flat, dim)).astype(bf)
        dup_all[at, :] = mul_tn(take(normed), gu_ref[...].reshape(flat, -1)).astype(bf)
        return carry

    lax.fori_loop(0, dim // CHUNK, rows_of, 0)

    @pl.when(is_a)
    def _():
        ddown_a[...] = ddown_all[...]
        dup_a[...] = dup_all[...]

    @pl.when(jnp.logical_not(is_a))
    def _():
        ddown_b[...] = ddown_all[...]
        dup_b[...] = dup_all[...]


def feed(low_half, normed, cot, base_grad, ups, downs, biases):
    again = base_grad is not None
    items, rows, dim = normed.shape
    units = ups[0].shape[1]
    per = units // BLOCK
    steps = 2 * per
    full3 = full((items, rows, dim))
    if not again:
        base_grad = biases[0]
    half = len(ups) // 2
    first = lambda j: jnp.minimum(j, per - 1)
    second = lambda j: jnp.maximum(j - per, 0)
    across = lambda part, place: pl.BlockSpec((part, BLOCK), lambda j, *_: (0, place(j)))
    down = lambda place: pl.BlockSpec((BLOCK, dim), lambda j, *_: (place(j), 0))
    return pl.pallas_call(
        functools.partial(feed_kernel, again, per),
        grid_spec=pltpu.PrefetchScalarGridSpec(
            num_scalar_prefetch=1,
            grid=(steps,),
            in_specs=[full3, full3, full3 if again else full(base_grad.shape)]
            + [across(dim // half, first)] * half
            + [across(dim // half, second)] * half
            + [down(first), down(second)]
            + [across(1, first), across(1, second)],
            out_specs=[
                full3,
                pl.BlockSpec((items, rows, BLOCK), lambda j, *_: (0, 0, j)),
                across(dim, first),
                across(dim, second),
                down(first),
                down(second),
                pl.BlockSpec((1, BLOCK), lambda j, *_: (0, j)),
            ],
            scratch_shapes=[pltpu.VMEM((items, rows, BLOCK), bf)] + [pltpu.VMEM((dim, dim), bf)] * 2,
        ),
        out_shape=[
            jax.ShapeDtypeStruct((items, rows, dim), f32),
            later((items, rows, 2 * units), bf),
            jax.ShapeDtypeStruct((dim, units), bf),
            jax.ShapeDtypeStruct((dim, units), bf),
            jax.ShapeDtypeStruct((units, dim), bf),
            jax.ShapeDtypeStruct((units, dim), bf),
            jax.ShapeDtypeStruct((1, 2 * units), f32),
        ],
        compiler_params=params(36 if again else 24),
        cost_estimate=lasting(TIMES["feed"]),
        name="feed",
    )(low_half, *(map(in_hbm, (normed, cot, base_grad, *ups, *downs)) if again else (normed, cot, base_grad, *ups, *downs)), *biases)


def project_kernel(middle, small, hidden_a, hidden_b, *refs):
    weights, out_ref = refs[:4], refs[4]
    units = weights[0].shape[0]
    total = middle[...] + small[5:6]
    for n, w in enumerate(weights):
        hidden = (hidden_a, hidden_b)[n // 2]
        total = total + mul_nn(hidden[:, (n % 2) * units : (n % 2 + 1) * units], w[...])
    out_ref[...] = total[: out_ref.shape[0]]


def project(middle, small, hidden_a, hidden_b, weights, seq):
    items, rows, dim = middle.shape
    both = per_item(hidden_a.shape[1:])
    return pl.pallas_call(
        project_kernel,
        grid=(items,),
        in_specs=[per_item((rows, dim)), full(small.shape), both, both] + [full(weights[0].shape)] * 4,
        out_specs=per_item((seq, dim)),
        out_shape=jax.ShapeDtypeStruct((items, seq, dim), f32),
        compiler_params=params(14),
        cost_estimate=lasting(TIMES["project"]),
        name="project",
    )(middle, small, hidden_a, hidden_b, *weights)


def unbranch_kernel(
    middle, cot, grad_in, vectors, mixed_a, mixed_b, w_a, w_b,
    grad_out, gmix_a, gmix_b, dw_out, small, branch_ref
):
    step = pl.program_id(0)
    unit, inv = unit_parts(middle[...])
    grad = grad_in[...]
    cot_f = cot[...].astype(f32)
    grad_middle = cot_f + norm_back(grad, unit, inv, vectors[3:4])
    grad_out[...] = grad_middle
    grad_branch = grad_middle.astype(bf)
    branch_ref[step] = grad_branch
    gmix_a[...] = mul_nt(grad_branch, w_a[...]).astype(bf)
    gmix_b[...] = mul_nt(grad_branch, w_b[...]).astype(bf)

    @pl.when(step == 0)
    def _():
        small[...] = jnp.zeros_like(small)

    small[0:1] += col_sum(grad * unit)
    small[1:2] += col_sum(grad)
    small[2:3] += col_sum(grad_branch.astype(f32))
    small[3:4] += col_sum(cot_f)

    @pl.when(step == pl.num_programs(0) - 1)
    def _():
        items, rows, dim = branch_ref.shape
        gb = branch_ref[...].reshape(items * rows, dim)
        width = mixed_a.shape[2]
        quarter = width // 2
        for n, mixed in ((0, mixed_a), (1, mixed_b)):
            dw = mul_tn(mixed[...].reshape(items * rows, width), gb).astype(bf)
            dw_out[2 * n] = dw[:quarter]
            dw_out[2 * n + 1] = dw[quarter:]


def unbranch(middle, cot, grad_in, vectors, mixed_a, mixed_b, w_a, w_b):
    items, rows, dim = middle.shape
    width = mixed_a.shape[2]
    each = per_item((rows, dim))
    return pl.pallas_call(
        unbranch_kernel,
        grid=(items,),
        in_specs=[each, each, each, full(vectors.shape)]
        + [full(mixed_a.shape)] * 2
        + [full(w_a.shape)] * 2,
        out_specs=[
            each,
            per_item((rows, width)),
            per_item((rows, width)),
            full((4, width // 2, dim)),
            full((8, dim)),
        ],
        out_shape=[
            jax.ShapeDtypeStruct((items, rows, dim), f32),
            jax.ShapeDtypeStruct((items, rows, width), bf),
            jax.ShapeDtypeStruct((items, rows, width), bf),
            jax.ShapeDtypeStruct((4, width // 2, dim), bf),
            jax.ShapeDtypeStruct((8, dim), f32),
        ],
        scratch_shapes=[pltpu.VMEM((items, rows, dim), bf)],
        compiler_params=params(12),
        cost_estimate=lasting(TIMES["unbranch"]),
        name="unbranch",
    )(middle, cot, grad_in, vectors, mixed_a, mixed_b, w_a, w_b)


def unattend_kernel(unroll, counts, q, k, v, gmix, logs, normed, g_ref, dw_out, db_out):
    step = pl.program_id(0)
    rows, width = q.shape
    valid = WORDS + counts[step]
    mask = jnp.where(lax.broadcasted_iota(jnp.int32, (rows, 1), 0) < valid, 0.0, masked_value)
    low = lax.broadcasted_iota(jnp.int32, (rows, LANES), 1) < HEAD
    def one_pair(p, carry):
        at = pl.ds(pl.multiple_of(p * LANES, LANES), LANES)
        q_two, k_two, v_two, g_two = q[:, at], k[:, at], v[:, at], gmix[:, at]
        dq, dk, dv = [], [], []
        for h in range(2):
            here = low if h == 0 else ~low
            scores = mul_nt(jnp.where(here, k_two, 0), q_two) + mask
            prob = jnp.exp(scores - logs[pl.ds(2 * p + h, 1)])
            grad_prob = mul_nt(jnp.where(here, v_two, 0), g_two)
            inner = jnp.sum(grad_prob * prob, axis=0, keepdims=True)
            grad_scores = (prob * (grad_prob - inner)).astype(bf)
            dv.append(mul_nn(prob.astype(bf), g_two))
            dk.append(mul_nn(grad_scores, q_two))
            dq.append(mul_tn(grad_scores, k_two))
        for c, pair in enumerate((dq, dk, dv)):
            merged = jnp.where(low, pair[0], pair[1]).astype(bf)
            if c == 0:
                merged = merged * jnp.asarray(0.125, bf)
            g_ref[step, :, pl.ds(pl.multiple_of(c * width + p * LANES, LANES), LANES)] = merged
        return carry

    lax.fori_loop(0, width // LANES, one_pair, 0, unroll=unroll)

    @pl.when(step == 0)
    def _():
        db_out[...] = jnp.zeros_like(db_out)

    db_out[0:1] += col_sum(g_ref[step, :, :width].astype(f32))
    db_out[1:2] += col_sum(g_ref[step, :, 2 * width :].astype(f32))

    @pl.when(step == pl.num_programs(0) - 1)
    def _():
        items, _, dim = normed.shape
        flat = normed[...].reshape(items * rows, dim)
        quarter = width // 2
        def one_kind(c, carry):
            at = pl.ds(pl.multiple_of(c * width, LANES), width)
            dw = mul_tn(g_ref[:, :, at].reshape(items * rows, width), flat).astype(bf)
            dw_out[0, c] = dw[:quarter]
            dw_out[1, c] = dw[quarter:]
            return carry

        lax.fori_loop(0, 3, one_kind, 0)


def unattend(unroll, counts, q, k, v, gmix, logs, normed):
    items, rows, width = q.shape
    dim = normed.shape[2]
    return pl.pallas_call(
        functools.partial(unattend_kernel, unroll),
        grid_spec=pltpu.PrefetchScalarGridSpec(
            num_scalar_prefetch=1,
            grid=(items,),
            in_specs=[per_item((rows, width))] * 4 + [per_item((8, rows)), full(normed.shape)],
            out_specs=[
                full((items, rows, 3 * width)),
                full((2, 3, width // 2, dim)),
                full((8, width)),
            ],
        ),
        out_shape=[
            jax.ShapeDtypeStruct((items, rows, 3 * width), bf),
            jax.ShapeDtypeStruct((2, 3, width // 2, dim), bf),
            jax.ShapeDtypeStruct((8, width), f32),
        ],
        compiler_params=params(12),
        cost_estimate=lasting(TIMES["unattend"]),
        name="unattend",
    )(counts, q, k, v, gmix, logs, normed)


def unnorm_kernel(g_a, g_b, w_one, w_two, w_three, w_four, tokens, vectors, grad_middle, x_out, small):
    rows = g_a.shape[0]
    grad = 0.0
    for g, one, two in ((g_a, w_one, w_two), (g_b, w_three, w_four)):
        w = jnp.concatenate([two_rows(one, two, c) for c in range(3)], axis=0)
        grad = grad + mul_nn(g[...], w)
    unit, inv = unit_parts(pad_rows(tokens[...].astype(f32), rows))

    @pl.when(pl.program_id(0) == 0)
    def _():
        small[...] = jnp.zeros_like(small)

    small[0:1] += col_sum(grad * unit)
    small[1:2] += col_sum(grad)
    x_out[...] = (grad_middle[...] + norm_back(grad, unit, inv, vectors[0:1]))[: x_out.shape[0]]


def unnorm(g_a, g_b, ws, tokens, vectors, grad_middle):
    items, rows, width3 = g_a.shape
    seq, dim = tokens.shape[1:]
    return pl.pallas_call(
        unnorm_kernel,
        grid=(items,),
        in_specs=[per_item((rows, width3))] * 2
        + [full(ws[0].shape)] * 4
        + [per_item((seq, dim)), full(vectors.shape), per_item((rows, dim))],
        out_specs=[per_item((seq, dim)), full((8, dim))],
        out_shape=[
            jax.ShapeDtypeStruct((items, seq, dim), f32),
            jax.ShapeDtypeStruct((8, dim), f32),
        ],
        compiler_params=params(12),
        cost_estimate=lasting(TIMES["unnorm"]),
        name="unnorm",
    )(g_a, g_b, *ws, tokens, vectors, grad_middle)


def outer_kernel(g, normed, dw_out):
    items, rows, dim = normed.shape
    dw = mul_tn(g[...].reshape(items * rows, -1), normed[...].reshape(items * rows, dim)).astype(bf)
    quarter = dw.shape[0] // 2
    dw_out[0] = dw[:quarter]
    dw_out[1] = dw[quarter:]


def outer(g, normed):
    items, rows, width3 = g.shape
    dim = normed.shape[2]
    width = width3 // 3
    return pl.pallas_call(
        outer_kernel,
        grid=(3,),
        in_specs=[pl.BlockSpec((items, rows, width), lambda c: (0, 0, c)), full(normed.shape)],
        out_specs=pl.BlockSpec((2, None, width // 2, dim), lambda c: (0, c, 0, 0)),
        out_shape=jax.ShapeDtypeStruct((2, 3, width // 2, dim), bf),
        compiler_params=params(10),
        cost_estimate=lasting(TIMES["outer"]),
        name="outer",
    )(g, normed)


def exchange(x, axis, size, mask):
    return lax.ppermute(x, axis, [(i, i ^ mask) for i in range(size)])


def tie(*values):
    return lax.optimization_barrier(values)


def add_bf(*parts):
    total = parts[0].astype(f32)
    for part in parts[1:]:
        total = total + part.astype(f32)
    return total.astype(bf)


def piece(x, index, count):
    rows = x.shape[0] // count
    return lax.dynamic_slice_in_dim(x, index * rows, rows, 0)


class Wide:
    def __init__(self, size):
        self.size = size
        self.me = lax.axis_index("wide")
        self.groups = [(1, 2)]
        bit = 2
        while bit < size:
            self.groups.append((bit, min(4, size // bit)))
            bit *= self.groups[-1][1]

    def send(self, group, x):
        bit, members = group
        mine = (self.me // bit) % members
        got = [
            exchange(piece(x, mine ^ k, members), "wide", self.size, bit * k)
            for k in range(1, members)
        ]
        return [piece(x, mine, members)] + got

    def gathered(self, group, x):
        bit, members = group
        return [x] + [exchange(x, "wide", self.size, bit * k) for k in range(1, members)]

    def place(self, group, pieces):
        bit, members = group
        mine = (self.me // bit) % members
        if members == 2:
            low = mine == 0
            x, got = pieces
            return jnp.concatenate([jnp.where(low, x, got), jnp.where(low, got, x)], axis=0)
        x = pieces[0]
        rows = x.shape[0]
        out = jnp.zeros((members * rows,) + x.shape[1:], x.dtype)
        for k, part in enumerate(pieces):
            out = lax.dynamic_update_slice_in_dim(out, part, (mine ^ k) * rows, 0)
        return out

    def gather(self, group, x):
        return self.place(group, self.gathered(group, x))

    def over(self, groups, x):
        for group in groups:
            x = add_bf(*self.send(group, x))
        return x

    def back(self, groups, x):
        for group in reversed(groups):
            x = self.gather(group, x)
        return x


def on_device(
    wide,
    narrow,
    tokens,
    patch_counts,
    ln1_gain,
    ln1_bias,
    w_qkv,
    b_qv,
    w_out,
    b_out,
    ln2_gain,
    ln2_bias,
    w_up,
    b_up,
    w_down,
    b_down,
    cotangent,
):
    own_rows, dim = tokens.shape
    items = patch_counts.shape[0] // narrow
    seq = own_rows // items
    rows = -(-seq // PACK) * PACK
    heads = w_qkv.shape[2]
    units = w_up.shape[1]
    me = lax.axis_index("narrow")
    counts = lax.dynamic_slice_in_dim(patch_counts, me * items, items, 0)
    tokens3 = tokens.reshape(items, seq, dim)
    cot3 = cotangent.reshape(items, seq, dim)
    mate = lambda x: exchange(x, "narrow", narrow, 1)
    peer = lambda x: exchange(x, "narrow", narrow, 2)

    ring = Wide(wide)
    across = lambda x: exchange(x, "wide", wide, 1)
    x_axis, z_axis, more = ring.groups[0], ring.groups[1], ring.groups[2:]
    low_half = (ring.me % 2).astype(jnp.int32)
    half_dim = dim // 2

    w_own = w_qkv.transpose(1, 2, 0)
    w_peer, w_mate = peer(w_own), mate(w_own)
    b_peer, b_mate = peer(b_qv), mate(b_qv)
    vectors = jnp.concatenate([ln1_gain, ln1_bias, b_out, ln2_gain, ln2_bias, b_down]).reshape(6, dim)
    w_a = [w_own, w_mate]
    q_a, k_a, v_a, mixed_a, log_a, normed1 = attend(
        True, counts, tokens3, vectors, w_a, [b_qv, b_mate], rows
    )

    log_a, out_later, w_up, w_down, b_up = tie(log_a, w_out, w_up, w_down, b_up)
    out_peer, bias_peer = peer(out_later), peer(b_up)
    out_mate, bias_mate = mate(out_later), mate(b_up)
    up_mate, down_mate = mate(w_up), mate(w_down)
    up_part = lax.dynamic_slice_in_dim(w_up, low_half * half_dim, half_dim, 0)
    log_a, w_peer, b_peer, up_part = tie(log_a, w_peer, b_peer, up_part)
    up_first = peer(up_part)
    w_b = [w_peer, mate(w_peer)]
    q_b, k_b, v_b, mixed_b, log_b = attend(
        False, counts, tokens3, vectors, w_b, [b_peer, mate(b_peer)], rows
    )
    mixed_b, out_peer, bias_peer, down_later = tie(mixed_b, out_peer, bias_peer, w_down)
    bias_far = mate(bias_peer)
    down_peer = peer(down_later)
    out_a = jnp.concatenate([w_out, out_mate], axis=0)
    out_b = jnp.concatenate([out_peer, mate(out_peer)], axis=0)
    middle, normed2, cot_pad = branch(
        tokens3, cot3, mixed_a, mixed_b, out_a, out_b, vectors
    )
    middle, normed2, cot_pad, up_first = tie(middle, normed2, cot_pad, up_first)
    up_second, up_first_far = across(up_first), mate(up_first)
    flag = low_half.reshape(1)
    grad_part, hidden_a, dup_own, dup_mate, ddown_own, ddown_mate, dbias_a = feed(
        flag, normed2, cot_pad, None, [w_up, up_mate], [w_down, down_mate], [b_up, bias_mate]
    )

    grad_part, dup_own, dup_mate, ddown_own, ddown_mate, up_second, up_first_far = tie(
        grad_part, dup_own, dup_mate, ddown_own, ddown_mate, up_second, up_first_far
    )
    got_up, got_down = mate(dup_mate), mate(ddown_mate)
    up_second_far = mate(up_second)
    grad_part, down_peer = tie(grad_part, down_peer)
    ups = [up_first, up_second, up_first_far, up_second_far]
    downs = [down_peer, mate(down_peer)]
    grad_norm2, hidden_b, dup_peer, dup_far, ddown_peer, ddown_far, dbias_b = feed(
        flag, normed2, cot_pad, grad_part, ups, downs, [bias_peer, bias_far]
    )
    grad_norm2, dup_peer, dup_far, ddown_peer, ddown_far, got_up, got_down = tie(
        grad_norm2, dup_peer, dup_far, ddown_peer, ddown_far, got_up, got_down
    )
    far_up, far_down = mate(dup_far), mate(ddown_far)
    grad_middle, gmix_a, gmix_b, dw_out, small_two = unbranch(
        middle, cot_pad, grad_norm2, vectors, mixed_a, mixed_b, out_a, out_b
    )

    grad_middle, gmix_a, gmix_b, dw_out, small_two, far_up, far_down = tie(
        grad_middle, gmix_a, gmix_b, dw_out, small_two, far_up, far_down
    )
    top = lambda x: x[:half_dim]
    bottom = lambda x: x[half_dim:]
    up_one = peer(add_bf(top(dup_peer), top(far_up)))
    pair_keep, pair_got = ring.send(x_axis, add_bf(ddown_peer, far_down))
    out_far, out_near = mate(dw_out[3]), mate(dw_out[1])
    g_b, dqkv_b, dbqv_b = unattend(False, counts, q_b, k_b, v_b, gmix_b, log_b, normed1)
    g_b, dqkv_b, dbqv_b, up_one, pair_keep, pair_got, ddown_own, got_down, out_far, out_near, far_up, dup_peer = tie(
        g_b, dqkv_b, dbqv_b, up_one, pair_keep, pair_got, ddown_own, got_down, out_far, out_near, far_up, dup_peer
    )
    down_keep, down_got = ring.send(x_axis, add_bf(ddown_own, got_down))

    def block(n, dqkv, dbqv, dbias):
        at = n % 2
        tail = [
            small_two[0:4],
            dbias[:, at * units : (at + 1) * units],
            jnp.pad(dbqv[0:2, at * heads : (at + 1) * heads], ((0, 0), (0, dim - heads))),
        ]
        tail = jnp.concatenate(tail, axis=0)
        pad = -(3 * heads + tail.shape[0]) % (8 * wide)
        tail = jnp.pad(tail, ((0, pad), (0, 0))).astype(bf)
        return jnp.concatenate([dqkv[at].reshape(3 * heads, dim), tail], axis=0)

    far_rest = mate(block(3, dqkv_b, dbqv_b, dbias_b))
    pair_half = peer(add_bf(pair_keep, pair_got))
    one_keep, one_got = ring.send(x_axis, add_bf(top(dup_own), top(got_up), up_one))
    vectors_late, dbqv_b = tie(vectors, dbqv_b)
    layer_out = project(middle, vectors_late, hidden_a, hidden_b, [w_down, down_mate] + downs, seq)
    gmix_a, far_rest, pair_half, layer_out, down_keep, down_got = tie(
        gmix_a, far_rest, pair_half, layer_out, down_keep, down_got
    )
    two_got = peer(
        jnp.concatenate([add_bf(bottom(dup_peer), bottom(far_up)), add_bf(dw_out[2], out_far)], axis=0)
    )
    rest_keep, rest_got = ring.send(x_axis, add_bf(block(2, dqkv_b, dbqv_b, dbias_b), far_rest))
    down_parts = ring.send(z_axis, add_bf(down_keep, down_got, pair_half))
    g_a, dqkv_a, dbqv_a = unattend(True, counts, q_a, k_a, v_a, gmix_a, log_a, normed1)
    g_a, dqkv_a, dbqv_a, rest_keep, rest_got, one_keep, one_got, two_got, *down_parts = tie(
        g_a, dqkv_a, dbqv_a, rest_keep, rest_got, one_keep, one_got, two_got, *down_parts
    )

    rest_mate = mate(block(1, dqkv_a, dbqv_a, dbias_a))
    rest_half = peer(add_bf(rest_keep, rest_got))
    two_own = jnp.concatenate([add_bf(bottom(dup_own), bottom(got_up)), add_bf(dw_out[0], out_near)], axis=0)
    two_keep, two_got = ring.send(x_axis, add_bf(two_own, two_got))
    down_all = ring.gathered(z_axis, ring.back(more, ring.over(more, add_bf(*down_parts))))
    rest_own = add_bf(block(0, dqkv_a, dbqv_a, dbias_a), rest_mate)
    rest_own, g_a = tie(rest_own, g_a)
    rest_keep, rest_got = ring.send(x_axis, rest_own)
    input_grad, small_one = unnorm(g_a, g_b, w_a + w_b, tokens3, vectors, grad_middle)
    small_one, rest_keep, rest_got, rest_half, two_keep, two_got, *down_all = tie(
        small_one, rest_keep, rest_got, rest_half, two_keep, two_got, *down_all
    )
    down_sum = ring.place(z_axis, down_all)
    up_half = jnp.concatenate([add_bf(one_keep, one_got), add_bf(two_keep, two_got)], axis=0)
    small_one, up_half = tie(small_one, up_half)
    firsts = small_one[0:2]
    firsts = firsts + mate(firsts)
    firsts = firsts + peer(firsts)
    firsts = firsts + across(firsts)
    rest_sum = add_bf(rest_keep, rest_got, rest_half)
    spot = lax.broadcasted_iota(jnp.int32, (rest_sum.shape[0], 1), 0) - (
        3 * heads + 7 - low_half * rest_sum.shape[0]
    )
    whole = firsts.astype(bf)
    rest_sum = jnp.where(spot == 0, whole[0:1], jnp.where(spot == 1, whole[1:2], rest_sum))
    rest_sum = ring.back(ring.groups, ring.over(ring.groups[1:], rest_sum))
    up_sum = ring.back(ring.groups, ring.over(ring.groups[1:], up_half))
    down_sum = ring.back([x_axis], down_sum)
    quarter = half_dim // 2
    parts = [up_sum[: up_sum.shape[0] // 2], up_sum[up_sum.shape[0] // 2 :]]
    up_sum = jnp.concatenate([x[:quarter] for x in parts] + [x[quarter:] for x in parts], axis=0)
    firsts = rest_sum[3 * heads + 7 : 3 * heads + 9].astype(f32)
    up_grad, out_grad = up_sum[:dim], up_sum[dim:]
    vec = rest_sum[3 * heads :].astype(f32)
    return (
        layer_out.reshape(own_rows, dim),
        input_grad.reshape(own_rows, dim),
        firsts[0],
        firsts[1],
        rest_sum[: 3 * heads].astype(f32).reshape(3, heads, dim).transpose(2, 0, 1),
        vec[5:7, :heads],
        out_grad.astype(f32),
        vec[2],
        vec[0],
        vec[1],
        up_grad.astype(f32),
        vec[4:5, :units],
        down_sum.astype(f32),
        vec[3],
    )


def solution(mesh):
    wide, narrow = mesh.shape["wide"], mesh.shape["narrow"]
    assert narrow == 4 and wide >= 4 and wide & (wide - 1) == 0
    rows = P(("wide", "narrow"), None)
    return jax.shard_map(
        functools.partial(on_device, wide, narrow),
        mesh=mesh,
        in_specs=(
            rows,
            P("wide"),
            P(),
            P(),
            P(None, None, "narrow"),
            P(None, "narrow"),
            P("narrow", None),
            P(),
            P(),
            P(),
            P(None, "narrow"),
            P(None, "narrow"),
            P("narrow", None),
            P(),
            rows,
        ),
        out_specs=(
            rows,
            rows,
            P(),
            P(),
            P(None, None, "narrow"),
            P(None, "narrow"),
            P("narrow", None),
            P(),
            P(),
            P(),
            P(None, "narrow"),
            P(None, "narrow"),
            P("narrow", None),
            P(),
        ),
        check_vma=False,
    )
```
